32 devices in a mesh: section: 2 (over core), dp: 16 (over z, y, x).
Axes of the slice: x: 2, y: 2, z: 4, core: 2. Of those that a mesh axis runs over, the one named last changes fastest.
Arguments:
- inputs: bfloat16 [2, 16, 256, 768], P(None, 'dp'), may hold values from -6 to 6
- cotangent: bfloat16 [2, 16, 256, 768], P(None, 'dp'), may hold values from -6 to 6
- lengths: int32 [2, 16], P(None, 'dp'), may hold values from 64 to 256, as said below
- w_query: bfloat16 [2, 768, 768], P('section'), may hold values from -0.21875 to 0.21875
- w_key: bfloat16 [2, 768, 768], P('section'), may hold values from -0.21875 to 0.21875
- w_value: bfloat16 [2, 768, 768], P('section'), may hold values from -0.21875 to 0.21875
- w_output: bfloat16 [2, 768, 768], P('section'), may hold values from -1.75 to 1.75
- w_in: bfloat16 [2, 768, 3072], P('section'), may hold values from -0.21875 to 0.21875
- w_out: bfloat16 [2, 3072, 768], P('section'), may hold values from -0.109375 to 0.109375
- gain_attn: float32 [2, 768], P('section'), may hold values from 0.5 to 1.5
- gain_ffn: float32 [2, 768], P('section'), may hold values from 0.5 to 1.5
- mix_pre: float32 [2, 12, 12], P('section'), may hold values from -1.75 to 1.75
- mix_post: float32 [2, 12, 12], P('section'), may hold values from -1.75 to 1.75
Outputs:
- layer_outputs: bfloat16 [2, 2, 16, 256, 768], P('section', None, 'dp')
- input_grads: bfloat16 [2, 2, 16, 256, 768], P('section', None, 'dp')
- grad_query: float32 [2, 768, 768], P('section')
- grad_key: float32 [2, 768, 768], P('section')
- grad_value: float32 [2, 768, 768], P('section')
- grad_output: float32 [2, 768, 768], P('section')
- grad_in: float32 [2, 768, 3072], P('section')
- grad_out: float32 [2, 3072, 768], P('section')
- grad_gain_attn: float32 [2, 768], P('section')
- grad_gain_ffn: float32 [2, 768], P('section')
- grad_mix_pre: float32 [2, 12, 12], P('section')
- grad_mix_post: float32 [2, 12, 12], P('section')
- rms_stats: float32 [2, 3], P('section')
The draws below stay inside these ranges and needn't reach their ends.
Inputs may be any that keep to these rules, and one draw needn't show every extreme that they name: Sequence s of micro-batch m holds valid tokens at positions 0 to lengths[m, s] - 1 of its padded row; some sequence has length 256 and some has length 64.
All inputs are finite; a program needn't handle non-finite values.
Results may differ from the reference program's by a relative error of at most 0.018.
Values may be sent and summed in bfloat16 or wider, within the bound.
No kernel may reach another device: no remote copies, remote signals or barrier semaphores. Data moves between devices by JAX's collectives and lax.ppermute only.
A program may use at most 256 MiB of HBM per device.

```python
import jax
import jax.numpy as jnp
from jax import lax

D = 768
H = 12
DH = 64
FF = 3072
SEQ_DEV = 1
P_SIZE = 256
LMIN = 64
MB = 2
SEQS = 16


def draw_lengths(key, part):
    device = lax.broadcasted_iota(jnp.int32, (MB, SEQS), 1) // SEQ_DEV
    devices = SEQS // SEQ_DEV
    span = (P_SIZE - LMIN) * (device + 1) // devices
    extra = jax.random.randint(key, (MB, SEQS), 0, 1 << 20) % (span + 1)
    result = LMIN + extra
    result = result.at[0, SEQS - 1].set(P_SIZE)
    result = result.at[0, 0].set(LMIN)
    return result.astype(jnp.int32)


def block_scale(rng, extent, shards, least, top_value):
    loudness, own = 1.0, jax.random.fold_in(rng, 6)
    for axis_at, parts in shards:
        steps = jnp.exp(jax.random.uniform(jax.random.fold_in(own, axis_at), (parts,), jnp.float32, least / len(shards), top_value / len(shards)))
        loudness = loudness * jnp.repeat(steps, extent[axis_at] // parts).reshape([-1 if axis == axis_at else 1 for axis in range(len(extent))])
    return loudness


def normal_values(rng, extent, scale, bound, pieces=(), kind=jnp.bfloat16):
    entries = scale * jax.random.normal(rng, extent, jnp.float32)
    if pieces:
        entries = entries * block_scale(rng, extent, pieces, -0.22, 0.18)
    return jnp.clip(entries, -bound, bound).astype(kind)


def setup_inputs(seed: int = 0) -> dict:
    streams_of = jax.random.split(jax.random.key(seed), 14)
    inputs = normal_values(streams_of[0], (MB, SEQS, P_SIZE, D), 1.0, 6.0, ((1, 16),))
    cotangent = normal_values(streams_of[1], (MB, SEQS, P_SIZE, D), 1.0, 6.0, ((1, 16),))
    lengths = draw_lengths(jax.random.fold_in(streams_of[13], 71), 0)
    w_query = normal_values(streams_of[3], (2, D, D), D ** -0.5, 0.21875, ((0, 2),))
    w_key = normal_values(streams_of[4], (2, D, D), D ** -0.5, 0.21875, ((0, 2),))
    w_value = normal_values(streams_of[5], (2, D, D), D ** -0.5, 0.21875, ((0, 2),))
    w_output = normal_values(streams_of[6], (2, D, D), (4 * D // P_SIZE) ** -0.5, 1.75, ((0, 2),))
    w_in = normal_values(streams_of[7], (2, D, FF), D ** -0.5, 0.21875, ((0, 2),))
    w_out = normal_values(streams_of[8], (2, FF, D), FF ** -0.5, 0.109375, ((0, 2),))
    gain_attn = jnp.clip(1.0 + 0.1 * jax.random.normal(streams_of[9], (2, D), jnp.float32), 0.5, 1.5)
    gain_ffn = jnp.clip(1.0 + 0.1 * jax.random.normal(streams_of[10], (2, D), jnp.float32), 0.5, 1.5)
    mix_pre = normal_values(streams_of[11], (2, H, H), H ** -0.5, 1.75, ((0, 2),), jnp.float32)
    mix_post = normal_values(streams_of[12], (2, H, H), H ** -0.5, 1.75, ((0, 2),), jnp.float32)
    return dict(inputs=inputs, cotangent=cotangent, lengths=lengths, w_query=w_query, w_key=w_key, w_value=w_value, w_output=w_output, w_in=w_in, w_out=w_out, gain_attn=gain_attn, gain_ffn=gain_ffn, mix_pre=mix_pre, mix_post=mix_post)


@jax.custom_vjp
def low(v):
    return lax.optimization_barrier(v.astype(jnp.bfloat16)).astype(jnp.float32)

@jax.custom_vjp
def low_back(v):
    return v

def low_keep(v):
    return (low(v), None)

def low_pass(kept, grad):
    return (grad,)

def back_keep(v):
    return (v, None)

def back_low(kept, grad):
    return (low(grad),)
low.defvjp(low_keep, low_pass)
low_back.defvjp(back_keep, back_low)
EPSILON = 1e-06
MASKED = -1e+30
HIGHEST = lax.Precision.HIGHEST

def norm_part(values, gain):
    return values * lax.rsqrt(lax.optimization_barrier(jnp.mean(values * values, axis=-1, keepdims=True)) + EPSILON) * gain

def gelu_tanh(values):
    return 0.5 * values * (1.0 + jnp.tanh(0.7978845608028654 * (values + 0.044715 * values * values * values)))

def talking(scores, mix_pre, mix_post):
    length = scores.shape[-1]
    rows = lax.broadcasted_iota(jnp.int32, (length, length), 0)
    columns = lax.broadcasted_iota(jnp.int32, (length, length), 1)
    logits = jnp.einsum('gh,...hij->...gij', mix_pre, scores, precision=HIGHEST)
    logits = jnp.where(columns <= rows, logits, MASKED)
    shifted = logits - lax.optimization_barrier(jnp.max(logits, axis=-1, keepdims=True))
    exponent = jnp.exp(shifted)
    normalized = exponent / lax.optimization_barrier(jnp.sum(exponent, axis=-1, keepdims=True))
    return jnp.einsum('gh,...hij->...gij', mix_post, normalized, precision=HIGHEST)

def layer(values, valid, params):
    w_query, w_key, w_value, w_output, w_in, w_out, gain_attn, gain_ffn, mix_pre, mix_post = params
    length = values.shape[0]
    normed = low(norm_part(values, gain_attn))
    query = low_back(low(jnp.dot(normed, w_query, precision=HIGHEST))).reshape(length, H, DH)
    key_rows = low_back(low(jnp.dot(normed, w_key, precision=HIGHEST))).reshape(length, H, DH)
    value_rows = low_back(low(jnp.dot(normed, w_value, precision=HIGHEST))).reshape(length, H, DH)
    scores = low_back(jnp.einsum('ihd,jhd->hij', query, key_rows, precision=HIGHEST) * DH ** (-0.5))
    attn_weights = low(talking(scores, mix_pre, mix_post))
    head_out = low_back(low(jnp.einsum('hij,jhd->ihd', attn_weights, value_rows, precision=HIGHEST))).reshape(length, D)
    branch_attn = low_back(jnp.dot(head_out, w_output, precision=HIGHEST))
    residual = values + branch_attn
    normed_ffn = low(norm_part(residual, gain_ffn))
    pre_act = low_back(jnp.dot(normed_ffn, w_in, precision=HIGHEST))
    activation = low(gelu_tanh(pre_act))
    branch_ffn = low_back(jnp.dot(activation, w_out, precision=HIGHEST))
    layer_out = valid[:, None] * (residual + branch_ffn)
    sums = jnp.stack([jnp.sum(lax.optimization_barrier(jnp.mean(layer_out * layer_out, axis=-1))), jnp.sum(valid * lax.optimization_barrier(jnp.mean(branch_attn * branch_attn, axis=-1))), jnp.sum(valid * lax.optimization_barrier(jnp.mean(branch_ffn * branch_ffn, axis=-1)))])
    return (layer_out, sums)

def reference(inputs, cotangent, lengths, w_query, w_key, w_value, w_output, w_in, w_out, gain_attn, gain_ffn, mix_pre, mix_post):
    params = (w_query.astype(jnp.float32), w_key.astype(jnp.float32), w_value.astype(jnp.float32), w_output.astype(jnp.float32), w_in.astype(jnp.float32), w_out.astype(jnp.float32), gain_attn, gain_ffn, mix_pre, mix_post)
    positions = lax.broadcasted_iota(jnp.int32, (MB, SEQS, P_SIZE), 2)
    valid = (positions < lengths[:, :, None]).astype(jnp.float32).reshape(MB * SEQS, P_SIZE)
    flat_inputs = inputs.astype(jnp.float32).reshape(MB * SEQS, P_SIZE, D)
    nudge = jnp.zeros((MB * SEQS, P_SIZE, D), jnp.float32)

    def forward(weights, layer_inputs, offsets):

        def sequence_pass(record):
            values, valid_row, offset = record
            first = tuple((weight[0] for weight in weights))
            second = tuple((weight[1] for weight in weights))
            first_out, first_sums = layer(values, valid_row, first)
            middle = low_back(low(first_out)) + offset
            second_out, second_sums = layer(middle, valid_row, second)
            return ((first_out, second_out), jnp.stack([first_sums, second_sums]))
        outputs, sums = lax.map(jax.checkpoint(sequence_pass), (layer_inputs, valid, offsets))
        return (outputs, lax.optimization_barrier(jnp.sum(sums, axis=0)))
    (first_out, second_out), pullback, square_sums = jax.vjp(forward, params, flat_inputs, nudge, has_aux=True)
    upstream_rows = cotangent.astype(jnp.float32).reshape(MB * SEQS, P_SIZE, D)
    grads, grad_inputs, grad_middle = pullback((jnp.zeros_like(first_out), upstream_rows))
    count = jnp.sum(valid)
    rms = jnp.sqrt(square_sums / count)
    layer_outputs = jnp.stack([first_out, second_out]).reshape(2, MB, SEQS, P_SIZE, D).astype(jnp.bfloat16)
    input_grads = jnp.stack([grad_inputs, grad_middle]).reshape(2, MB, SEQS, P_SIZE, D).astype(jnp.bfloat16)
    return (layer_outputs, input_grads, grads[0], grads[1], grads[2], grads[3], grads[4], grads[5], grads[6], grads[7], grads[8], grads[9], rms)
```

```python
import jax
import jax.numpy as jnp
from jax import lax
from jax.sharding import PartitionSpec as P

EPSILON = 1e-06
MASKED = -1e30
F32 = jnp.float32
BF16 = jnp.bfloat16


def dot(a, b, dims):
    return lax.dot_general(a, b, ((dims[0], dims[1]), ((), ())), preferred_element_type=F32)


def mix_heads(mix, values):
    return jnp.einsum("gh,hij->gij", mix, values, precision=lax.Precision.HIGH)


def norm_scale(values):
    return lax.rsqrt(jnp.mean(values * values, axis=-1, keepdims=True) + EPSILON)


def norm_back(values, gain, grad):
    scale = norm_scale(values)
    weighted = grad * gain
    inner = jnp.mean(values * weighted, axis=-1, keepdims=True)
    grad_values = scale * weighted - values * (scale * scale * scale) * inner
    grad_gain = jnp.sum(grad * values * scale, axis=0)
    return grad_values, grad_gain


def gelu_pair(values):
    inner = 0.7978845608028654 * (values + 0.044715 * values * values * values)
    tanh = jnp.tanh(inner)
    value = 0.5 * values * (1.0 + tanh)
    slope = 0.5 * (1.0 + tanh) + 0.5 * values * (1.0 - tanh * tanh) * (
        0.7978845608028654 * (1.0 + 3.0 * 0.044715 * values * values)
    )
    return value, slope


def forward(values, valid, params):
    w_query, w_key, w_value, w_output, w_in, w_out, gain_attn, gain_ffn, mix_pre, mix_post = params
    length, width = values.shape
    heads = mix_pre.shape[0]
    split = (length, heads, width // heads)
    normed = (values * norm_scale(values) * gain_attn).astype(BF16)
    query = dot(normed, w_query, ((1,), (0,))).astype(BF16).reshape(split)
    key = dot(normed, w_key, ((1,), (0,))).astype(BF16).reshape(split)
    value = dot(normed, w_value, ((1,), (0,))).astype(BF16).reshape(split)
    scores = jnp.einsum("ihd,jhd->hij", query, key, preferred_element_type=F32) * (split[2] ** -0.5)
    rows = lax.broadcasted_iota(jnp.int32, (length, length), 0)
    columns = lax.broadcasted_iota(jnp.int32, (length, length), 1)
    logits = jnp.where(columns <= rows, mix_heads(mix_pre, scores), MASKED)
    exponent = jnp.exp(logits - jnp.max(logits, axis=-1, keepdims=True))
    probs = exponent / jnp.sum(exponent, axis=-1, keepdims=True)
    weights = mix_heads(mix_post, probs).astype(BF16)
    head_out = jnp.einsum("hij,jhd->ihd", weights, value, preferred_element_type=F32)
    head_out = head_out.astype(BF16).reshape(length, width)
    branch_attn = dot(head_out, w_output, ((1,), (0,)))
    residual = values + branch_attn
    normed_ffn = (residual * norm_scale(residual) * gain_ffn).astype(BF16)
    pre_act = dot(normed_ffn, w_in, ((1,), (0,)))
    activation, slope = gelu_pair(pre_act)
    activation = activation.astype(BF16)
    branch_ffn = dot(activation, w_out, ((1,), (0,)))
    out = valid * (residual + branch_ffn)
    squares = jnp.stack(
        [
            jnp.sum(jnp.mean(out * out, axis=-1)),
            jnp.sum(valid[:, 0] * jnp.mean(branch_attn * branch_attn, axis=-1)),
            jnp.sum(valid[:, 0] * jnp.mean(branch_ffn * branch_ffn, axis=-1)),
        ]
    )
    saved = (
        normed, query, key, value, scores, probs, weights, head_out, residual, normed_ffn, activation, slope,
    )
    return out.astype(BF16), squares, saved


def backward_ffn(grad_sum, params, saved):
    w_in, w_out, gain_ffn = params[4], params[5], params[7]
    residual, normed_ffn, activation, slope = saved[8:]
    grad_branch = grad_sum.astype(BF16)
    grad_act = dot(grad_branch, w_out, ((1,), (1,)))
    grad_pre = (grad_act * slope).astype(BF16)
    grad_normed = dot(grad_pre, w_in, ((1,), (1,)))
    back, grad_gain = norm_back(residual, gain_ffn, grad_normed)
    return grad_sum + back, grad_gain, (activation, grad_branch, normed_ffn, grad_pre)


def backward_attention(values, grad_resid, params, saved):
    w_query, w_key, w_value, w_output = params[:4]
    gain_attn, mix_pre, mix_post = params[6], params[8], params[9]
    normed, query, key, value, scores, probs, weights, head_out = saved[:8]
    length, heads, size = query.shape
    grad_attn = grad_resid.astype(BF16)
    grad_heads = dot(grad_attn, w_output, ((1,), (1,))).astype(BF16).reshape(query.shape)
    grad_weights = jnp.einsum("ihd,jhd->hij", grad_heads, value, preferred_element_type=F32)
    grad_value = jnp.einsum("hij,ihd->jhd", weights, grad_heads, preferred_element_type=F32)
    grad_mix_post = jnp.einsum("gij,hij->gh", grad_weights, probs, precision=lax.Precision.HIGH)
    grad_probs = mix_heads(mix_post.T, grad_weights)
    grad_logits = probs * (grad_probs - jnp.sum(probs * grad_probs, axis=-1, keepdims=True))
    grad_mix_pre = jnp.einsum("gij,hij->gh", grad_logits, scores, precision=lax.Precision.HIGH)
    grad_scores = mix_heads(mix_pre.T, grad_logits).astype(BF16)
    scale = size**-0.5
    grad_query = jnp.einsum("hij,jhd->ihd", grad_scores, key, preferred_element_type=F32) * scale
    grad_key = jnp.einsum("hij,ihd->jhd", grad_scores, query, preferred_element_type=F32) * scale
    width = heads * size
    pieces = tuple(
        piece.astype(BF16).reshape(length, width) for piece in (grad_query, grad_key, grad_value)
    )
    grad_normed = sum(
        dot(piece, matrix, ((1,), (1,))) for piece, matrix in zip(pieces, (w_query, w_key, w_value))
    )
    back, grad_gain = norm_back(values, gain_attn, grad_normed)
    return grad_resid + back, grad_gain, grad_mix_pre, grad_mix_post, (normed, head_out, grad_attn) + pieces


def local(
    inputs, cotangent, lengths, w_query, w_key, w_value, w_output, w_in, w_out, gain_attn, gain_ffn, mix_pre, mix_post,
):
    core = lax.axis_index("section")
    is_first = core == 0
    swap = lambda shard: lax.ppermute(shard, "section", [(0, 1), (1, 0)])
    length, width = inputs.shape[2:]
    hidden = w_in.shape[2]

    own = (w_query, w_key, w_value, w_output, w_in, w_out, gain_attn, gain_ffn, mix_pre, mix_post)
    other = tuple(swap(weight) for weight in own)
    layers = (
        tuple(jnp.where(is_first, a, b)[0] for a, b in zip(own, other)),
        tuple(jnp.where(is_first, b, a)[0] for a, b in zip(own, other)),
    )
    take = lambda whole: lax.dynamic_index_in_dim(whole, core, 0, keepdims=False)[0]
    values = take(inputs).astype(F32)
    upstream = take(cotangent).astype(F32)
    valid = (lax.broadcasted_iota(jnp.int32, (length, 1), 0) < take(lengths)).astype(F32)

    outputs, squares, kept, starts = [], [], [], []
    layer_in = values
    for params in layers:
        starts.append(layer_in)
        rounded, square, saved = forward(layer_in, valid, params)
        outputs.append(rounded)
        squares.append(square)
        kept.append(saved)
        layer_in = rounded.astype(F32)

    def split_cols(array):
        half = array.shape[1] // 2
        mine = lax.dynamic_slice_in_dim(array, core * half, half, 1)
        theirs = lax.dynamic_slice_in_dim(array, (1 - core) * half, half, 1)
        return mine, theirs

    def both_rows(array):
        return jnp.concatenate([array, swap(array)], axis=0)

    def both_half(array):
        mine, theirs = split_cols(array)
        return jnp.concatenate([mine, swap(theirs)], axis=0)

    def weight_grad(left, right):
        return dot(left, right, ((0,), (0,))).astype(BF16)

    grads = [None, None]
    small = [None, None]
    input_grads = [None, None]
    for index in (1, 0):
        params, saved = layers[index], kept[index]
        grad_sum = valid * upstream
        grad_resid, gain_ffn_grad, ffn = backward_ffn(grad_sum, params, saved)
        activation, grad_branch, normed_ffn, grad_pre = ffn
        down = weight_grad(both_half(activation), both_rows(grad_branch))
        up = weight_grad(both_rows(normed_ffn), both_half(grad_pre))
        grad_in, gain_attn_grad, mix_pre_grad, mix_post_grad, attn = backward_attention(
            starts[index], grad_resid, params, saved
        )
        normed, head_out, grad_attn, grad_query, grad_key, grad_value = attn
        rows = both_rows(normed)
        sides = [weight_grad(rows, both_half(piece)) for piece in (grad_query, grad_key, grad_value)]
        sides.append(weight_grad(both_rows(head_out), both_half(grad_attn)))
        blocks = [down]
        blocks += [up[:, at * width : (at + 1) * width] for at in range(up.shape[1] // width)]
        blocks += [jnp.concatenate(sides[:2], axis=1), jnp.concatenate(sides[2:], axis=1)]
        grads[index] = jnp.concatenate(blocks, axis=0)
        small[index] = jnp.concatenate(
            [gain_attn_grad, gain_ffn_grad, mix_pre_grad.reshape(-1), mix_post_grad.reshape(-1), squares[index]]
        )
        input_grads[index] = grad_in.astype(BF16)
        upstream = input_grads[index].astype(F32)

    shards = [lax.psum_scatter(grad, "dp", scatter_dimension=0, tiled=True) for grad in grads]
    mine = jnp.where(is_first, shards[0], shards[1])
    theirs = swap(jnp.where(is_first, shards[1], shards[0]))
    halves = jnp.concatenate([jnp.where(is_first, mine, theirs), jnp.where(is_first, theirs, mine)], axis=0)
    whole = lax.all_gather(halves, "dp", axis=0)
    ranks = whole.shape[0]
    whole = whole.reshape(ranks, 2, -1, width).transpose(1, 0, 2, 3).reshape(2, -1, width).astype(F32)
    half = width // 2
    count = hidden // 2
    w_out_grad = whole[:, :count].reshape(1, hidden, width)
    blocks = (hidden // 2) // width
    up = whole[:, count : count + blocks * width].reshape(2 * blocks, width, width)
    w_in_grad = up.transpose(1, 0, 2).reshape(1, width, hidden)
    rest = whole[:, count + blocks * width :].reshape(2, 2, width, 2, half)
    rest = rest.transpose(1, 3, 2, 0, 4).reshape(4, 1, width, width)

    both = jnp.stack(small)
    total_small = jnp.where(is_first, both, both[::-1])
    mine_small = total_small[0] + swap(total_small[1])
    tail = jnp.concatenate([mine_small, jnp.sum(valid)[None] + swap(jnp.sum(valid)[None])])
    tail = lax.psum(tail, "dp")
    heads = mix_pre.shape[1]
    square = heads * heads
    at = 2 * width
    rms = jnp.sqrt(tail[at + 2 * square : at + 2 * square + 3] / tail[-1])[None]

    def place(pair):
        mine = jnp.where(is_first, pair[0], pair[1])
        theirs = swap(jnp.where(is_first, pair[1], pair[0]))
        ordered = [jnp.where(is_first, mine, theirs), jnp.where(is_first, theirs, mine)]
        return jnp.stack(ordered)[None, :, None]

    return (
        place(outputs),
        place(input_grads),
        rest[0],
        rest[1],
        rest[2],
        rest[3],
        w_in_grad,
        w_out_grad,
        tail[None, :width],
        tail[None, width:at],
        tail[at : at + square].reshape(1, heads, heads),
        tail[at + square : at + 2 * square].reshape(1, heads, heads),
        rms,
    )


def solution(mesh):
    in_specs = (
        P(None, "dp", None, None),
        P(None, "dp", None, None),
        P(None, "dp"),
        P("section", None, None),
        P("section", None, None),
        P("section", None, None),
        P("section", None, None),
        P("section", None, None),
        P("section", None, None),
        P("section", None),
        P("section", None),
        P("section", None, None),
        P("section", None, None),
    )
    out_specs = (
        P("section", None, "dp", None, None),
        P("section", None, "dp", None, None),
        P("section", None, None),
        P("section", None, None),
        P("section", None, None),
        P("section", None, None),
        P("section", None, None),
        P("section", None, None),
        P("section", None),
        P("section", None),
        P("section", None, None),
        P("section", None, None),
        P("section", None),
    )
    return jax.shard_map(local, mesh=mesh, in_specs=in_specs, out_specs=out_specs, check_vma=False)
```

```python
import functools

import jax
import jax.numpy as jnp
from jax import lax
from jax.experimental import pallas as pl
from jax.experimental.pallas import tpu as pltpu
from jax.sharding import PartitionSpec as P

EPSILON = 1e-06
MASKED = -1e30
F32 = jnp.float32
BF16 = jnp.bfloat16


HEADS_ROWS = 32
SPAN = 512


def row_scale(values):
    return lax.rsqrt(jnp.mean(values * values, axis=-1, keepdims=True) + EPSILON)


def norm_back(values, gain, grad):
    scale = row_scale(values)
    weighted = grad * gain
    inner = jnp.mean(values * weighted, axis=-1, keepdims=True)
    grad_values = scale * weighted - values * (scale * scale * scale) * inner
    return grad_values, jnp.sum(grad * values * scale, axis=0, keepdims=True)


def gelu_pair(values):
    square = values * values
    tanh = jnp.tanh(values * (0.7978845608028654 + 0.7978845608028654 * 0.044715 * square))
    half = 0.5 * (1.0 + tanh)
    slope = half + 0.5 * values * (1.0 - tanh * tanh) * (
        0.7978845608028654 + 3.0 * 0.7978845608028654 * 0.044715 * square
    )
    return values * half, slope


def dot_nn(left, right):
    return lax.dot_general(left, right, (((1,), (0,)), ((), ())), preferred_element_type=F32)


def dot_nt(left, right):
    return lax.dot_general(left, right, (((1,), (1,)), ((), ())), preferred_element_type=F32)


def dot_tn(left, right):
    return lax.dot_general(left, right, (((0,), (0,)), ((), ())), preferred_element_type=F32)


class Weight:
    def __init__(self, mine, own, other, held, sem):
        self.mine, self.own, self.other, self.held, self.sem = mine, own, other, held, sem

    def copy(self, source, cut):
        return pltpu.make_async_copy(source.at[(0,) + cut], self.held.at[cut], self.sem)

    def start(self, cut=(slice(None), slice(None))):
        @pl.when(self.mine)
        def _():
            self.copy(self.own, cut).start()

        @pl.when(jnp.logical_not(self.mine))
        def _():
            self.copy(self.other, cut).start()

    def wait(self, cut=(slice(None), slice(None))):
        self.copy(self.own, cut).wait()


def param_row(mine, own, other, at, count=1):
    rows = pl.ds(at, count)
    return jnp.where(mine, own[rows, :], other[rows, :])


def attention_kernel(
    layer, heads, meta, x, own_rows, other_rows, wq, wk, wv, wo, wq2, wk2, wv2, wo2,
    both_out, query_out, key_out, value_out, probs_out, residual_out, stats_out,
    held_q, held_k, held_v, held_o, total, sems,
):
    mine = meta[0] == layer
    weights = [
        Weight(mine, own, other, held, sems.at[at])
        for at, (own, other, held) in enumerate(
            ((wq, wq2, held_q), (wk, wk2, held_k), (wv, wv2, held_v), (wo, wo2, held_o))
        )
    ]
    for weight in weights:
        weight.start()
    length, width = x.shape
    half = length // 2
    values = x[...].astype(F32)
    gain = param_row(mine, own_rows, other_rows, 0)
    both_out[:, :width] = (values * row_scale(values) * gain).astype(BF16)
    for weight, held, out, factor in (
        (weights[0], held_q, query_out, (width // heads) ** -0.5),
        (weights[1], held_k, key_out, 1.0),
        (weights[2], held_v, value_out, 1.0),
    ):
        weight.wait()
        made = dot_nn(both_out[:, :width], held[...]).astype(BF16)
        out[...] = (made.astype(F32) * factor).astype(BF16) if factor != 1.0 else made
    total[...] = jnp.zeros_like(total)

    def softmax(logits, first):
        rows = lax.broadcasted_iota(jnp.int32, logits.shape, 0) + first
        columns = lax.broadcasted_iota(jnp.int32, logits.shape, 1)
        logits = jnp.where(columns <= rows, logits, MASKED)
        exponent = jnp.exp(logits - jnp.max(logits, axis=-1, keepdims=True))
        return exponent / jnp.sum(exponent, axis=-1, keepdims=True)

    def head(at, _):
        mixed = key_out[...].astype(F32) * param_row(mine, own_rows, other_rows, 2 + at)
        high = mixed.astype(BF16)
        low = (mixed - high.astype(F32)).astype(BF16)
        upper = dot_nt(query_out[:half, :], high[:half]) + dot_nt(query_out[:half, :], low[:half])
        lower = dot_nt(query_out[half:, :], high) + dot_nt(query_out[half:, :], low)
        row = pl.multiple_of(at * length, length)
        probs_out[pl.ds(row, half), :half] = softmax(upper, 0).astype(BF16)
        probs_out[pl.ds(row, half), half:] = jnp.zeros((half, length - half), BF16)
        probs_out[pl.ds(row + half, half), :] = softmax(lower, half).astype(BF16)
        scaled = (value_out[...].astype(F32) * param_row(mine, own_rows, other_rows, 2 + heads + at)).astype(BF16)
        total[:half, :] += dot_nn(probs_out[pl.ds(row, half), :half], scaled[:half])
        total[half:, :] += dot_nn(probs_out[pl.ds(row + half, half), :], scaled)
        return 0

    lax.fori_loop(0, heads, head, 0)
    both_out[:, width:] = total[...].astype(BF16)
    weights[3].wait()
    branch = dot_nn(both_out[:, width:], held_o[...])
    residual_out[...] = values + branch
    valid = lax.broadcasted_iota(jnp.int32, (length, 1), 0) < meta[1]
    stats_out[...] = jnp.broadcast_to(
        jnp.sum(jnp.where(valid, branch * branch, 0.0), axis=0, keepdims=True), stats_out.shape
    )


def ffn_kernel(
    layer, backward, meta, residual, own_rows, other_rows, w_in, w_out, w_in2, w_out2, *refs
):
    if backward:
        upstream, refs = refs[0], refs[1:]
        out, own_first, send_first, own_second, send_second, resid_out, stats_out = refs[:7]
        held_in, held_out, normed, act, total, pre_grad, branch_grad, back_total, sems, out_sems = refs[7:]
    else:
        out, own_first, send_first, slope_out, stats_out = refs[:5]
        held_in, held_out, normed, act, total, sems, out_sems = refs[5:]
    core = meta[0]
    mine = core == layer
    length, width = residual.shape
    hidden = held_in.shape[1]
    steps = hidden // SPAN
    half = hidden // 2
    cuts_in = [(slice(None), pl.ds(step * SPAN, SPAN)) for step in range(steps)]
    cuts_out = [(pl.ds(step * SPAN, SPAN), slice(None)) for step in range(steps)]
    ins = [Weight(mine, w_in, w_in2, held_in, sems.at[step]) for step in range(steps)]
    outs = [Weight(mine, w_out, w_out2, held_out, sems.at[steps + step]) for step in range(steps)]
    for step in range(steps):
        ins[step].start(cuts_in[step])
        outs[step].start(cuts_out[step])
    values = residual[...]
    normed[...] = (values * row_scale(values) * param_row(mine, own_rows, other_rows, 1)).astype(BF16)
    valid = lax.broadcasted_iota(jnp.int32, (length, 1), 0) < meta[1]
    copies = []

    def send(source, target, at):
        copy = pltpu.make_async_copy(source, target, out_sems.at[at])
        copy.start()
        copies.append(copy)

    send(normed, own_first.at[:, pl.ds(half, width)], 0)
    send(normed, send_first.at[:, pl.ds(half, width)], 1)
    if backward:
        branch_grad[...] = jnp.where(valid, upstream[...], jnp.zeros_like(upstream))
        send(branch_grad, own_second.at[:, pl.ds(half, width)], 2)
        send(branch_grad, send_second.at[:, pl.ds(half, width)], 3)
    for step in range(steps):
        span = pl.ds(step * SPAN, SPAN)
        ins[step].wait(cuts_in[step])
        made, slope = gelu_pair(dot_nn(normed[...], held_in[:, span]))
        act[:, span] = made.astype(BF16)
        outs[step].wait(cuts_out[step])
        part = dot_nn(act[:, span], held_out[span, :])
        total[...] = part if step == 0 else total[...] + part
        if backward:
            grad = (dot_nt(branch_grad[...], held_out[span, :]) * slope).astype(BF16)
            pre_grad[:, span] = grad
            part = dot_nt(pre_grad[:, span], held_in[:, span])
            back_total[...] = part if step == 0 else back_total[...] + part
        else:
            slope_out[:, span] = slope.astype(BF16)
    mine_at = pl.ds(pl.multiple_of(core * half, 128), half)
    other_at = pl.ds(pl.multiple_of((1 - core) * half, 128), half)
    send(act.at[:, mine_at], own_first.at[:, pl.ds(0, half)], 4)
    send(act.at[:, other_at], send_first.at[:, pl.ds(0, half)], 5)
    if backward:
        send(pre_grad.at[:, mine_at], own_second.at[:, pl.ds(0, half)], 6)
        send(pre_grad.at[:, other_at], send_second.at[:, pl.ds(0, half)], 7)
    branch = total[...]
    made = jnp.where(valid, residual[...] + branch, 0.0)
    out[...] = made.astype(BF16)
    stats_out[0:1, :] = jnp.sum(made * made, axis=0, keepdims=True)
    stats_out[1:2, :] = jnp.sum(jnp.where(valid, branch * branch, 0.0), axis=0, keepdims=True)
    if backward:
        back, gain_grad = norm_back(
            residual[...], param_row(mine, own_rows, other_rows, 1), back_total[...]
        )
        resid_out[...] = branch_grad[...].astype(F32) + back
        stats_out[2:3, :] = gain_grad
    for copy in copies:
        copy.wait()


def ffn_back_kernel(
    layer, meta, residual, upstream, slope, own_rows, other_rows, w_in, w_out, w_in2, w_out2,
    own_second, send_second, resid_out, stats_out,
    held_in, held_out, pre_grad, branch_grad, back_total, sems, out_sems,
):
    core = meta[0]
    mine = core == layer
    length, width = residual.shape
    hidden = held_in.shape[1]
    steps = hidden // SPAN
    half = hidden // 2
    cuts_in = [(slice(None), pl.ds(step * SPAN, SPAN)) for step in range(steps)]
    cuts_out = [(pl.ds(step * SPAN, SPAN), slice(None)) for step in range(steps)]
    ins = [Weight(mine, w_in, w_in2, held_in, sems.at[step]) for step in range(steps)]
    outs = [Weight(mine, w_out, w_out2, held_out, sems.at[steps + step]) for step in range(steps)]
    for step in range(steps):
        outs[step].start(cuts_out[step])
        ins[step].start(cuts_in[step])
    valid = lax.broadcasted_iota(jnp.int32, (length, 1), 0) < meta[1]
    branch_grad[...] = jnp.where(valid, upstream[...], jnp.zeros_like(upstream))
    copies = []

    def send(source, target, at):
        copy = pltpu.make_async_copy(source, target, out_sems.at[at])
        copy.start()
        copies.append(copy)

    send(branch_grad, own_second.at[:, pl.ds(half, width)], 0)
    send(branch_grad, send_second.at[:, pl.ds(half, width)], 1)
    for step in range(steps):
        span = pl.ds(step * SPAN, SPAN)
        outs[step].wait(cuts_out[step])
        grad = dot_nt(branch_grad[...], held_out[span, :]) * slope[:, span].astype(F32)
        pre_grad[:, span] = grad.astype(BF16)
        ins[step].wait(cuts_in[step])
        part = dot_nt(pre_grad[:, span], held_in[:, span])
        back_total[...] = part if step == 0 else back_total[...] + part
    send(pre_grad.at[:, pl.ds(pl.multiple_of(core * half, 128), half)], own_second.at[:, pl.ds(0, half)], 2)
    send(pre_grad.at[:, pl.ds(pl.multiple_of((1 - core) * half, 128), half)], send_second.at[:, pl.ds(0, half)], 3)
    back, gain_grad = norm_back(residual[...], param_row(mine, own_rows, other_rows, 1), back_total[...])
    resid_out[...] = branch_grad[...].astype(F32) + back
    stats_out[0:1, :] = gain_grad
    for copy in copies:
        copy.wait()


def attention_back_kernel(
    layer, heads, meta, x, resid_grad, query, key, value, probs, own_rows, other_rows,
    wq, wk, wv, wo, wq2, wk2, wv2, wo2,
    own_pack, send_pack, grad_out, stats_out,
    held_q, held_k, held_v, held_o, attn_grad, head_grad, logit_grad, heads_scaled, query_scaled,
    query_grad, piece, total, sems, out_sems,
):
    core = meta[0]
    mine = core == layer
    weights = [
        Weight(mine, own, other, held, sems.at[at])
        for at, (own, other, held) in enumerate(
            ((wo, wo2, held_o), (wq, wq2, held_q), (wk, wk2, held_k), (wv, wv2, held_v))
        )
    ]
    for weight in weights:
        weight.start()
    length, width = x.shape
    half = width // 2
    copies = []

    def send(source, at, sem):
        for target, which in ((own_pack, core), (send_pack, 1 - core)):
            copy = pltpu.make_async_copy(
                source.at[:, pl.ds(pl.multiple_of(which * half, 128), half)],
                target.at[:, pl.ds(at * half, half)],
                out_sems.at[sem + (0 if target is own_pack else 1)],
            )
            copy.start()
            copies.append(copy)

    attn_grad[...] = resid_grad[...].astype(BF16)
    send(attn_grad, 3, 0)
    weights[0].wait()
    head_grad[...] = dot_nt(attn_grad[...], held_o[...]).astype(BF16)
    query_grad[...] = jnp.zeros_like(query_grad)

    def head(at, _):
        row = pl.multiple_of(at * length, length)
        rows = pl.ds(row, length)
        pre = param_row(mine, own_rows, other_rows, 2 + at)
        post = param_row(mine, own_rows, other_rows, 2 + heads + at)
        scaled = (value[...].astype(F32) * post).astype(BF16)
        grad_probs = dot_nt(head_grad[...], scaled)
        prob = probs[rows, :].astype(F32)
        inner = jnp.sum(prob * grad_probs, axis=-1, keepdims=True)
        logit_grad[rows, :] = (prob * (grad_probs - inner)).astype(BF16)
        heads_scaled[rows, :] = (head_grad[...].astype(F32) * post).astype(BF16)
        query_scaled[rows, :] = (query[...].astype(F32) * pre).astype(BF16)
        weighed = dot_nn(probs[rows, :], value[...])
        stats_out[pl.ds(HEADS_ROWS // 2 + at, 1), :] = jnp.sum(
            weighed * head_grad[...].astype(F32), axis=0, keepdims=True
        )
        routed = dot_nn(logit_grad[rows, :], key[...])
        stats_out[pl.ds(at, 1), :] = jnp.sum(routed * query[...].astype(F32), axis=0, keepdims=True)
        query_grad[...] += routed * pre
        return 0

    lax.fori_loop(0, heads, head, 0)
    factor = (width // heads) ** -0.5
    piece[0] = (query_grad[...] * factor).astype(BF16)
    send(piece.at[0], 0, 2)
    weights[1].wait()
    total[...] = dot_nt(piece[0], held_q[...])
    piece[1] = dot_tn(logit_grad[...], query_scaled[...]).astype(BF16)
    send(piece.at[1], 1, 4)
    weights[2].wait()
    total[...] += dot_nt(piece[1], held_k[...])
    piece[2] = dot_tn(probs[...], heads_scaled[...]).astype(BF16)
    send(piece.at[2], 2, 6)
    weights[3].wait()
    back, gain_grad = norm_back(
        x[...].astype(F32),
        param_row(mine, own_rows, other_rows, 0),
        total[...] + dot_nt(piece[2], held_v[...]),
    )
    grad_out[...] = (resid_grad[...] + back).astype(BF16)
    stats_out[pl.ds(heads, 1), :] = gain_grad
    for copy in copies:
        copy.wait()


def vmem():
    return pl.BlockSpec(memory_space=pltpu.VMEM)


def smem():
    return pl.BlockSpec(memory_space=pltpu.SMEM)


def shaped(shape, kind):
    return jax.ShapeDtypeStruct(shape, kind)


def call(kernel, in_specs, outs, out_specs, scratch, flops, bytes_accessed):
    return pl.pallas_call(
        kernel,
        out_shape=outs,
        in_specs=in_specs,
        out_specs=out_specs,
        scratch_shapes=scratch,
        compiler_params=pltpu.CompilerParams(vmem_limit_bytes=56 << 20),
        cost_estimate=pl.CostEstimate(flops=flops, bytes_accessed=bytes_accessed, transcendentals=0),
    )


def attention_forward(layer, heads, meta, x, rows, weights):
    length, width = x.shape
    square = length * width
    outs = (
        shaped((length, 2 * width), BF16),
        shaped((length, width), BF16),
        shaped((length, width), BF16),
        shaped((length, width), BF16),
        shaped((heads * length, length), BF16),
        shaped((length, width), F32),
        shaped((8, width), F32),
    )
    scratch = [pltpu.VMEM((width, width), BF16)] * 4
    scratch += [pltpu.VMEM((length, width), F32), pltpu.SemaphoreType.DMA((4,))]
    kernel = functools.partial(attention_kernel, layer, heads)
    run = call(
        kernel, [smem(), vmem(), vmem(), vmem()] + [hbm()] * 8, outs, [vmem()] * 7, scratch,
        8 * square * width + 6 * heads * length * square, 8 * width * width + 20 * square,
    )
    own, other = weights
    return run(meta, x, *rows, *own[:4], *other[:4])


def ffn_forward(layer, meta, residual, rows, weights, upstream=None):
    length, width = residual.shape
    hidden = weights[0][4].shape[2]
    half = hidden // 2
    pack = shaped((length, half + width), BF16)
    steps = hidden // SPAN
    held = [pltpu.VMEM((width, hidden), BF16), pltpu.VMEM((hidden, width), BF16)]
    held += [pltpu.VMEM((length, width), BF16), pltpu.VMEM((length, hidden), BF16), pltpu.VMEM((length, width), F32)]
    sems = [pltpu.SemaphoreType.DMA((2 * steps,)), pltpu.SemaphoreType.DMA((8,))]
    ins = [smem(), vmem(), vmem(), vmem()] + [hbm()] * 4
    work = 4 * length * width * hidden
    moved = 4 * width * hidden + 8 * length * hidden
    own, other = weights
    args = (meta, residual) + rows + own[4:6] + other[4:6]
    if upstream is None:
        outs = (shaped((length, width), BF16), pack, pack, shaped((length, hidden), BF16), shaped((8, width), F32))
        specs = [vmem(), hbm(), hbm(), vmem(), vmem()]
        return call(functools.partial(ffn_kernel, layer, False), ins, outs, specs, held + sems, work, moved)(*args)
    outs = (shaped((length, width), BF16), pack, pack, pack, pack, shaped((length, width), F32), shaped((8, width), F32))
    specs = [vmem()] + [hbm()] * 4 + [vmem()] * 2
    held += [pltpu.VMEM((length, hidden), BF16), pltpu.VMEM((length, width), BF16), pltpu.VMEM((length, width), F32)]
    kernel = functools.partial(ffn_kernel, layer, True)
    return call(kernel, ins + [vmem()], outs, specs, held + sems, 2 * work, moved)(*args, upstream)


def ffn_backward(layer, meta, residual, upstream, slope, rows, weights):
    length, width = residual.shape
    hidden = slope.shape[1]
    pack = shaped((length, hidden // 2 + width), BF16)
    steps = hidden // SPAN
    scratch = [pltpu.VMEM((width, hidden), BF16), pltpu.VMEM((hidden, width), BF16)]
    scratch += [pltpu.VMEM((length, hidden), BF16), pltpu.VMEM((length, width), BF16), pltpu.VMEM((length, width), F32)]
    scratch += [pltpu.SemaphoreType.DMA((2 * steps,)), pltpu.SemaphoreType.DMA((4,))]
    own, other = weights
    return call(
        functools.partial(ffn_back_kernel, layer),
        [smem()] + [vmem()] * 5 + [hbm()] * 4,
        (pack, pack, shaped((length, width), F32), shaped((8, width), F32)),
        [hbm(), hbm(), vmem(), vmem()],
        scratch,
        4 * length * width * hidden,
        4 * width * hidden + 6 * length * hidden,
    )(meta, residual, upstream, slope, *rows, *own[4:6], *other[4:6])


def attention_backward(layer, heads, meta, x, resid_grad, saved, rows, weights):
    length, width = x.shape
    square = length * width
    pack = shaped((length, 2 * width), BF16)
    scratch = [pltpu.VMEM((width, width), BF16)] * 4
    scratch += [pltpu.VMEM((length, width), BF16)] * 2
    scratch += [pltpu.VMEM((heads * length, length), BF16)]
    scratch += [pltpu.VMEM((heads * length, width), BF16)] * 2
    scratch += [pltpu.VMEM((length, width), F32), pltpu.VMEM((3, length, width), BF16), pltpu.VMEM((length, width), F32)]
    scratch += [pltpu.SemaphoreType.DMA((4,)), pltpu.SemaphoreType.DMA((8,))]
    own, other = weights
    return call(
        functools.partial(attention_back_kernel, layer, heads),
        [smem()] + [vmem()] * 8 + [hbm()] * 8,
        (pack, pack, shaped((length, width), BF16), shaped((HEADS_ROWS, width), F32)),
        [hbm(), hbm(), vmem(), vmem()],
        scratch,
        8 * square * width + 10 * heads * length * square,
        8 * width * width + 24 * square,
    )(meta, x, resid_grad, *saved, *rows, *own[:4], *other[:4])


BLOCKS = 8
HALF_BLOCKS = BLOCKS // 2
FFN_BITS = ((1, 2), (2, 4), (4, 1))
ATTN_BITS = ((4, 4), (1, 1), (2, 2))


def hbm():
    return pl.BlockSpec(memory_space=pl.ANY)


def block_shift(bits, core, rank):
    shift = 0
    for pair in bits:
        on = jnp.where(core == 0, (rank & pair[0]) != 0, (rank & pair[1]) != 0)
        shift = shift * 2 + on.astype(jnp.int32)
    return shift


def exchange(array, bits):
    count = lax.axis_size("dp")
    pairs = [(at, at ^ bits[0]) for at in range(count)]
    pairs += [(count + at, count + (at ^ bits[1])) for at in range(count)]
    return lax.ppermute(array, ("section", "dp"), pairs)


def add(left, right):
    return (left.astype(F32) + right.astype(F32)).astype(BF16)


def two_dots(own, other, right_own, right_other):
    return (dot_tn(own, right_own) + dot_tn(other, right_other)).astype(BF16)


def ffn_grad_kernel(shift_ref, first, first2, second, second2, send, keep):
    step = pl.program_id(0)
    relative = (step + HALF_BLOCKS) % BLOCKS
    block = relative ^ shift_ref[0]
    rows, width = keep.shape
    half = first.shape[1] - width

    def emit(value):
        @pl.when(step < HALF_BLOCKS)
        def _():
            send[...] = value

        @pl.when(step >= HALF_BLOCKS)
        def _():
            keep[...] = value

    per = width // rows
    place = jnp.maximum(block - HALF_BLOCKS, 0)
    down = block < HALF_BLOCKS
    left = pl.ds(pl.multiple_of(jnp.where(down, block * rows, half + (place % per) * rows), 128), rows)
    right = pl.ds(pl.multiple_of(jnp.where(down, half, (place // per) * width), 128), width)
    emit(two_dots(first[:, left], first2[:, left], second[:, right], second2[:, right]))


def attn_grad_kernel(shift_ref, both, both2, pack, pack2, send, keep):
    step = pl.program_id(0)
    relative = (step + HALF_BLOCKS) % BLOCKS
    block = relative ^ shift_ref[0]
    rows = keep.shape[0]
    which = block // 2
    left = pl.ds(pl.multiple_of(jnp.where(which == 3, 2 * rows, 0) + (block % 2) * rows, 128), rows)
    right = pl.ds(pl.multiple_of(which * rows, 128), rows)
    value = two_dots(both[:, left], both2[:, left], pack[:, right], pack2[:, right])

    @pl.when(step < HALF_BLOCKS)
    def _():
        send[...] = value

    @pl.when(step >= HALF_BLOCKS)
    def _():
        keep[...] = value


def grad_blocks(kernel, shift, factors, rows, width):
    whole = lambda array: pl.BlockSpec(array.shape, lambda step, shift_ref: (0, 0))
    out = jax.ShapeDtypeStruct((HALF_BLOCKS * rows, width), BF16)
    tokens = 2 * factors[0].shape[0]
    return pl.pallas_call(
        kernel,
        out_shape=(out, out),
        grid_spec=pltpu.PrefetchScalarGridSpec(
            num_scalar_prefetch=1,
            grid=(BLOCKS,),
            in_specs=[whole(array) for array in factors],
            out_specs=[
                pl.BlockSpec((rows, width), lambda step, shift_ref: (jnp.minimum(step, HALF_BLOCKS - 1), 0)),
                pl.BlockSpec((rows, width), lambda step, shift_ref: (jnp.maximum(step - HALF_BLOCKS, 0), 0)),
            ],
        ),
        compiler_params=pltpu.CompilerParams(vmem_limit_bytes=48 << 20),
        cost_estimate=pl.CostEstimate(
            flops=2 * tokens * BLOCKS * rows * width, bytes_accessed=2 * BLOCKS * rows * width, transcendentals=0
        ),
    )(shift.reshape(1), *factors)


def reduce_blocks(send, keep, bits):
    for at, pair in enumerate(bits):
        got = exchange(send, pair)
        if at + 1 < len(bits):
            half = keep.shape[0] // 2
            send, keep = add(keep[half:], got[half:]), add(keep[:half], got[:half])
        else:
            total = add(keep, got)
    return total


def finish_sum(total):
    bit = 8
    while bit < lax.axis_size("dp"):
        total = add(total, exchange(total, (bit, bit)))
        bit *= 2
    return total


def gather_blocks(total, bits):
    for pair in bits[:0:-1]:
        total = jnp.concatenate([total, exchange(total, pair)], axis=0)
    return total, exchange(total, bits[0])


def unpack_kernel(place, meta, *refs):
    sources, rest = refs[:8], refs[8:]
    outs, (taken, given, taken_sem, given_sem) = rest[:-4], rest[-4:]
    core = meta[0]
    rows = taken.shape[1]
    steps = 2 * BLOCKS

    def fetch(step):
        half, relative = divmod(step, BLOCKS)
        slot = step % 2
        for layer in range(2):
            for swapped in range(2):
                source = sources[4 * layer + 2 * swapped + relative // HALF_BLOCKS]
                window = source.at[pl.ds((relative % HALF_BLOCKS) * rows, rows)]

                @pl.when((core == layer) & ((half == core) == (swapped == 0)))
                def _():
                    pltpu.make_async_copy(window, taken.at[slot], taken_sem.at[slot]).start()

    def store(step, start):
        half, relative = divmod(step, BLOCKS)
        slot = step % 2
        block = relative ^ meta[1 + half]
        for chosen, window in place(half, block, outs):
            @pl.when(chosen)
            def _():
                copy = pltpu.make_async_copy(given.at[slot], window, given_sem.at[slot])
                copy.start() if start else copy.wait()

    fetch(0)
    for step in range(steps):
        slot = step % 2
        if step + 1 < steps:
            fetch(step + 1)
        pltpu.make_async_copy(sources[0].at[pl.ds(0, rows)], taken.at[slot], taken_sem.at[slot]).wait()
        if step >= 2:
            store(step - 2, False)
        given[slot] = taken[slot].astype(F32)
        store(step, True)
    store(steps - 2, False)
    store(steps - 1, False)


def place_ffn(half, block, outs):
    grad_in, grad_out = outs
    width, hidden = grad_in.shape[1:]
    rows = hidden // BLOCKS
    per = width // rows
    inner = jnp.maximum(block - HALF_BLOCKS, 0)
    at_out = pl.multiple_of(half * (hidden // 2) + jnp.minimum(block, HALF_BLOCKS - 1) * rows, rows)
    at_row = pl.multiple_of((inner % per) * rows, rows)
    at_column = pl.multiple_of(half * (hidden // 2) + (inner // per) * width, 128)
    return [
        (block < HALF_BLOCKS, grad_out.at[0, pl.ds(at_out, rows), :]),
        (block >= HALF_BLOCKS, grad_in.at[0, pl.ds(at_row, rows), pl.ds(at_column, width)]),
    ]


def place_attn(half, block, outs):
    width = outs[0].shape[1]
    rows = width // 2
    at_row = pl.multiple_of((block % 2) * rows, rows)
    return [
        (block // 2 == which, outs[which].at[0, pl.ds(at_row, rows), pl.ds(half * rows, rows)]) for which in range(4)
    ]


def unpack(place, meta, sources, outs):
    rows = sources[0].shape[0] // HALF_BLOCKS
    width = sources[0].shape[1]
    return pl.pallas_call(
        functools.partial(unpack_kernel, place),
        out_shape=outs,
        in_specs=[pl.BlockSpec(memory_space=pltpu.SMEM)] + [hbm()] * 8,
        out_specs=[hbm()] * len(outs),
        scratch_shapes=[
            pltpu.VMEM((2, rows, width), BF16),
            pltpu.VMEM((2, rows, width), F32),
            pltpu.SemaphoreType.DMA((2,)),
            pltpu.SemaphoreType.DMA((2,)),
        ],
        compiler_params=pltpu.CompilerParams(vmem_limit_bytes=32 << 20),
        cost_estimate=pl.CostEstimate(
            flops=0, bytes_accessed=12 * BLOCKS * rows * width, transcendentals=0
        ),
    )(meta, *sources)


def after(values, done):
    return lax.optimization_barrier(tuple(values) + tuple(done))[: len(values)]


def param_rows(gain_attn, gain_ffn, mix_pre, mix_post):
    heads = mix_pre.shape[1]
    width = gain_attn.shape[1]
    spread = lambda mix: jnp.repeat(mix, width // heads, axis=1)
    rows = jnp.concatenate([gain_attn, gain_ffn, spread(mix_pre[0]), spread(mix_post[0].T)], axis=0)
    return jnp.pad(rows, ((0, HEADS_ROWS - rows.shape[0]), (0, 0)))


def local(
    inputs, cotangent, lengths, w_query, w_key, w_value, w_output, w_in, w_out, gain_attn, gain_ffn, mix_pre, mix_post,
):
    core = lax.axis_index("section")
    rank = lax.axis_index("dp")
    is_first = core == 0
    swap = lambda shard: lax.ppermute(shard, "section", [(0, 1), (1, 0)])
    length, width = inputs.shape[2:]
    hidden = w_in.shape[2]
    heads = mix_pre.shape[1]

    own_rows = param_rows(gain_attn, gain_ffn, mix_pre, mix_post)
    own = (w_query, w_key, w_value, w_output, w_in, w_out)
    other_rows = swap(own_rows)
    other = tuple(swap(weight) for weight in own[:4])
    other += tuple(swap(weight) for weight in after(own[4:], other))
    rows = (own_rows, other_rows)
    weights = (own, other)
    take = lambda whole: lax.dynamic_index_in_dim(whole, core, 0, keepdims=False)[0]
    count = take(lengths)
    meta = jnp.stack([core, count]).astype(jnp.int32)

    ffn_shift = block_shift(FFN_BITS, core, rank)
    attn_shift = block_shift(ATTN_BITS, core, rank)

    def ffn_blocks(first, second):
        factors = (first[0], swap(first[1]), second[0], swap(second[1]))
        return grad_blocks(ffn_grad_kernel, ffn_shift, factors, hidden // BLOCKS, width)

    def attn_blocks(both, pack):
        factors = (both, swap(both), pack[0], swap(pack[1]))
        return grad_blocks(attn_grad_kernel, attn_shift, factors, width // 2, width // 2)

    start0 = take(inputs)
    both0, *qkvp0, residual0, stats_a0 = attention_forward(0, heads, meta, start0, rows, weights)
    mid, own0, send0, slope0, stats_f0 = ffn_forward(0, meta, residual0, rows, weights)
    both1, *qkvp1, residual1, stats_a1 = attention_forward(1, heads, meta, mid, rows, weights)
    last, own1, send1, own1b, send1b, resid1, stats_f1 = ffn_forward(
        1, meta, residual1, rows, weights, take(cotangent)
    )
    ffn1 = ffn_blocks((own1, send1), (own1b, send1b))
    (resid1,) = after((resid1,), ffn1)
    pack1, send_pack1, grad1, stats_b1 = attention_backward(1, heads, meta, mid, resid1, qkvp1, rows, weights)
    own0b, send0b, resid0, stats_g0 = ffn_backward(0, meta, residual0, grad1, slope0, rows, weights)
    (both1,) = after((both1,), (resid0,))
    attn1 = attn_blocks(both1, (pack1, send_pack1))
    (own0,) = after((own0,), attn1)
    ffn0 = ffn_blocks((own0, send0), (own0b, send0b))
    (resid0,) = after((resid0,), ffn0)
    pack0, send_pack0, grad0, stats_b0 = attention_backward(0, heads, meta, start0, resid0, qkvp0, rows, weights)
    attn0 = attn_blocks(both0, (pack0, send_pack0))

    gathered = [None, None]
    for index, ffn_pair, attn_pair in ((1, ffn1, attn1), (0, ffn0, attn0)):
        ffn_sum = finish_sum(reduce_blocks(*ffn_pair, FFN_BITS))
        attn_sum = finish_sum(reduce_blocks(*attn_pair, ATTN_BITS))
        ffn_parts = gather_blocks(ffn_sum, FFN_BITS)
        attn_parts = gather_blocks(attn_sum, ATTN_BITS)
        hand = lambda array: lax.ppermute(array, "section", [(1 - index, index)])
        gathered[index] = (
            ffn_parts + tuple(hand(part) for part in ffn_parts),
            attn_parts + tuple(hand(part) for part in attn_parts),
        )

    def shifts(bits):
        return jnp.stack([core, block_shift(bits, 0, rank), block_shift(bits, 1, rank)]).astype(jnp.int32)

    w_in_grad, w_out_grad = unpack(
        place_ffn,
        shifts(FFN_BITS),
        gathered[0][0] + gathered[1][0],
        (jax.ShapeDtypeStruct(w_in.shape, F32), jax.ShapeDtypeStruct(w_out.shape, F32)),
    )
    rest = unpack(
        place_attn,
        shifts(ATTN_BITS),
        gathered[0][1] + gathered[1][1],
        tuple(jax.ShapeDtypeStruct(w_query.shape, F32) for _ in range(4)),
    )

    def small_sums(back, gain_row, attn_row, ffn_rows):
        mixes = back.reshape(HEADS_ROWS, heads, width // heads).sum(axis=-1)
        at = HEADS_ROWS // 2
        squares = jnp.stack([ffn_rows[0], attn_row, ffn_rows[1]]).sum(axis=-1) / width
        return [back[heads], gain_row, mixes[:heads].reshape(-1), mixes[at : at + heads].T.reshape(-1), squares]

    parts = small_sums(stats_b0, stats_g0[0], stats_a0[0], stats_f0)
    parts += small_sums(stats_b1, stats_f1[2], stats_a1[0], stats_f1)
    tail = jnp.concatenate(parts + [count[None].astype(F32)])
    size = tail.shape[0]
    tail = jnp.pad(tail, (0, -size % 1024)).reshape(-1, 128)
    tail = tail + swap(tail)
    bit = 1
    while bit < lax.axis_size("dp"):
        tail = tail + exchange(tail, (bit, bit))
        bit *= 2
    tail = tail.reshape(-1)
    tokens = tail[size - 1]
    each = (size - 1) // 2
    tail = jnp.where(is_first, tail[:each], tail[each : 2 * each])
    square = heads * heads
    at = 2 * width
    rms = jnp.sqrt(tail[at + 2 * square : at + 2 * square + 3] / tokens)[None]

    def put(pair):
        mine = jnp.where(is_first, pair[0], pair[1])
        theirs = swap(jnp.where(is_first, pair[1], pair[0]))
        ordered = [jnp.where(is_first, mine, theirs), jnp.where(is_first, theirs, mine)]
        return jnp.stack(ordered)[None, :, None]

    return (
        put((mid, last)),
        put((grad0, grad1)),
        rest[0],
        rest[1],
        rest[2],
        rest[3],
        w_in_grad,
        w_out_grad,
        tail[None, :width],
        tail[None, width:at],
        tail[at : at + square].reshape(1, heads, heads),
        tail[at + square : at + 2 * square].reshape(1, heads, heads),
        rms,
    )


def solution(mesh):
    in_specs = (
        P(None, "dp", None, None),
        P(None, "dp", None, None),
        P(None, "dp"),
        P("section", None, None),
        P("section", None, None),
        P("section", None, None),
        P("section", None, None),
        P("section", None, None),
        P("section", None, None),
        P("section", None),
        P("section", None),
        P("section", None, None),
        P("section", None, None),
    )
    out_specs = (
        P("section", None, "dp", None, None),
        P("section", None, "dp", None, None),
        P("section", None, None),
        P("section", None, None),
        P("section", None, None),
        P("section", None, None),
        P("section", None, None),
        P("section", None, None),
        P("section", None),
        P("section", None),
        P("section", None, None),
        P("section", None, None),
        P("section", None),
    )
    return jax.shard_map(local, mesh=mesh, in_specs=in_specs, out_specs=out_specs, check_vma=False)
```

```python
import functools

import jax
import jax.numpy as jnp
from jax import lax
from jax.experimental import pallas as pl
from jax.experimental.pallas import tpu as pltpu
from jax.sharding import PartitionSpec as P

EPSILON = 1e-06
MASKED = -1e30
F32 = jnp.float32
BF16 = jnp.bfloat16


HEADS_ROWS = 32
GROUP = 2
VMEM = 60 << 20
SPAN = 1536


def row_scale(values):
    return lax.rsqrt(jnp.mean(values * values, axis=-1, keepdims=True) + EPSILON)


def norm_back(values, gain, grad):
    scale = row_scale(values)
    weighted = grad * gain
    inner = jnp.mean(values * weighted, axis=-1, keepdims=True)
    grad_values = scale * weighted - values * (scale * scale * scale) * inner
    return grad_values, jnp.sum(grad * values * scale, axis=0, keepdims=True)


def gelu_pair(values):
    square = values * values
    tanh = jnp.tanh(values * (0.7978845608028654 + 0.7978845608028654 * 0.044715 * square))
    half = 0.5 * (1.0 + tanh)
    slope = half + 0.5 * values * (1.0 - tanh * tanh) * (
        0.7978845608028654 + 3.0 * 0.7978845608028654 * 0.044715 * square
    )
    return values * half, slope


def dot_nn(left, right):
    return lax.dot_general(left, right, (((1,), (0,)), ((), ())), preferred_element_type=F32)


def dot_nt(left, right):
    return lax.dot_general(left, right, (((1,), (1,)), ((), ())), preferred_element_type=F32)


def dot_tn(left, right):
    return lax.dot_general(left, right, (((0,), (0,)), ((), ())), preferred_element_type=F32)


class Weight:
    def __init__(self, mine, own, other, held, sem):
        self.mine, self.own, self.other, self.held, self.sem = mine, own, other, held, sem

    def copy(self, source, cut):
        return pltpu.make_async_copy(source.at[(0,) + cut], self.held.at[cut], self.sem)

    def start(self, cut=(slice(None), slice(None))):
        @pl.when(self.mine)
        def _():
            self.copy(self.own, cut).start()

        @pl.when(jnp.logical_not(self.mine))
        def _():
            self.copy(self.other, cut).start()

    def wait(self, cut=(slice(None), slice(None))):
        self.copy(self.own, cut).wait()


def param_row(mine, own, other, at, count=1):
    rows = pl.ds(at, count)
    return jnp.where(mine, own[rows, :], other[rows, :])


def attention_kernel(
    layer, heads, meta, x, own_rows, other_rows, wq, wk, wv, wo, wq2, wk2, wv2, wo2,
    both_out, query_out, key_out, value_out, probs_out, residual_out, stats_out,
    held_q, held_k, held_v, held_o, keys_upper, keys_lower, values_mixed, sems,
):
    mine = meta[0] == layer
    weights = [
        Weight(mine, own, other, held, sems.at[at])
        for at, (own, other, held) in enumerate(
            ((wq, wq2, held_q), (wk, wk2, held_k), (wv, wv2, held_v), (wo, wo2, held_o))
        )
    ]
    for weight in weights:
        weight.start()
    length, width = x.shape
    half = length // 2
    values = x[...].astype(F32)
    gain = param_row(mine, own_rows, other_rows, 0)
    both_out[:, :width] = (values * row_scale(values) * gain).astype(BF16)
    for weight, held, out, factor in (
        (weights[0], held_q, query_out, (width // heads) ** -0.5),
        (weights[1], held_k, key_out, 1.0),
        (weights[2], held_v, value_out, 1.0),
    ):
        weight.wait()
        made = dot_nn(both_out[:, :width], held[...]).astype(BF16)
        out[...] = (made.astype(F32) * factor).astype(BF16) if factor != 1.0 else made

    def softmax(logits, first):
        rows = lax.broadcasted_iota(jnp.int32, logits.shape, 0)
        columns = lax.broadcasted_iota(jnp.int32, logits.shape, 1) + first
        logits = jnp.where(rows <= columns, logits, MASKED)
        exponent = jnp.exp(logits - jnp.max(logits, axis=0, keepdims=True))
        return (exponent * (1.0 / jnp.sum(exponent, axis=0, keepdims=True))).astype(BF16)

    for first in range(0, heads, GROUP):
        for at in range(first, first + GROUP):
            mixed = key_out[...].astype(F32) * param_row(mine, own_rows, other_rows, 2 + at)
            high = mixed.astype(BF16)
            low = (mixed - high.astype(F32)).astype(BF16)
            place = (at - first) * half
            for which, part in enumerate((high, low)):
                keys_upper[which, place : place + half, :] = part[:half]
                keys_lower[which, place : place + half, :] = part[half:]
        upper = dot_nt(keys_upper[0], query_out[...]) + dot_nt(keys_upper[1], query_out[...])
        lower = dot_nt(keys_lower[0], query_out[half:, :]) + dot_nt(keys_lower[1], query_out[half:, :])
        for at in range(first, first + GROUP):
            row = at * length
            part = slice((at - first) * half, (at - first + 1) * half)
            probs_out[row : row + half, :half] = softmax(upper[part, :half], 0)
            probs_out[row + half : row + length, :half] = jnp.zeros((length - half, half), BF16)
            late = jnp.concatenate([upper[part, half:], lower[part]], axis=0)
            probs_out[row : row + length, half:] = softmax(late, half)
            scale = param_row(mine, own_rows, other_rows, 2 + heads + at)
            values_mixed[row : row + length, :] = value_out[...] * scale.astype(BF16)
    both_out[:, width:] = dot_tn(probs_out[...], values_mixed[...]).astype(BF16)
    weights[3].wait()
    branch = dot_nn(both_out[:, width:], held_o[...])
    residual_out[...] = values + branch
    valid = lax.broadcasted_iota(jnp.int32, (length, 1), 0) < meta[1]
    stats_out[...] = jnp.broadcast_to(
        jnp.sum(jnp.where(valid, branch * branch, 0.0), axis=0, keepdims=True), stats_out.shape
    )


def ffn_kernel(
    layer, backward, meta, residual, own_rows, other_rows, w_in, w_out, w_in2, w_out2, *refs
):
    if backward:
        upstream, refs = refs[0], refs[1:]
        out, own_first, send_first, own_second, send_second, resid_out, stats_out = refs[:7]
        held_in, held_out, normed, act, total, pre_grad, branch_grad, back_total, sems, out_sems = refs[7:]
    else:
        out, own_first, send_first, slope_out, stats_out = refs[:5]
        held_in, held_out, normed, act, total, sems, out_sems = refs[5:]
    core = meta[0]
    mine = core == layer
    length, width = residual.shape
    hidden = held_in.shape[1]
    steps = hidden // SPAN
    half = hidden // 2
    cuts_in = [(slice(None), pl.ds(step * SPAN, SPAN)) for step in range(steps)]
    cuts_out = [(pl.ds(step * SPAN, SPAN), slice(None)) for step in range(steps)]
    ins = [Weight(mine, w_in, w_in2, held_in, sems.at[step]) for step in range(steps)]
    outs = [Weight(mine, w_out, w_out2, held_out, sems.at[steps + step]) for step in range(steps)]
    for step in range(steps):
        ins[step].start(cuts_in[step])
        outs[step].start(cuts_out[step])
    values = residual[...]
    normed[...] = (values * row_scale(values) * param_row(mine, own_rows, other_rows, 1)).astype(BF16)
    valid = lax.broadcasted_iota(jnp.int32, (length, 1), 0) < meta[1]
    copies = []

    def send(source, target, at):
        copy = pltpu.make_async_copy(source, target, out_sems.at[at])
        copy.start()
        copies.append(copy)

    send(normed, own_first.at[:, pl.ds(half, width)], 0)
    send(normed, send_first.at[:, pl.ds(half, width)], 1)
    if backward:
        branch_grad[...] = jnp.where(valid, upstream[...], jnp.zeros_like(upstream))
        send(branch_grad, own_second.at[:, pl.ds(half, width)], 2)
        send(branch_grad, send_second.at[:, pl.ds(half, width)], 3)
    for step in range(steps):
        span = pl.ds(step * SPAN, SPAN)
        ins[step].wait(cuts_in[step])
        made, slope = gelu_pair(dot_nn(normed[...], held_in[:, span]))
        act[:, span] = made.astype(BF16)
        outs[step].wait(cuts_out[step])
        part = dot_nn(act[:, span], held_out[span, :])
        total[...] = part if step == 0 else total[...] + part
        if backward:
            grad = (dot_nt(branch_grad[...], held_out[span, :]) * slope).astype(BF16)
            pre_grad[:, span] = grad
            part = dot_nt(pre_grad[:, span], held_in[:, span])
            back_total[...] = part if step == 0 else back_total[...] + part
        else:
            slope_out[:, span] = slope.astype(BF16)
    mine_at = pl.ds(pl.multiple_of(core * half, 128), half)
    other_at = pl.ds(pl.multiple_of((1 - core) * half, 128), half)
    send(act.at[:, mine_at], own_first.at[:, pl.ds(0, half)], 4)
    send(act.at[:, other_at], send_first.at[:, pl.ds(0, half)], 5)
    if backward:
        send(pre_grad.at[:, mine_at], own_second.at[:, pl.ds(0, half)], 6)
        send(pre_grad.at[:, other_at], send_second.at[:, pl.ds(0, half)], 7)
    branch = total[...]
    made = jnp.where(valid, residual[...] + branch, 0.0)
    out[...] = made.astype(BF16)
    stats_out[0:1, :] = jnp.sum(made * made, axis=0, keepdims=True)
    stats_out[1:2, :] = jnp.sum(jnp.where(valid, branch * branch, 0.0), axis=0, keepdims=True)
    if backward:
        back, gain_grad = norm_back(
            residual[...], param_row(mine, own_rows, other_rows, 1), back_total[...]
        )
        resid_out[...] = branch_grad[...].astype(F32) + back
        stats_out[2:3, :] = gain_grad
    for copy in copies:
        copy.wait()


def ffn_back_kernel(
    layer, meta, residual, upstream, slope, own_rows, other_rows, w_in, w_out, w_in2, w_out2,
    own_second, send_second, resid_out, stats_out,
    held_in, held_out, pre_grad, branch_grad, back_total, sems, out_sems,
):
    core = meta[0]
    mine = core == layer
    length, width = residual.shape
    hidden = held_in.shape[1]
    steps = hidden // SPAN
    half = hidden // 2
    cuts_in = [(slice(None), pl.ds(step * SPAN, SPAN)) for step in range(steps)]
    cuts_out = [(pl.ds(step * SPAN, SPAN), slice(None)) for step in range(steps)]
    ins = [Weight(mine, w_in, w_in2, held_in, sems.at[step]) for step in range(steps)]
    outs = [Weight(mine, w_out, w_out2, held_out, sems.at[steps + step]) for step in range(steps)]
    for step in range(steps):
        outs[step].start(cuts_out[step])
        ins[step].start(cuts_in[step])
    valid = lax.broadcasted_iota(jnp.int32, (length, 1), 0) < meta[1]
    branch_grad[...] = jnp.where(valid, upstream[...], jnp.zeros_like(upstream))
    copies = []

    def send(source, target, at):
        copy = pltpu.make_async_copy(source, target, out_sems.at[at])
        copy.start()
        copies.append(copy)

    send(branch_grad, own_second.at[:, pl.ds(half, width)], 0)
    send(branch_grad, send_second.at[:, pl.ds(half, width)], 1)
    for step in range(steps):
        span = pl.ds(step * SPAN, SPAN)
        outs[step].wait(cuts_out[step])
        grad = dot_nt(branch_grad[...], held_out[span, :]) * slope[:, span].astype(F32)
        pre_grad[:, span] = grad.astype(BF16)
        ins[step].wait(cuts_in[step])
        part = dot_nt(pre_grad[:, span], held_in[:, span])
        back_total[...] = part if step == 0 else back_total[...] + part
    send(pre_grad.at[:, pl.ds(pl.multiple_of(core * half, 128), half)], own_second.at[:, pl.ds(0, half)], 2)
    send(pre_grad.at[:, pl.ds(pl.multiple_of((1 - core) * half, 128), half)], send_second.at[:, pl.ds(0, half)], 3)
    back, gain_grad = norm_back(residual[...], param_row(mine, own_rows, other_rows, 1), back_total[...])
    resid_out[...] = branch_grad[...].astype(F32) + back
    stats_out[0:1, :] = gain_grad
    for copy in copies:
        copy.wait()


def attention_back_kernel(
    layer, heads, meta, x, resid_grad, query, key, value, probs, own_rows, other_rows,
    wq, wk, wv, wo, wq2, wk2, wv2, wo2,
    own_pack, send_pack, grad_out, stats_out,
    held_q, held_k, held_v, held_o, attn_grad, head_grad, logit_grad, key_scaled, value_scaled,
    key_grad, value_grad, piece, total, sems, out_sems,
):
    core = meta[0]
    mine = core == layer
    weights = [
        Weight(mine, own, other, held, sems.at[at])
        for at, (own, other, held) in enumerate(
            ((wo, wo2, held_o), (wq, wq2, held_q), (wk, wk2, held_k), (wv, wv2, held_v))
        )
    ]
    for weight in weights:
        weight.start()
    length, width = x.shape
    half = width // 2
    copies = []

    def send(source, at, sem):
        for target, which in ((own_pack, core), (send_pack, 1 - core)):
            copy = pltpu.make_async_copy(
                source.at[:, pl.ds(pl.multiple_of(which * half, 128), half)],
                target.at[:, pl.ds(at * half, half)],
                out_sems.at[sem + (0 if target is own_pack else 1)],
            )
            copy.start()
            copies.append(copy)

    attn_grad[...] = resid_grad[...].astype(BF16)
    send(attn_grad, 3, 0)
    weights[0].wait()
    head_grad[...] = dot_nt(attn_grad[...], held_o[...]).astype(BF16)

    for first in range(0, heads, GROUP):
        span = slice(first * length, (first + GROUP) * length)
        pres, posts = [], []
        for at in range(first, first + GROUP):
            pres.append(param_row(mine, own_rows, other_rows, 2 + at))
            posts.append(param_row(mine, own_rows, other_rows, 2 + heads + at))
            rows = slice(at * length, (at + 1) * length)
            key_scaled[rows, :] = key[...] * pres[-1].astype(BF16)
            place = (at - first) * length
            value_scaled[place : place + length, :] = value[...] * posts[-1].astype(BF16)
        grad_probs = dot_nt(value_scaled[...], head_grad[...])
        routed = dot_nn(probs[span, :], head_grad[...])
        for at in range(first, first + GROUP):
            part = slice((at - first) * length, (at - first + 1) * length)
            prob = probs[at * length : (at + 1) * length, :].astype(F32)
            inner = jnp.sum(prob * grad_probs[part], axis=0, keepdims=True)
            logit_grad[at * length : (at + 1) * length, :] = (prob * (grad_probs[part] - inner)).astype(BF16)
            stats_out[HEADS_ROWS // 2 + at : HEADS_ROWS // 2 + at + 1, :] = jnp.sum(
                routed[part] * value[...].astype(F32), axis=0, keepdims=True
            )
            more = routed[part] * posts[at - first]
            value_grad[...] = more if at == 0 else value_grad[...] + more
        routed = dot_nn(logit_grad[span, :], query[...])
        for at in range(first, first + GROUP):
            part = slice((at - first) * length, (at - first + 1) * length)
            stats_out[at : at + 1, :] = jnp.sum(routed[part] * key[...].astype(F32), axis=0, keepdims=True)
            more = routed[part] * pres[at - first]
            key_grad[...] = more if at == 0 else key_grad[...] + more
    piece[2] = value_grad[...].astype(BF16)
    send(piece.at[2], 2, 6)
    piece[1] = key_grad[...].astype(BF16)
    send(piece.at[1], 1, 4)
    weights[3].wait()
    total[...] = dot_nt(piece[2], held_v[...])
    weights[2].wait()
    total[...] += dot_nt(piece[1], held_k[...])
    factor = (width // heads) ** -0.5
    piece[0] = (dot_tn(logit_grad[...], key_scaled[...]) * factor).astype(BF16)
    send(piece.at[0], 0, 2)
    weights[1].wait()
    back, gain_grad = norm_back(
        x[...].astype(F32),
        param_row(mine, own_rows, other_rows, 0),
        total[...] + dot_nt(piece[0], held_q[...]),
    )
    grad_out[...] = (resid_grad[...] + back).astype(BF16)
    stats_out[heads : heads + 1, :] = gain_grad
    for copy in copies:
        copy.wait()


def vmem():
    return pl.BlockSpec(memory_space=pltpu.VMEM)


def smem():
    return pl.BlockSpec(memory_space=pltpu.SMEM)


def shaped(shape, kind):
    return jax.ShapeDtypeStruct(shape, kind)


def call(kernel, in_specs, outs, out_specs, scratch, flops, bytes_accessed):
    return pl.pallas_call(
        kernel,
        out_shape=outs,
        in_specs=in_specs,
        out_specs=out_specs,
        scratch_shapes=scratch,
        compiler_params=pltpu.CompilerParams(vmem_limit_bytes=VMEM),
        cost_estimate=pl.CostEstimate(flops=flops, bytes_accessed=bytes_accessed, transcendentals=0) if flops else LIGHT,
    )


def attention_forward(layer, heads, meta, x, rows, weights):
    length, width = x.shape
    square = length * width
    outs = (
        shaped((length, 2 * width), BF16),
        shaped((length, width), BF16),
        shaped((length, width), BF16),
        shaped((length, width), BF16),
        shaped((heads * length, length), BF16),
        shaped((length, width), F32),
        shaped((8, width), F32),
    )
    scratch = [pltpu.VMEM((width, width), BF16)] * 4
    scratch += [pltpu.VMEM((2, GROUP * length // 2, width), BF16)] * 2
    scratch += [pltpu.VMEM((heads * length, width), BF16), pltpu.SemaphoreType.DMA((4,))]
    kernel = functools.partial(attention_kernel, layer, heads)
    run = call(
        kernel, [smem(), vmem(), vmem(), vmem()] + [hbm()] * 8, outs, [vmem()] * 7, scratch,
        8 * square * width + 6 * heads * length * square, 8 * width * width + 20 * square,
    )
    own, other = weights
    return run(meta, x, *rows, *own[:4], *other[:4])


def ffn_forward(layer, meta, residual, rows, weights, upstream=None):
    length, width = residual.shape
    hidden = weights[0][4].shape[2]
    half = hidden // 2
    pack = shaped((length, half + width), BF16)
    steps = hidden // SPAN
    held = [pltpu.VMEM((width, hidden), BF16), pltpu.VMEM((hidden, width), BF16)]
    held += [pltpu.VMEM((length, width), BF16), pltpu.VMEM((length, hidden), BF16), pltpu.VMEM((length, width), F32)]
    sems = [pltpu.SemaphoreType.DMA((2 * steps,)), pltpu.SemaphoreType.DMA((8,))]
    ins = [smem(), vmem(), vmem(), vmem()] + [hbm()] * 4
    work = 4 * length * width * hidden
    moved = 4 * width * hidden + 8 * length * hidden
    own, other = weights
    args = (meta, residual) + rows + own[4:6] + other[4:6]
    if upstream is None:
        outs = (shaped((length, width), BF16), pack, pack, shaped((length, hidden), BF16), shaped((8, width), F32))
        specs = [vmem(), hbm(), hbm(), vmem(), vmem()]
        return call(functools.partial(ffn_kernel, layer, False), ins, outs, specs, held + sems, work, moved)(*args)
    outs = (shaped((length, width), BF16), pack, pack, pack, pack, shaped((length, width), F32), shaped((8, width), F32))
    specs = [vmem()] + [hbm()] * 4 + [vmem()] * 2
    held += [pltpu.VMEM((length, hidden), BF16), pltpu.VMEM((length, width), BF16), pltpu.VMEM((length, width), F32)]
    kernel = functools.partial(ffn_kernel, layer, True)
    return call(kernel, ins + [vmem()], outs, specs, held + sems, 2 * work, moved)(*args, upstream)


def ffn_backward(layer, meta, residual, upstream, slope, rows, weights):
    length, width = residual.shape
    hidden = slope.shape[1]
    pack = shaped((length, hidden // 2 + width), BF16)
    steps = hidden // SPAN
    scratch = [pltpu.VMEM((width, hidden), BF16), pltpu.VMEM((hidden, width), BF16)]
    scratch += [pltpu.VMEM((length, hidden), BF16), pltpu.VMEM((length, width), BF16), pltpu.VMEM((length, width), F32)]
    scratch += [pltpu.SemaphoreType.DMA((2 * steps,)), pltpu.SemaphoreType.DMA((4,))]
    own, other = weights
    return call(
        functools.partial(ffn_back_kernel, layer),
        [smem()] + [vmem()] * 5 + [hbm()] * 4,
        (pack, pack, shaped((length, width), F32), shaped((8, width), F32)),
        [hbm(), hbm(), vmem(), vmem()],
        scratch,
        0,
        0,
    )(meta, residual, upstream, slope, *rows, *own[4:6], *other[4:6])


def attention_backward(layer, heads, meta, x, resid_grad, saved, rows, weights):
    length, width = x.shape
    square = length * width
    pack = shaped((length, 2 * width), BF16)
    scratch = [pltpu.VMEM((width, width), BF16)] * 4
    scratch += [pltpu.VMEM((length, width), BF16)] * 2
    scratch += [pltpu.VMEM((heads * length, length), BF16)]
    scratch += [pltpu.VMEM((heads * length, width), BF16), pltpu.VMEM((GROUP * length, width), BF16)]
    scratch += [pltpu.VMEM((length, width), F32)] * 2
    scratch += [pltpu.VMEM((3, length, width), BF16), pltpu.VMEM((length, width), F32)]
    scratch += [pltpu.SemaphoreType.DMA((4,)), pltpu.SemaphoreType.DMA((8,))]
    own, other = weights
    return call(
        functools.partial(attention_back_kernel, layer, heads),
        [smem()] + [vmem()] * 8 + [hbm()] * 8,
        (pack, pack, shaped((length, width), BF16), shaped((HEADS_ROWS, width), F32)),
        [hbm(), hbm(), vmem(), vmem()],
        scratch,
        0,
        0,
    )(meta, x, resid_grad, *saved, *rows, *own[:4], *other[:4])


LIGHT = pl.CostEstimate(flops=1, bytes_accessed=1, transcendentals=0)
BLOCKS = 8
HALF_BLOCKS = BLOCKS // 2
FFN_BITS = ((1, 2), (2, 4), (4, 1))
ATTN_BITS = ((4, 4), (1, 1), (2, 2))
ORDER = (
    "P1w K1 D0 Q1w",
    "P0w K0 T0 Q1a1",
    "P1a1 Q0w P1a2 Q1a2",
    "L1a3 P0a1 Q0a1 P0a2",
    "Q0a2 L1ax L0a3 O0",
    "O1 G0 G1 L0ax",
    "g3 g2 g1 uA",
    "uB T1 uC",
)


def hbm():
    return pl.BlockSpec(memory_space=pl.ANY)


def block_shift(bits, core, rank):
    shift = 0
    for pair in bits:
        on = jnp.where(core == 0, (rank & pair[0]) != 0, (rank & pair[1]) != 0)
        shift = shift * 2 + on.astype(jnp.int32)
    return shift


def exchange(array, bits):
    count = lax.axis_size("dp")
    pairs = [(at, at ^ bits[0]) for at in range(count)]
    pairs += [(count + at, count + (at ^ bits[1])) for at in range(count)]
    return lax.ppermute(array, ("section", "dp"), pairs)


def add(left, right):
    return (left.astype(F32) + right.astype(F32)).astype(BF16)


def grad_kernel(locate, meta, first, first2, second, second2, send, keep, lefts, rights, made, in_sems, out_sems):
    length = first.shape[0]
    rows = made.shape[1]
    fetched = []
    for at, (source, target) in enumerate(((first, lefts), (second, rights), (first2, lefts), (second2, rights))):
        window = target.at[pl.ds((at // 2) * length, length)]
        fetched.append(pltpu.make_async_copy(source, window, in_sems.at[at]))
        fetched[-1].start()
    for copy in fetched:
        copy.wait()
    stored = []
    for step in range(BLOCKS):
        block = ((step + HALF_BLOCKS) % BLOCKS) ^ meta[0]
        left, right = locate(block)
        made[step] = dot_tn(lefts[:, left], rights[:, right]).astype(BF16)
        target = send if step < HALF_BLOCKS else keep
        window = target.at[pl.ds((step % HALF_BLOCKS) * rows, rows)]
        stored.append(pltpu.make_async_copy(made.at[step], window, out_sems.at[step]))
        stored[-1].start()
    for copy in stored:
        copy.wait()


def locate_ffn(rows, width, half, block):
    per = width // rows
    place = jnp.maximum(block - HALF_BLOCKS, 0)
    down = block < HALF_BLOCKS
    left = pl.multiple_of(jnp.where(down, block * rows, half + (place % per) * rows), 128)
    right = pl.multiple_of(jnp.where(down, half, (place // per) * width), 128)
    return pl.ds(left, rows), pl.ds(right, width)


def locate_attn(rows, block):
    which = block // 2
    left = pl.multiple_of(jnp.where(which == 3, 2 * rows, 0) + (block % 2) * rows, 128)
    return pl.ds(left, rows), pl.ds(pl.multiple_of(which * rows, 128), rows)


def grad_blocks(locate, shift, factors, rows, width):
    first, first2, second, second2 = factors
    out = shaped((HALF_BLOCKS * rows, width), BF16)
    length = first.shape[0]
    return light_call(
        functools.partial(grad_kernel, locate),
        (out, out),
        [smem()] + [hbm()] * 4,
        [hbm()] * 2,
        scratch=[
            pltpu.VMEM((2 * length, first.shape[1]), BF16),
            pltpu.VMEM((2 * length, second.shape[1]), BF16),
            pltpu.VMEM((BLOCKS, rows, width), BF16),
            pltpu.SemaphoreType.DMA((4,)),
            pltpu.SemaphoreType.DMA((BLOCKS,)),
        ],
    )(shift.reshape(1), *factors)


def light_call(kernel, outs, in_specs, out_specs, grid=(), scratch=(), aliases=None):
    return pl.pallas_call(
        kernel,
        out_shape=outs,
        grid=grid,
        in_specs=in_specs,
        out_specs=out_specs,
        scratch_shapes=list(scratch),
        input_output_aliases=aliases or {},
        compiler_params=pltpu.CompilerParams(vmem_limit_bytes=VMEM),
        cost_estimate=LIGHT,
    )


def put_ride(total, send, rows):
    count = total.shape[0]
    width = total.shape[1]
    high = total.astype(BF16)
    send[rows : rows + count, :width] = high
    send[rows + count :, :width] = (total - high.astype(F32)).astype(BF16)


def take_ride(total, got, rows):
    count, width = total.shape
    return total + got[rows : rows + count, :width].astype(F32) + got[rows + count :, :width].astype(F32)


def add_split_kernel(*refs):
    count = len(refs) // 6
    for at in range(count):
        keep_low, keep_high, got_low, got_high = refs[4 * at : 4 * at + 4]
        send, keep = refs[4 * count + 2 * at : 4 * count + 2 * at + 2]
        keep[...] = add(keep_low[...], got_low[...])
        send[...] = add(keep_high[...], got_high[...])


def add_split(pairs):
    args, in_specs, outs, out_specs = [], [], [], []
    for keep, got in pairs:
        rows, width = keep.shape
        low = pl.BlockSpec((rows // 4, width), lambda at: (at, 0))
        high = pl.BlockSpec((rows // 4, width), lambda at: (at + 2, 0))
        args += [keep, keep, got, got]
        in_specs += [low, high, low, high]
        outs += [shaped((rows // 2, width), BF16)] * 2
        out_specs += [low, low]
    made = light_call(add_split_kernel, outs, in_specs, out_specs, (2,))(*args)
    return list(zip(made[0::2], made[1::2]))


def add_split_ride_kernel(riding, keep_in, got, tail, more, send, keep, tail_out):
    rows = keep.shape[0]
    keep[...] = add(keep_in[:rows, :], got[:rows, :])
    send[:rows, :] = add(keep_in[rows:, :], got[rows : 2 * rows, :])
    total = take_ride(tail[...], got, 2 * rows) if riding else tail[...] + more[...]
    tail_out[...] = total
    put_ride(total, send, rows)


def add_split_ride(keep, got, tail, more=None):
    rows, width = keep.shape
    half = rows // 2
    count = 2 * tail.shape[0]
    outs = (shaped((half + count, width), BF16), shaped((half, width), BF16), shaped(tail.shape, F32))
    kernel = functools.partial(add_split_ride_kernel, more is None)
    return light_call(kernel, outs, [vmem()] * 4, [vmem()] * 3)(keep, got, tail, tail if more is None else more)


def add_pack_kernel(keep, got, keep2, got2, *refs):
    rows, width = keep.shape
    out = refs[-1]
    if len(refs) > 1:
        tail, tail_out, out = refs
        total = take_ride(tail[...], got, rows)
        tail_out[...] = total
        put_ride(total, out, rows)
        out[rows:, width:] = jnp.zeros((out.shape[0] - rows, out.shape[1] - width), BF16)
    out[:rows, :width] = add(keep[...], got[:rows, :])
    out[:rows, width:] = add(keep2[...], got2[...])


def add_pack(first, second, tail=None):
    rows, width = first[0].shape
    more = 0 if tail is None else 2 * tail.shape[0]
    out = shaped((rows + more, width + second[0].shape[1]), BF16)
    if tail is None:
        return light_call(add_pack_kernel, out, [vmem()] * 4, vmem())(*first, *second)
    outs = (shaped(tail.shape, F32), out)
    return light_call(add_pack_kernel, outs, [vmem()] * 5, [vmem()] * 2)(*first, *second, tail)


def add_sum_kernel(left, right, *refs):
    if len(refs) > 1:
        tail, out, tail_out = refs
        tail_out[...] = take_ride(tail[...], right, out.shape[0])
    else:
        (out,) = refs
    rows = out.shape[0]
    out[...] = add(left[:rows, :], right[:rows, :])


def add_sum(left, right, tail=None):
    more = 0 if tail is None else 2 * tail.shape[0]
    out = shaped((left.shape[0] - more, left.shape[1]), BF16)
    if tail is None:
        return light_call(add_sum_kernel, out, [vmem()] * 2, vmem())(left, right)
    outs = (out, shaped(tail.shape, F32))
    return light_call(add_sum_kernel, outs, [vmem()] * 3, [vmem()] * 2)(left, right, tail)


def choose_kernel(meta, first, second, first_other, second_other, *outs):
    width = outs[0].shape[1]
    for core, pair in ((0, (first, first_other)), (1, (second, second_other))):
        @pl.when(meta[0] == core)
        def _():
            for at, source in enumerate(pair):
                outs[2 * at][...] = source[:, :width]
                outs[2 * at + 1][...] = source[:, width:]


def choose(meta, arrays, width):
    rows, both = arrays[0].shape
    outs = [shaped((rows, width), BF16), shaped((rows, both - width), BF16)] * 2
    return light_call(choose_kernel, outs, [smem()] + [vmem()] * 4, [vmem()] * 4)(meta, *arrays)


def add_kernel(left, right, out):
    out[...] = add(left[...], right[...]) if out.dtype == BF16 else left[...] + right[...]


def light_add(left, right):
    return light_call(add_kernel, shaped(left.shape, left.dtype), [vmem()] * 2, vmem())(left, right)


def join_kernel(count, *refs):
    outs = refs[-count:]
    for at in range(count):
        rows = refs[2 * at].shape[0]
        outs[at][:rows] = refs[2 * at][...]
        outs[at][rows : 2 * rows] = refs[2 * at + 1][...]
    if len(refs) > 3 * count:
        put_ride(refs[2 * count][...], outs[0], 2 * refs[0].shape[0])


def join(pairs, tail=None):
    outs = [shaped((2 * upper.shape[0], upper.shape[1]), upper.dtype) for upper, _ in pairs]
    args = [array for pair in pairs for array in pair]
    if tail is not None:
        args.append(tail)
        outs[0] = shaped((outs[0].shape[0] + 2 * tail.shape[0], outs[0].shape[1]), BF16)
    kernel = functools.partial(join_kernel, len(pairs))
    return light_call(kernel, outs, [vmem()] * len(args), [vmem()] * len(outs))(*args)


def pick_kernel(meta, first, second, out):
    @pl.when(meta[0] == 0)
    def _():
        out[...] = second[...]

    @pl.when(meta[0] == 1)
    def _():
        out[...] = first[...]


def pick(meta, first, second):
    return light_call(pick_kernel, shaped(first.shape, first.dtype), [smem(), vmem(), vmem()], vmem())(
        meta, first, second
    )


def lay_kernel(meta, first, second, other, out):
    for at, mine in ((0, first), (1, second)):
        @pl.when(meta[0] == at)
        def _():
            out[0, at, 0] = mine[...]
            out[0, 1 - at, 0] = other[...]


def lay(meta, first, second, other):
    out = shaped((1, 2, 1) + first.shape, first.dtype)
    return light_call(lay_kernel, out, [smem()] + [vmem()] * 3, vmem())(meta, first, second, other)


def collect_kernel(heads, meta, back0, gain0, attn0, ffn0, back1, attn1, ffn1, keep, send):
    width = keep.shape[1]
    at = HEADS_ROWS // 2
    count = jnp.full((1, width), meta[1], jnp.int32).astype(F32)
    for layer, back, gain, attn, ffn in ((0, back0, gain0[0:1, :], attn0, ffn0), (1, back1, ffn1[2:3, :], attn1, ffn1)):
        rows = jnp.concatenate(
            [
                back[: heads + 1, :], gain, jnp.zeros((at - heads - 2, width), F32), back[at : at + heads, :],
                ffn[0:1, :], attn[0:1, :], ffn[1:2, :], count,
            ],
            axis=0,
        )

        @pl.when(meta[0] == layer)
        def _():
            keep[...] = rows

        @pl.when(meta[0] != layer)
        def _():
            send[...] = rows


def collect(heads, meta, *stats):
    out = jax.ShapeDtypeStruct((HEADS_ROWS, stats[0].shape[1]), F32)
    return pl.pallas_call(
        functools.partial(collect_kernel, heads),
        out_shape=(out, out),
        in_specs=[smem()] + [vmem()] * len(stats),
        out_specs=[vmem()] * 2,
        cost_estimate=LIGHT,
    )(meta, *stats)


def small_kernel(heads, tail, got, attn_out, ffn_out, pre_out, post_out, rms_out):
    width = tail.shape[1]
    total = take_ride(tail[...], got, 0)
    at = HEADS_ROWS // 2
    attn_out[...] = total[heads : heads + 1, :]
    ffn_out[...] = total[heads + 1 : heads + 2, :]
    lane = lax.broadcasted_iota(jnp.int32, (width, heads), 0) // (width // heads)
    ones = (lane == lax.broadcasted_iota(jnp.int32, (width, heads), 1)).astype(F32)
    high = lax.Precision.HIGHEST
    pre_out[0] = lax.dot_general(
        total[:heads, :], ones, (((1,), (0,)), ((), ())), precision=high, preferred_element_type=F32
    )
    post_out[0] = lax.dot_general(
        ones, total[at : at + heads, :], (((0,), (1,)), ((), ())), precision=high, preferred_element_type=F32
    )
    tokens = total[HEADS_ROWS - 1 : HEADS_ROWS, 0:1]
    for which in range(3):
        row = total[at + heads + which : at + heads + which + 1, :]
        rms_out[:, which : which + 1] = jnp.sqrt(jnp.sum(row, axis=1, keepdims=True) / width / tokens)


def small_outputs(heads, tail, got):
    width = tail.shape[1]
    shapes = ((1, width), (1, width), (1, heads, heads), (1, heads, heads), (1, 3))
    return pl.pallas_call(
        functools.partial(small_kernel, heads),
        out_shape=tuple(jax.ShapeDtypeStruct(shape, F32) for shape in shapes),
        cost_estimate=LIGHT,
    )(tail, got)


def unpack_kernel(part, owns, meta, *refs):
    count = 2 * len(owns)
    sources, outs, scratch = refs[:count], refs[count + 6 : count + 12], refs[count + 12 :]
    taken_ffn, given_ffn, taken_attn, given_attn, taken_sem, given_sem = scratch
    core = meta[0]
    moves = []
    for which, own in enumerate(owns):
        half = core if own else 1 - core
        for group, (taken, given, place, grads) in enumerate((
            (taken_ffn, given_ffn, place_ffn, outs[:2]), (taken_attn, given_attn, place_attn, outs[2:]),
        )):
            rows = taken.shape[1]
            shift = jnp.where(half == 0, meta[1 + 2 * group], meta[2 + 2 * group])
            for step in range(HALF_BLOCKS):
                slot = HALF_BLOCKS * which + step
                at = BLOCKS * group + slot
                block = (HALF_BLOCKS * part + step) ^ shift
                window = sources[2 * which + group].at[pl.ds(step * rows, rows)]
                fetch = pltpu.make_async_copy(window, taken.at[slot], taken_sem.at[at])
                stores = [
                    (chosen, pltpu.make_async_copy(given.at[slot], target, given_sem.at[at]))
                    for chosen, target in place(half, block, grads)
                ]
                moves.append((fetch, stores, taken, given, slot))
    for fetch, *_ in moves:
        fetch.start()
    for fetch, stores, taken, given, slot in moves:
        fetch.wait()
        given[slot] = taken[slot].astype(F32)
        for chosen, copy in stores:
            pl.when(chosen)(copy.start)
    for _, stores, *_ in moves:
        for chosen, copy in stores:
            pl.when(chosen)(copy.wait)


def unpack(part, owns, meta, sources, outs):
    scratch = []
    for source, rows in zip(sources, (outs[0].shape[2] // BLOCKS, outs[2].shape[1] // 2)):
        width = source.shape[1]
        scratch += [pltpu.VMEM((BLOCKS, rows, width), BF16), pltpu.VMEM((BLOCKS, rows, width), F32)]
    scratch += [pltpu.SemaphoreType.DMA((2 * BLOCKS,))] * 2
    return light_call(
        functools.partial(unpack_kernel, part, owns),
        [shaped(out.shape, F32) for out in outs],
        [smem()] + [hbm()] * (len(sources) + len(outs)),
        [hbm()] * len(outs),
        scratch=scratch,
        aliases={1 + len(sources) + at: at for at in range(len(outs))},
    )(meta, *sources, *outs)


def blank_kernel(*refs):
    pass


def blank(shapes):
    return pl.pallas_call(
        blank_kernel,
        out_shape=tuple(jax.ShapeDtypeStruct(shape, F32) for shape in shapes),
        out_specs=[hbm()] * len(shapes),
        cost_estimate=LIGHT,
    )()


def place_ffn(half, block, outs):
    grad_in, grad_out = outs
    width, hidden = grad_in.shape[1:]
    rows = hidden // BLOCKS
    per = width // rows
    inner = jnp.maximum(block - HALF_BLOCKS, 0)
    at_out = pl.multiple_of(half * (hidden // 2) + jnp.minimum(block, HALF_BLOCKS - 1) * rows, rows)
    at_row = pl.multiple_of((inner % per) * rows, rows)
    at_column = pl.multiple_of(half * (hidden // 2) + (inner // per) * width, 128)
    return [
        (block < HALF_BLOCKS, grad_out.at[0, pl.ds(at_out, rows), :]),
        (block >= HALF_BLOCKS, grad_in.at[0, pl.ds(at_row, rows), pl.ds(at_column, width)]),
    ]


def place_attn(half, block, outs):
    width = outs[0].shape[1]
    rows = width // 2
    at_row = pl.multiple_of((block % 2) * rows, rows)
    return [
        (block // 2 == which, outs[which].at[0, pl.ds(at_row, rows), pl.ds(half * rows, rows)]) for which in range(4)
    ]


def after(values, done):
    return lax.optimization_barrier(tuple(values) + tuple(done))[: len(values)]


def param_rows(gain_attn, gain_ffn, mix_pre, mix_post):
    heads = mix_pre.shape[1]
    width = gain_attn.shape[1]
    spread = lambda mix: jnp.repeat(mix, width // heads, axis=1)
    rows = jnp.concatenate([gain_attn, gain_ffn, spread(mix_pre[0]), spread(mix_post[0].T)], axis=0)
    return jnp.pad(rows, ((0, HEADS_ROWS - rows.shape[0]), (0, 0)))


def local(
    inputs, cotangent, lengths, w_query, w_key, w_value, w_output, w_in, w_out, gain_attn, gain_ffn, mix_pre, mix_post,
):
    core = lax.axis_index("section")
    rank = lax.axis_index("dp")
    is_first = core == 0
    swap = lambda shard: lax.ppermute(shard, "section", [(0, 1), (1, 0)])
    length, width = inputs.shape[2:]
    hidden = w_in.shape[2]
    heads = mix_pre.shape[1]

    own_rows = param_rows(gain_attn, gain_ffn, mix_pre, mix_post)
    own = (w_query, w_key, w_value, w_output, w_in, w_out)
    other_rows = swap(own_rows)
    other = tuple(swap(weight) for weight in own[:4])
    other += tuple(swap(weight) for weight in after(own[4:], other))
    rows = (own_rows, other_rows)
    weights = (own, other)
    take = lambda whole: lax.dynamic_index_in_dim(whole, core, 0, keepdims=False)[0]
    count = take(lengths)
    meta = jnp.stack([core, count]).astype(jnp.int32)

    ffn_shift = block_shift(FFN_BITS, core, rank)
    attn_shift = block_shift(ATTN_BITS, core, rank)

    steps = {}
    state = {"last": ()}

    def tie(value):
        return after((value,), state["last"])[0] if state["last"] else value

    def chain(layer, make_ffn, make_attn):
        bits = (FFN_BITS, ATTN_BITS)
        keep, got, whole = [None, None], [None, None], {}
        riding = layer == 0

        def made(group, make):
            def run():
                send, keep[group] = make()
                got[group] = exchange(send, bits[group][0])
                return keep[group]
            return run

        def split(at, groups):
            def run():
                keep[groups[0]] = tie(keep[groups[0]])
                if riding and groups == (0,):
                    send, kept, made_all["tail"] = add_split_ride(
                        keep[0], got[0], made_all["tail"], made_all["more"] if at == 1 else None
                    )
                    parts = [(send, kept)]
                else:
                    parts = add_split([(keep[group], got[group]) for group in groups])
                for group, (send, kept) in zip(groups, parts):
                    keep[group] = kept
                    got[group] = exchange(send, bits[group][at])
                return keep[groups[0]]
            return run

        def third():
            keep[0] = tie(keep[0])
            pairs = ((keep[0], got[0]), (keep[1], got[1]))
            if riding:
                made_all["tail"], whole["sum"] = add_pack(*pairs, made_all["tail"])
            else:
                whole["sum"] = add_pack(*pairs)
            whole["got"] = exchange(whole["sum"], (8, 8))
            return whole["sum"]

        def summed():
            total, more, bit = tie(whole["sum"]), whole["got"], 16
            while bit < lax.axis_size("dp"):
                rows = keep[0].shape[0]
                summed_rows = add(total[:rows], more[:rows])
                if riding:
                    tail = made_all["tail"]
                    tail = tail + more[rows : rows + HEADS_ROWS, :width].astype(F32)
                    tail = tail + more[rows + HEADS_ROWS :, :width].astype(F32)
                    high = tail.astype(BF16)
                    terms = jnp.concatenate([high, (tail - high.astype(F32)).astype(BF16)], axis=0)
                    made_all["tail"] = tail
                    terms = jnp.pad(terms, ((0, 0), (0, total.shape[1] - width)))
                    summed_rows = jnp.concatenate([summed_rows, terms], axis=0)
                total = summed_rows
                more = exchange(total, (bit, bit))
                bit *= 2
            if riding:
                made_all[layer], made_all["tail"] = add_sum(total, more, made_all["tail"])
            else:
                made_all[layer] = add_sum(total, more)
            made_all["hand", layer] = lax.ppermute(made_all[layer], "section", [(1 - layer, layer)])
            return made_all[layer]

        name = str(layer)
        steps.update({
            "P" + name + "w": made(0, make_ffn), "Q" + name + "w": made(1, make_attn),
            "P" + name + "a1": split(1, (0,)), "Q" + name + "a1": split(1, (1,)), "L" + name + "a1": split(1, (0, 1)),
            "P" + name + "a2": split(2, (0,)), "Q" + name + "a2": split(2, (1,)), "L" + name + "a2": split(2, (0, 1)),
            "L" + name + "a3": third, "L" + name + "ax": summed,
        })

    def gather():
        bits = [FFN_BITS, ATTN_BITS] + [[pair[::-1] for pair in group] for group in (FFN_BITS, ATTN_BITS)]
        held, got = [None] * 4, [None] * 4

        def send(at):
            got[:] = [exchange(held[part], bits[part][at]) for part in range(4)]
            return held[0]

        def start():
            arrays = (tie(made_all[0]), made_all[1], made_all["hand", 0], made_all["hand", 1])
            held[:] = choose(meta, arrays, width)
            return send(2)

        def joined(at):
            def run():
                pairs = [(tie(held[0]), got[0])] + list(zip(held[1:], got[1:]))
                held[:] = join(pairs, made_all["tail"] if at == 0 else None)
                return send(at)
            return run

        def first():
            made_all["grads"] = unpack(0, (True, False), place_meta, (tie(held[0]), *held[1:]), made_all["grads"])
            return made_all["grads"][0]

        def second(own):
            def run():
                pair = got[:2] if own else got[2:]
                made_all["grads"] = unpack(1, (own,), place_meta, (tie(pair[0]), pair[1]), made_all["grads"])
                return made_all["grads"][0]
            return run

        def small_end():
            rows = HALF_BLOCKS * (hidden // BLOCKS)
            made["small"] = small_outputs(heads, tie(made_all["tail"]), got[0][rows:])
            return made["small"][0]

        steps.update({
            "g3": start, "g2": joined(1), "g1": joined(0), "uA": first, "uB": second(True), "uC": second(False), "T1": small_end,
        })

    def ffn_blocks(first, second):
        factors = (tie(first[0]), first[1], second[0], swap(second[1]))
        locate = functools.partial(locate_ffn, hidden // BLOCKS, width, hidden // 2)
        return grad_blocks(locate, ffn_shift, factors, hidden // BLOCKS, width)

    def attn_blocks(both, pack):
        factors = (tie(both[0]), both[1], pack[0], swap(pack[1]))
        locate = functools.partial(locate_attn, width // 2)
        return grad_blocks(locate, attn_shift, factors, width // 2, width // 2)

    start0 = take(inputs)
    both0, *qkvp0, residual0, stats_a0 = attention_forward(0, heads, meta, start0, rows, weights)
    mid, own0, send0, slope0, stats_f0 = ffn_forward(0, meta, residual0, rows, weights)
    both0_other, send0_other = swap(both0), swap(send0)
    both1, *qkvp1, residual1, stats_a1 = attention_forward(1, heads, meta, mid, rows, weights)
    (residual1,) = after((residual1,), (both0_other, send0_other))
    both1_other = swap(both1)
    last, own1, send1, own1b, send1b, resid1, stats_f1 = ffn_forward(
        1, meta, residual1, rows, weights, take(cotangent)
    )
    own1, send1_other = after((own1, swap(send1)), (both1_other,))
    made = {}

    def attention1():
        made["pack1"], made["send_pack1"], made["grad1"], made["stats_b1"] = attention_backward(
            1, heads, meta, mid, tie(resid1), qkvp1, rows, weights
        )
        return made["grad1"]

    def ffn0():
        made["own0b"], made["send0b"], made["resid0"], made["stats_g0"] = ffn_backward(
            0, meta, residual0, tie(made["grad1"]), slope0, rows, weights
        )
        return made["resid0"]

    def attention0():
        made["pack0"], made["send_pack0"], made["grad0"], made["stats_b0"] = attention_backward(
            0, heads, meta, start0, tie(made["resid0"]), qkvp0, rows, weights
        )
        return made["grad0"]

    steps.update({"K1": attention1, "D0": ffn0, "K0": attention0})
    place_meta = jnp.stack(
        [core] + [block_shift(bits, which, rank) for bits in (FFN_BITS, ATTN_BITS) for which in range(2)]
    ).astype(jnp.int32)
    made_all = {"grads": blank((w_in.shape, w_out.shape) + (w_query.shape,) * 4)}
    chain(
        1,
        lambda: ffn_blocks((own1, send1_other), (own1b, send1b)),
        lambda: attn_blocks((both1, both1_other), (made["pack1"], made["send_pack1"])),
    )
    chain(
        0,
        lambda: ffn_blocks((own0, send0_other), (made["own0b"], made["send0b"])),
        lambda: attn_blocks((both0, both0_other), (made["pack0"], made["send_pack0"])),
    )

    def small_start():
        made_all["tail"], send = collect(
            heads, meta, tie(made["stats_b0"]), made["stats_g0"], stats_a0, stats_f0, made["stats_b1"], stats_a1, stats_f1
        )
        made_all["more"] = swap(send)
        return made_all["tail"]

    def send_rows(name, first, second):
        def run():
            made[name] = swap(pick(meta, tie(first()), second()))
            return first()
        return run

    def lay_rows(name, first, second):
        def run():
            made[name] = lay(meta, tie(first()), second(), made[name])
            return made[name]
        return run

    mids = ("outputs", lambda: mid, lambda: last)
    grads = ("grads", lambda: made["grad0"], lambda: made["grad1"])
    steps.update({"O0": send_rows(*mids), "O1": lay_rows(*mids), "G0": send_rows(*grads), "G1": lay_rows(*grads)})
    steps["T0"] = small_start
    gather()
    for name in [name for line in ORDER for name in line.split()]:
        with jax.named_scope(name):
            state["last"] = (steps[name](),)

    w_in_grad, w_out_grad, *rest = made_all["grads"]
    return (made["outputs"], made["grads"], *rest, w_in_grad, w_out_grad, *made["small"])


def solution(mesh):
    in_specs = (
        P(None, "dp", None, None),
        P(None, "dp", None, None),
        P(None, "dp"),
        P("section", None, None),
        P("section", None, None),
        P("section", None, None),
        P("section", None, None),
        P("section", None, None),
        P("section", None, None),
        P("section", None),
        P("section", None),
        P("section", None, None),
        P("section", None, None),
    )
    out_specs = (
        P("section", None, "dp", None, None),
        P("section", None, "dp", None, None),
        P("section", None, None),
        P("section", None, None),
        P("section", None, None),
        P("section", None, None),
        P("section", None, None),
        P("section", None, None),
        P("section", None),
        P("section", None),
        P("section", None, None),
        P("section", None, None),
        P("section", None),
    )
    return jax.shard_map(local, mesh=mesh, in_specs=in_specs, out_specs=out_specs, check_vma=False)
```

```python
import functools

import jax
import jax.numpy as jnp
from jax import lax
from jax.experimental import pallas as pl
from jax.experimental.pallas import tpu as pltpu
from jax.sharding import PartitionSpec as P

EPSILON = 1e-06
MASKED = -1e30
F32 = jnp.float32
BF16 = jnp.bfloat16


HEADS_ROWS = 32
GROUP = 2
VMEM = 60 << 20
SPAN = 1536


def row_scale(values):
    return lax.rsqrt(jnp.mean(values * values, axis=-1, keepdims=True) + EPSILON)


def norm_back(values, gain, grad):
    scale = row_scale(values)
    weighted = grad * gain
    inner = jnp.mean(values * weighted, axis=-1, keepdims=True)
    grad_values = scale * weighted - values * (scale * scale * scale) * inner
    return grad_values, jnp.sum(grad * values * scale, axis=0, keepdims=True)


def gelu_pair(values):
    square = values * values
    tanh = jnp.tanh(values * (0.7978845608028654 + 0.7978845608028654 * 0.044715 * square))
    half = 0.5 * (1.0 + tanh)
    slope = half + 0.5 * values * (1.0 - tanh * tanh) * (
        0.7978845608028654 + 3.0 * 0.7978845608028654 * 0.044715 * square
    )
    return values * half, slope


def dot_nn(left, right):
    return lax.dot_general(left, right, (((1,), (0,)), ((), ())), preferred_element_type=F32)


def dot_nt(left, right):
    return lax.dot_general(left, right, (((1,), (1,)), ((), ())), preferred_element_type=F32)


def dot_tn(left, right):
    return lax.dot_general(left, right, (((0,), (0,)), ((), ())), preferred_element_type=F32)


def this_core():
    return lax.axis_index("section")


def sequence_rows(array):
    return array.at[this_core(), 0] if len(array.shape) == 4 else array


class Weight:
    def __init__(self, mine, own, other, held, sem):
        self.mine, self.own, self.other, self.held, self.sem = mine, own, other, held, sem

    def copy(self, source, cut):
        return pltpu.make_async_copy(source.at[(0,) + cut], self.held.at[cut], self.sem)

    def start(self, cut=(slice(None), slice(None))):
        @pl.when(self.mine)
        def _():
            self.copy(self.own, cut).start()

        @pl.when(jnp.logical_not(self.mine))
        def _():
            self.copy(self.other, cut).start()

    def wait(self, cut=(slice(None), slice(None))):
        self.copy(self.own, cut).wait()


def param_row(mine, own, other, at, count=1):
    rows = pl.ds(at, count)
    return jnp.where(mine, own[rows, :], other[rows, :])


def attention_kernel(
    layer, heads, lengths, x_in, own_rows, other_rows, wq, wk, wv, wo, wq2, wk2, wv2, wo2,
    both_out, query_out, key_out, value_out, probs_out, residual_out, stats_out,
    held_q, held_k, held_v, held_o, x, keys_upper, keys_lower, values_mixed, sems,
):
    mine = this_core() == layer
    brought = pltpu.make_async_copy(sequence_rows(x_in), x, sems.at[4])
    brought.start()
    weights = [
        Weight(mine, own, other, held, sems.at[at])
        for at, (own, other, held) in enumerate(
            ((wq, wq2, held_q), (wk, wk2, held_k), (wv, wv2, held_v), (wo, wo2, held_o))
        )
    ]
    for weight in weights:
        weight.start()
    length, width = x.shape
    half = length // 2
    brought.wait()
    values = x[...].astype(F32)
    gain = param_row(mine, own_rows, other_rows, 0)
    both_out[:, :width] = (values * row_scale(values) * gain).astype(BF16)
    for weight, held, out, factor in (
        (weights[0], held_q, query_out, (width // heads) ** -0.5),
        (weights[1], held_k, key_out, 1.0),
        (weights[2], held_v, value_out, 1.0),
    ):
        weight.wait()
        made = dot_nn(both_out[:, :width], held[...]).astype(BF16)
        out[...] = (made.astype(F32) * factor).astype(BF16) if factor != 1.0 else made

    def softmax(logits, first):
        rows = lax.broadcasted_iota(jnp.int32, logits.shape, 0)
        columns = lax.broadcasted_iota(jnp.int32, logits.shape, 1) + first
        logits = jnp.where(rows <= columns, logits, MASKED)
        exponent = jnp.exp(logits - jnp.max(logits, axis=0, keepdims=True))
        return (exponent * (1.0 / jnp.sum(exponent, axis=0, keepdims=True))).astype(BF16)

    for first in range(0, heads, GROUP):
        for at in range(first, first + GROUP):
            mixed = key_out[...].astype(F32) * param_row(mine, own_rows, other_rows, 2 + at)
            high = mixed.astype(BF16)
            low = (mixed - high.astype(F32)).astype(BF16)
            place = (at - first) * half
            for which, part in enumerate((high, low)):
                keys_upper[which, place : place + half, :] = part[:half]
                keys_lower[which, place : place + half, :] = part[half:]
        upper = dot_nt(keys_upper[0], query_out[...]) + dot_nt(keys_upper[1], query_out[...])
        lower = dot_nt(keys_lower[0], query_out[half:, :]) + dot_nt(keys_lower[1], query_out[half:, :])
        for at in range(first, first + GROUP):
            row = at * length
            part = slice((at - first) * half, (at - first + 1) * half)
            probs_out[row : row + half, :half] = softmax(upper[part, :half], 0)
            probs_out[row + half : row + length, :half] = jnp.zeros((length - half, half), BF16)
            late = jnp.concatenate([upper[part, half:], lower[part]], axis=0)
            probs_out[row : row + length, half:] = softmax(late, half)
            scale = param_row(mine, own_rows, other_rows, 2 + heads + at)
            values_mixed[row : row + length, :] = value_out[...] * scale.astype(BF16)
    both_out[:, width:] = dot_tn(probs_out[...], values_mixed[...]).astype(BF16)
    weights[3].wait()
    branch = dot_nn(both_out[:, width:], held_o[...])
    residual_out[...] = values + branch
    valid = lax.broadcasted_iota(jnp.int32, (length, 1), 0) < lengths[this_core(), 0]
    stats_out[...] = jnp.broadcast_to(
        jnp.sum(jnp.where(valid, branch * branch, 0.0), axis=0, keepdims=True), stats_out.shape
    )


def ffn_kernel(
    layer, backward, lengths, residual, own_rows, other_rows, w_in, w_out, w_in2, w_out2, *refs
):
    if backward:
        upstream_in, refs = refs[0], refs[1:]
        out, own_first, send_first, own_second, send_second, resid_out, stats_out = refs[:7]
        held_in, held_out, normed, act, total, pre_grad, branch_grad, back_total, upstream, sems, out_sems = refs[7:]
        brought = pltpu.make_async_copy(sequence_rows(upstream_in), upstream, out_sems.at[8])
        brought.start()
    else:
        out, own_first, send_first, slope_out, stats_out = refs[:5]
        held_in, held_out, normed, act, total, sems, out_sems = refs[5:]
    core = this_core()
    mine = core == layer
    length, width = residual.shape
    hidden = held_in.shape[1]
    steps = hidden // SPAN
    half = hidden // 2
    cuts_in = [(slice(None), pl.ds(step * SPAN, SPAN)) for step in range(steps)]
    cuts_out = [(pl.ds(step * SPAN, SPAN), slice(None)) for step in range(steps)]
    ins = [Weight(mine, w_in, w_in2, held_in, sems.at[step]) for step in range(steps)]
    outs = [Weight(mine, w_out, w_out2, held_out, sems.at[steps + step]) for step in range(steps)]
    for step in range(steps):
        ins[step].start(cuts_in[step])
        outs[step].start(cuts_out[step])
    values = residual[...]
    normed[...] = (values * row_scale(values) * param_row(mine, own_rows, other_rows, 1)).astype(BF16)
    valid = lax.broadcasted_iota(jnp.int32, (length, 1), 0) < lengths[core, 0]
    copies = []

    def send(source, target, at):
        copy = pltpu.make_async_copy(source, target, out_sems.at[at])
        copy.start()
        copies.append(copy)

    send(normed, own_first.at[:, pl.ds(half, width)], 0)
    send(normed, send_first.at[:, pl.ds(half, width)], 1)
    if backward:
        brought.wait()
        branch_grad[...] = jnp.where(valid, upstream[...], jnp.zeros_like(upstream))
        send(branch_grad, own_second.at[:, pl.ds(half, width)], 2)
        send(branch_grad, send_second.at[:, pl.ds(half, width)], 3)
    for step in range(steps):
        span = pl.ds(step * SPAN, SPAN)
        ins[step].wait(cuts_in[step])
        made, slope = gelu_pair(dot_nn(normed[...], held_in[:, span]))
        act[:, span] = made.astype(BF16)
        outs[step].wait(cuts_out[step])
        part = dot_nn(act[:, span], held_out[span, :])
        total[...] = part if step == 0 else total[...] + part
        if backward:
            grad = (dot_nt(branch_grad[...], held_out[span, :]) * slope).astype(BF16)
            pre_grad[:, span] = grad
            part = dot_nt(pre_grad[:, span], held_in[:, span])
            back_total[...] = part if step == 0 else back_total[...] + part
        else:
            slope_out[:, span] = slope.astype(BF16)
    mine_at = pl.ds(pl.multiple_of(core * half, 128), half)
    other_at = pl.ds(pl.multiple_of((1 - core) * half, 128), half)
    send(act.at[:, mine_at], own_first.at[:, pl.ds(0, half)], 4)
    send(act.at[:, other_at], send_first.at[:, pl.ds(0, half)], 5)
    if backward:
        send(pre_grad.at[:, mine_at], own_second.at[:, pl.ds(0, half)], 6)
        send(pre_grad.at[:, other_at], send_second.at[:, pl.ds(0, half)], 7)
    branch = total[...]
    made = jnp.where(valid, residual[...] + branch, 0.0)
    out[...] = made.astype(BF16)
    stats_out[0:1, :] = jnp.sum(made * made, axis=0, keepdims=True)
    stats_out[1:2, :] = jnp.sum(jnp.where(valid, branch * branch, 0.0), axis=0, keepdims=True)
    if backward:
        back, gain_grad = norm_back(
            residual[...], param_row(mine, own_rows, other_rows, 1), back_total[...]
        )
        resid_out[...] = branch_grad[...].astype(F32) + back
        stats_out[2:3, :] = gain_grad
    for copy in copies:
        copy.wait()


def ffn_back_kernel(
    layer, lengths, residual, upstream, slope, own_rows, other_rows, w_in, w_out, w_in2, w_out2,
    own_second, send_second, resid_out, stats_out,
    held_in, held_out, pre_grad, branch_grad, back_total, sems, out_sems,
):
    core = this_core()
    mine = core == layer
    length, width = residual.shape
    hidden = held_in.shape[1]
    steps = hidden // SPAN
    half = hidden // 2
    cuts_in = [(slice(None), pl.ds(step * SPAN, SPAN)) for step in range(steps)]
    cuts_out = [(pl.ds(step * SPAN, SPAN), slice(None)) for step in range(steps)]
    ins = [Weight(mine, w_in, w_in2, held_in, sems.at[step]) for step in range(steps)]
    outs = [Weight(mine, w_out, w_out2, held_out, sems.at[steps + step]) for step in range(steps)]
    for step in range(steps):
        outs[step].start(cuts_out[step])
        ins[step].start(cuts_in[step])
    valid = lax.broadcasted_iota(jnp.int32, (length, 1), 0) < lengths[core, 0]
    branch_grad[...] = jnp.where(valid, upstream[...], jnp.zeros_like(upstream))
    copies = []

    def send(source, target, at):
        copy = pltpu.make_async_copy(source, target, out_sems.at[at])
        copy.start()
        copies.append(copy)

    send(branch_grad, own_second.at[:, pl.ds(half, width)], 0)
    send(branch_grad, send_second.at[:, pl.ds(half, width)], 1)
    for step in range(steps):
        span = pl.ds(step * SPAN, SPAN)
        outs[step].wait(cuts_out[step])
        grad = dot_nt(branch_grad[...], held_out[span, :]) * slope[:, span].astype(F32)
        pre_grad[:, span] = grad.astype(BF16)
        ins[step].wait(cuts_in[step])
        part = dot_nt(pre_grad[:, span], held_in[:, span])
        back_total[...] = part if step == 0 else back_total[...] + part
    send(pre_grad.at[:, pl.ds(pl.multiple_of(core * half, 128), half)], own_second.at[:, pl.ds(0, half)], 2)
    send(pre_grad.at[:, pl.ds(pl.multiple_of((1 - core) * half, 128), half)], send_second.at[:, pl.ds(0, half)], 3)
    back, gain_grad = norm_back(residual[...], param_row(mine, own_rows, other_rows, 1), back_total[...])
    resid_out[...] = branch_grad[...].astype(F32) + back
    stats_out[0:1, :] = gain_grad
    for copy in copies:
        copy.wait()


def attention_back_kernel(
    layer, heads, x_in, resid_grad, query, key, value, probs, own_rows, other_rows,
    wq, wk, wv, wo, wq2, wk2, wv2, wo2,
    own_pack, send_pack, grad_out, stats_out,
    held_q, held_k, held_v, held_o, x, attn_grad, head_grad, logit_grad, key_scaled, value_scaled,
    key_grad, value_grad, piece, total, sems, out_sems,
):
    core = this_core()
    brought = pltpu.make_async_copy(sequence_rows(x_in), x, sems.at[4])
    brought.start()
    mine = core == layer
    weights = [
        Weight(mine, own, other, held, sems.at[at])
        for at, (own, other, held) in enumerate(
            ((wo, wo2, held_o), (wq, wq2, held_q), (wk, wk2, held_k), (wv, wv2, held_v))
        )
    ]
    for weight in weights:
        weight.start()
    length, width = x.shape
    half = width // 2
    copies = []

    def send(source, at, sem):
        for target, which in ((own_pack, core), (send_pack, 1 - core)):
            copy = pltpu.make_async_copy(
                source.at[:, pl.ds(pl.multiple_of(which * half, 128), half)],
                target.at[:, pl.ds(at * half, half)],
                out_sems.at[sem + (0 if target is own_pack else 1)],
            )
            copy.start()
            copies.append(copy)

    attn_grad[...] = resid_grad[...].astype(BF16)
    send(attn_grad, 3, 0)
    weights[0].wait()
    head_grad[...] = dot_nt(attn_grad[...], held_o[...]).astype(BF16)

    for first in range(0, heads, GROUP):
        span = slice(first * length, (first + GROUP) * length)
        pres, posts = [], []
        for at in range(first, first + GROUP):
            pres.append(param_row(mine, own_rows, other_rows, 2 + at))
            posts.append(param_row(mine, own_rows, other_rows, 2 + heads + at))
            rows = slice(at * length, (at + 1) * length)
            key_scaled[rows, :] = key[...] * pres[-1].astype(BF16)
            place = (at - first) * length
            value_scaled[place : place + length, :] = value[...] * posts[-1].astype(BF16)
        grad_probs = dot_nt(value_scaled[...], head_grad[...])
        routed = dot_nn(probs[span, :], head_grad[...])
        for at in range(first, first + GROUP):
            part = slice((at - first) * length, (at - first + 1) * length)
            prob = probs[at * length : (at + 1) * length, :].astype(F32)
            inner = jnp.sum(prob * grad_probs[part], axis=0, keepdims=True)
            logit_grad[at * length : (at + 1) * length, :] = (prob * (grad_probs[part] - inner)).astype(BF16)
            stats_out[HEADS_ROWS // 2 + at : HEADS_ROWS // 2 + at + 1, :] = jnp.sum(
                routed[part] * value[...].astype(F32), axis=0, keepdims=True
            )
            more = routed[part] * posts[at - first]
            value_grad[...] = more if at == 0 else value_grad[...] + more
        routed = dot_nn(logit_grad[span, :], query[...])
        for at in range(first, first + GROUP):
            part = slice((at - first) * length, (at - first + 1) * length)
            stats_out[at : at + 1, :] = jnp.sum(routed[part] * key[...].astype(F32), axis=0, keepdims=True)
            more = routed[part] * pres[at - first]
            key_grad[...] = more if at == 0 else key_grad[...] + more
    piece[2] = value_grad[...].astype(BF16)
    send(piece.at[2], 2, 6)
    piece[1] = key_grad[...].astype(BF16)
    send(piece.at[1], 1, 4)
    weights[3].wait()
    total[...] = dot_nt(piece[2], held_v[...])
    weights[2].wait()
    total[...] += dot_nt(piece[1], held_k[...])
    factor = (width // heads) ** -0.5
    piece[0] = (dot_tn(logit_grad[...], key_scaled[...]) * factor).astype(BF16)
    send(piece.at[0], 0, 2)
    weights[1].wait()
    brought.wait()
    back, gain_grad = norm_back(
        x[...].astype(F32),
        param_row(mine, own_rows, other_rows, 0),
        total[...] + dot_nt(piece[0], held_q[...]),
    )
    grad_out[...] = (resid_grad[...] + back).astype(BF16)
    stats_out[heads : heads + 1, :] = gain_grad
    for copy in copies:
        copy.wait()


def vmem():
    return pl.BlockSpec(memory_space=pltpu.VMEM)


def smem():
    return pl.BlockSpec(memory_space=pltpu.SMEM)


def shaped(shape, kind):
    return jax.ShapeDtypeStruct(shape, kind)


def call(kernel, in_specs, outs, out_specs, scratch, flops, bytes_accessed):
    return pl.pallas_call(
        kernel,
        out_shape=outs,
        in_specs=in_specs,
        out_specs=out_specs,
        scratch_shapes=scratch,
        compiler_params=pltpu.CompilerParams(vmem_limit_bytes=VMEM),
        cost_estimate=pl.CostEstimate(flops=flops, bytes_accessed=bytes_accessed, transcendentals=0) if flops else LIGHT,
    )


def attention_forward(layer, heads, lengths, x, rows, weights):
    length, width = x.shape[-2:]
    square = length * width
    outs = (
        shaped((length, 2 * width), BF16),
        shaped((length, width), BF16),
        shaped((length, width), BF16),
        shaped((length, width), BF16),
        shaped((heads * length, length), BF16),
        shaped((length, width), F32),
        shaped((8, width), F32),
    )
    scratch = [pltpu.VMEM((width, width), BF16)] * 4 + [pltpu.VMEM((length, width), BF16)]
    scratch += [pltpu.VMEM((2, GROUP * length // 2, width), BF16)] * 2
    scratch += [pltpu.VMEM((heads * length, width), BF16), pltpu.SemaphoreType.DMA((5,))]
    kernel = functools.partial(attention_kernel, layer, heads)
    run = call(
        kernel, [smem(), hbm(), vmem(), vmem()] + [hbm()] * 8, outs, [vmem()] * 7, scratch,
        8 * square * width + 6 * heads * length * square, 8 * width * width + 20 * square,
    )
    own, other = weights
    return run(lengths, x, *rows, *own[:4], *other[:4])


def ffn_forward(layer, lengths, residual, rows, weights, upstream=None):
    length, width = residual.shape
    hidden = weights[0][4].shape[2]
    half = hidden // 2
    pack = shaped((length, half + width), BF16)
    steps = hidden // SPAN
    held = [pltpu.VMEM((width, hidden), BF16), pltpu.VMEM((hidden, width), BF16)]
    held += [pltpu.VMEM((length, width), BF16), pltpu.VMEM((length, hidden), BF16), pltpu.VMEM((length, width), F32)]
    sems = [pltpu.SemaphoreType.DMA((2 * steps,)), pltpu.SemaphoreType.DMA((9,))]
    ins = [smem(), vmem(), vmem(), vmem()] + [hbm()] * 4
    work = 4 * length * width * hidden
    moved = 4 * width * hidden + 8 * length * hidden
    own, other = weights
    args = (lengths, residual) + rows + own[4:6] + other[4:6]
    if upstream is None:
        outs = (shaped((length, width), BF16), pack, pack, shaped((length, hidden), BF16), shaped((8, width), F32))
        specs = [vmem(), hbm(), hbm(), vmem(), vmem()]
        return call(functools.partial(ffn_kernel, layer, False), ins, outs, specs, held + sems, work, moved)(*args)
    outs = (shaped((length, width), BF16), pack, pack, pack, pack, shaped((length, width), F32), shaped((8, width), F32))
    specs = [vmem()] + [hbm()] * 4 + [vmem()] * 2
    held += [pltpu.VMEM((length, hidden), BF16), pltpu.VMEM((length, width), BF16), pltpu.VMEM((length, width), F32)]
    held += [pltpu.VMEM((length, width), BF16)]
    kernel = functools.partial(ffn_kernel, layer, True)
    return call(kernel, ins + [hbm()], outs, specs, held + sems, 2 * work, moved)(*args, upstream)


def ffn_backward(layer, lengths, residual, upstream, slope, rows, weights):
    length, width = residual.shape
    hidden = slope.shape[1]
    pack = shaped((length, hidden // 2 + width), BF16)
    steps = hidden // SPAN
    scratch = [pltpu.VMEM((width, hidden), BF16), pltpu.VMEM((hidden, width), BF16)]
    scratch += [pltpu.VMEM((length, hidden), BF16), pltpu.VMEM((length, width), BF16), pltpu.VMEM((length, width), F32)]
    scratch += [pltpu.SemaphoreType.DMA((2 * steps,)), pltpu.SemaphoreType.DMA((4,))]
    own, other = weights
    return call(
        functools.partial(ffn_back_kernel, layer),
        [smem()] + [vmem()] * 5 + [hbm()] * 4,
        (pack, pack, shaped((length, width), F32), shaped((8, width), F32)),
        [hbm(), hbm(), vmem(), vmem()],
        scratch,
        0,
        0,
    )(lengths, residual, upstream, slope, *rows, *own[4:6], *other[4:6])


def attention_backward(layer, heads, x, resid_grad, saved, rows, weights):
    length, width = x.shape[-2:]
    square = length * width
    pack = shaped((length, 2 * width), BF16)
    scratch = [pltpu.VMEM((width, width), BF16)] * 4 + [pltpu.VMEM((length, width), BF16)]
    scratch += [pltpu.VMEM((length, width), BF16)] * 2
    scratch += [pltpu.VMEM((heads * length, length), BF16)]
    scratch += [pltpu.VMEM((heads * length, width), BF16), pltpu.VMEM((GROUP * length, width), BF16)]
    scratch += [pltpu.VMEM((length, width), F32)] * 2
    scratch += [pltpu.VMEM((3, length, width), BF16), pltpu.VMEM((length, width), F32)]
    scratch += [pltpu.SemaphoreType.DMA((5,)), pltpu.SemaphoreType.DMA((8,))]
    own, other = weights
    return call(
        functools.partial(attention_back_kernel, layer, heads),
        [hbm()] + [vmem()] * 7 + [hbm()] * 8,
        (pack, pack, shaped((length, width), BF16), shaped((HEADS_ROWS, width), F32)),
        [hbm(), hbm(), vmem(), vmem()],
        scratch,
        0,
        0,
    )(x, resid_grad, *saved, *rows, *own[:4], *other[:4])


LIGHT = pl.CostEstimate(flops=1, bytes_accessed=1, transcendentals=0)
BLOCKS = 8
HALF_BLOCKS = BLOCKS // 2
FFN_BITS = ((1, 2), (2, 4), (4, 1))
ATTN_BITS = ((4, 4), (1, 1), (2, 2))
ORDER = (
    "P1w K1 D0 Q1w",
    "P1a1 P0w K0 Q0w",
    "T0 Q1a1 P1a2 P0a1",
    "Q1a2 P1a3 Q0a1 P0a2",
    "Q1a3 Q0a2 P0a3 Q0a3",
    "L1ax O0 O1 G0",
    "G1 L0ax g3 g2",
    "g1 uA g1x uB",
    "T1 uC",
)


def hbm():
    return pl.BlockSpec(memory_space=pl.ANY)


def block_shift(bits, core, rank):
    shift = 0
    for pair in bits:
        on = jnp.where(core == 0, (rank & pair[0]) != 0, (rank & pair[1]) != 0)
        shift = shift * 2 + on.astype(jnp.int32)
    return shift


def exchange(array, bits):
    count = lax.axis_size("dp")
    pairs = [(at, at ^ bits[0]) for at in range(count)]
    pairs += [(count + at, count + (at ^ bits[1])) for at in range(count)]
    return lax.ppermute(array, ("section", "dp"), pairs)


def add(left, right):
    return (left.astype(F32) + right.astype(F32)).astype(BF16)


def grad_kernel(locate, meta, first, first2, second, second2, send, keep, lefts, rights, made, in_sems, out_sems):
    length = first.shape[0]
    rows = made.shape[1]
    fetched = []
    for at, (source, target) in enumerate(((first, lefts), (second, rights), (first2, lefts), (second2, rights))):
        window = target.at[pl.ds((at // 2) * length, length)]
        fetched.append(pltpu.make_async_copy(source, window, in_sems.at[at]))
        fetched[-1].start()
    for copy in fetched:
        copy.wait()
    stored = []
    for step in range(BLOCKS):
        block = ((step + HALF_BLOCKS) % BLOCKS) ^ meta[0]
        left, right = locate(block)
        made[step] = dot_tn(lefts[:, left], rights[:, right]).astype(BF16)
        target = send if step < HALF_BLOCKS else keep
        window = target.at[pl.ds((step % HALF_BLOCKS) * rows, rows)]
        stored.append(pltpu.make_async_copy(made.at[step], window, out_sems.at[step]))
        stored[-1].start()
    for copy in stored:
        copy.wait()


def locate_ffn(rows, width, half, block):
    per = width // rows
    place = jnp.maximum(block - HALF_BLOCKS, 0)
    down = block < HALF_BLOCKS
    left = pl.multiple_of(jnp.where(down, block * rows, half + (place % per) * rows), 128)
    right = pl.multiple_of(jnp.where(down, half, (place // per) * width), 128)
    return pl.ds(left, rows), pl.ds(right, width)


def locate_attn(rows, block):
    which = block // 2
    left = pl.multiple_of(jnp.where(which == 3, 2 * rows, 0) + (block % 2) * rows, 128)
    return pl.ds(left, rows), pl.ds(pl.multiple_of(which * rows, 128), rows)


def grad_blocks(locate, shift, factors, rows, width):
    first, first2, second, second2 = factors
    out = shaped((HALF_BLOCKS * rows, width), BF16)
    length = first.shape[0]
    return light_call(
        functools.partial(grad_kernel, locate),
        (out, out),
        [smem()] + [hbm()] * 4,
        [hbm()] * 2,
        scratch=[
            pltpu.VMEM((2 * length, first.shape[1]), BF16),
            pltpu.VMEM((2 * length, second.shape[1]), BF16),
            pltpu.VMEM((BLOCKS, rows, width), BF16),
            pltpu.SemaphoreType.DMA((4,)),
            pltpu.SemaphoreType.DMA((BLOCKS,)),
        ],
    )(shift.reshape(1), *factors)


def light_call(kernel, outs, in_specs, out_specs, grid=(), scratch=(), aliases=None):
    return pl.pallas_call(
        kernel,
        out_shape=outs,
        grid=grid,
        in_specs=in_specs,
        out_specs=out_specs,
        scratch_shapes=list(scratch),
        input_output_aliases=aliases or {},
        compiler_params=pltpu.CompilerParams(vmem_limit_bytes=VMEM),
        cost_estimate=LIGHT,
    )


def put_ride(total, send, rows):
    count = total.shape[0]
    width = total.shape[1]
    high = total.astype(BF16)
    send[rows : rows + count, :width] = high
    send[rows + count :, :width] = (total - high.astype(F32)).astype(BF16)


def take_ride(total, got, rows):
    count, width = total.shape
    return total + got[rows : rows + count, :width].astype(F32) + got[rows + count :, :width].astype(F32)


def add_split_kernel(*refs):
    count = len(refs) // 6
    for at in range(count):
        keep_low, keep_high, got_low, got_high = refs[4 * at : 4 * at + 4]
        send, keep = refs[4 * count + 2 * at : 4 * count + 2 * at + 2]
        keep[...] = add(keep_low[...], got_low[...])
        send[...] = add(keep_high[...], got_high[...])


def add_split(pairs):
    args, in_specs, outs, out_specs = [], [], [], []
    for keep, got in pairs:
        rows, width = keep.shape
        low = pl.BlockSpec((rows // 4, width), lambda at: (at, 0))
        high = pl.BlockSpec((rows // 4, width), lambda at: (at + 2, 0))
        args += [keep, keep, got, got]
        in_specs += [low, high, low, high]
        outs += [shaped((rows // 2, width), BF16)] * 2
        out_specs += [low, low]
    made = light_call(add_split_kernel, outs, in_specs, out_specs, (2,))(*args)
    return list(zip(made[0::2], made[1::2]))


def add_split_ride_kernel(riding, keep_in, got, tail, more, send, keep, tail_out):
    rows = keep.shape[0]
    keep[...] = add(keep_in[:rows, :], got[:rows, :])
    send[:rows, :] = add(keep_in[rows:, :], got[rows : 2 * rows, :])
    total = take_ride(tail[...], got, 2 * rows) if riding else tail[...] + more[...]
    tail_out[...] = total
    put_ride(total, send, rows)


def add_split_ride(keep, got, tail, more=None):
    rows, width = keep.shape
    half = rows // 2
    count = 2 * tail.shape[0]
    outs = (shaped((half + count, width), BF16), shaped((half, width), BF16), shaped(tail.shape, F32))
    kernel = functools.partial(add_split_ride_kernel, more is None)
    return light_call(kernel, outs, [vmem()] * 4, [vmem()] * 3)(keep, got, tail, tail if more is None else more)


def add_ride_kernel(keep, got, tail, out, tail_out):
    rows = keep.shape[0]
    total = take_ride(tail[...], got, rows)
    tail_out[...] = total
    put_ride(total, out, rows)
    out[:rows, :] = add(keep[...], got[:rows, :])


def add_ride(keep, got, tail):
    rows, width = keep.shape
    outs = (shaped((rows + 2 * tail.shape[0], width), BF16), shaped(tail.shape, F32))
    return light_call(add_ride_kernel, outs, [vmem()] * 3, [vmem()] * 2)(keep, got, tail)


def add_pack_kernel(first, first_got, second, second_got, *refs):
    rows, width = second.shape[0], first.shape[1]
    if len(refs) > 1:
        tail, out, tail_out = refs
        tail_out[...] = take_ride(tail[...], first_got, rows)
    else:
        (out,) = refs
    out[:, :width] = add(first[:rows, :], first_got[:rows, :])
    out[:, width:] = add(second[...], second_got[...])


def add_pack(first, second, tail=None):
    rows, width = second[0].shape[0], first[0].shape[1]
    out = shaped((rows, width + second[0].shape[1]), BF16)
    if tail is None:
        return light_call(add_pack_kernel, out, [vmem()] * 4, vmem())(*first, *second)
    outs = (out, shaped(tail.shape, F32))
    return light_call(add_pack_kernel, outs, [vmem()] * 5, [vmem()] * 2)(*first, *second, tail)


def choose_kernel(first, second, first_other, second_other, *outs):
    width = outs[0].shape[1]
    for core, pair in ((0, (first, first_other)), (1, (second, second_other))):
        @pl.when(this_core() == core)
        def _():
            for at, source in enumerate(pair):
                outs[2 * at][...] = source[:, :width]
                outs[2 * at + 1][...] = source[:, width:]


def choose(arrays, width):
    rows, both = arrays[0].shape
    outs = [shaped((rows, width), BF16), shaped((rows, both - width), BF16)] * 2
    return light_call(choose_kernel, outs, [vmem()] * 4, [vmem()] * 4)(*arrays)


def add_kernel(left, right, out):
    out[...] = add(left[...], right[...]) if out.dtype == BF16 else left[...] + right[...]


def light_add(left, right):
    return light_call(add_kernel, shaped(left.shape, left.dtype), [vmem()] * 2, vmem())(left, right)


def join_kernel(count, *refs):
    outs = refs[-count:]
    for at in range(count):
        rows = refs[2 * at].shape[0]
        outs[at][:rows] = refs[2 * at][...]
        outs[at][rows : 2 * rows] = refs[2 * at + 1][...]
    if len(refs) > 3 * count:
        put_ride(refs[2 * count][...], outs[0], 2 * refs[0].shape[0])


def join(pairs, tail=None):
    outs = [shaped((2 * upper.shape[0], upper.shape[1]), upper.dtype) for upper, _ in pairs]
    args = [array for pair in pairs for array in pair]
    if tail is not None:
        args.append(tail)
        outs[0] = shaped((outs[0].shape[0] + 2 * tail.shape[0], outs[0].shape[1]), BF16)
    kernel = functools.partial(join_kernel, len(pairs))
    return light_call(kernel, outs, [vmem()] * len(args), [vmem()] * len(outs))(*args)


def pick_kernel(first, second, out):
    @pl.when(this_core() == 0)
    def _():
        out[...] = second[...]

    @pl.when(this_core() == 1)
    def _():
        out[...] = first[...]


def pick(first, second):
    return light_call(pick_kernel, shaped(first.shape, first.dtype), [vmem()] * 2, vmem())(first, second)


def lay_kernel(first, second, other, out, sems):
    core = this_core()
    theirs = pltpu.make_async_copy(other, out.at[0, 1 - core, 0], sems.at[0])
    theirs.start()
    for at, source in ((0, first), (1, second)):
        @pl.when(core == at)
        def _():
            mine = pltpu.make_async_copy(source, out.at[0, at, 0], sems.at[1])
            mine.start()
            mine.wait()
    theirs.wait()


def lay(first, second, other):
    out = shaped((1, 2, 1) + first.shape, first.dtype)
    scratch = [pltpu.SemaphoreType.DMA((2,))]
    return light_call(lay_kernel, out, [vmem()] * 3, hbm(), scratch=scratch)(first, second, other)


def collect_kernel(heads, lengths, back0, gain0, attn0, ffn0, back1, attn1, ffn1, keep, send):
    width = keep.shape[1]
    at = HEADS_ROWS // 2
    count = jnp.full((1, width), lengths[this_core(), 0], jnp.int32).astype(F32)
    for layer, back, gain, attn, ffn in ((0, back0, gain0[0:1, :], attn0, ffn0), (1, back1, ffn1[2:3, :], attn1, ffn1)):
        rows = jnp.concatenate(
            [
                back[: heads + 1, :], gain, jnp.zeros((at - heads - 2, width), F32), back[at : at + heads, :],
                ffn[0:1, :], attn[0:1, :], ffn[1:2, :], count,
            ],
            axis=0,
        )

        @pl.when(this_core() == layer)
        def _():
            keep[...] = rows

        @pl.when(this_core() != layer)
        def _():
            send[...] = rows


def collect(heads, lengths, *stats):
    out = jax.ShapeDtypeStruct((HEADS_ROWS, stats[0].shape[1]), F32)
    return pl.pallas_call(
        functools.partial(collect_kernel, heads),
        out_shape=(out, out),
        in_specs=[smem()] + [vmem()] * len(stats),
        out_specs=[vmem()] * 2,
        cost_estimate=LIGHT,
    )(lengths, *stats)


def small_kernel(heads, tail, got, attn_out, ffn_out, pre_out, post_out, rms_out):
    width = tail.shape[1]
    total = take_ride(tail[...], got, 0)
    at = HEADS_ROWS // 2
    attn_out[...] = total[heads : heads + 1, :]
    ffn_out[...] = total[heads + 1 : heads + 2, :]
    lane = lax.broadcasted_iota(jnp.int32, (width, heads), 0) // (width // heads)
    ones = (lane == lax.broadcasted_iota(jnp.int32, (width, heads), 1)).astype(F32)
    high = lax.Precision.HIGHEST
    pre_out[0] = lax.dot_general(
        total[:heads, :], ones, (((1,), (0,)), ((), ())), precision=high, preferred_element_type=F32
    )
    post_out[0] = lax.dot_general(
        ones, total[at : at + heads, :], (((0,), (1,)), ((), ())), precision=high, preferred_element_type=F32
    )
    tokens = total[HEADS_ROWS - 1 : HEADS_ROWS, 0:1]
    for which in range(3):
        row = total[at + heads + which : at + heads + which + 1, :]
        rms_out[:, which : which + 1] = jnp.sqrt(jnp.sum(row, axis=1, keepdims=True) / width / tokens)


def small_outputs(heads, tail, got):
    width = tail.shape[1]
    shapes = ((1, width), (1, width), (1, heads, heads), (1, heads, heads), (1, 3))
    return pl.pallas_call(
        functools.partial(small_kernel, heads),
        out_shape=tuple(jax.ShapeDtypeStruct(shape, F32) for shape in shapes),
        cost_estimate=LIGHT,
    )(tail, got)


def unpack_kernel(part, owns, meta, *refs):
    count = 2 * len(owns)
    sources, outs, scratch = refs[:count], refs[count + 6 : count + 12], refs[count + 12 :]
    taken_ffn, given_ffn, taken_attn, given_attn, taken_sem, given_sem = scratch
    core = this_core()
    moves = []
    for which, own in enumerate(owns):
        half = core if own else 1 - core
        for group, (taken, given, place, grads) in enumerate((
            (taken_ffn, given_ffn, place_ffn, outs[:2]), (taken_attn, given_attn, place_attn, outs[2:]),
        )):
            rows = taken.shape[1]
            shift = jnp.where(half == 0, meta[1 + 2 * group], meta[2 + 2 * group])
            for step in range(HALF_BLOCKS):
                slot = HALF_BLOCKS * which + step
                at = BLOCKS * group + slot
                block = (HALF_BLOCKS * part + step) ^ shift
                window = sources[2 * which + group].at[pl.ds(step * rows, rows)]
                fetch = pltpu.make_async_copy(window, taken.at[slot], taken_sem.at[at])
                stores = [
                    (chosen, pltpu.make_async_copy(given.at[slot], target, given_sem.at[at]))
                    for chosen, target in place(half, block, grads)
                ]
                moves.append((fetch, stores, taken, given, slot))
    for fetch, *_ in moves:
        fetch.start()
    for fetch, stores, taken, given, slot in moves:
        fetch.wait()
        given[slot] = taken[slot].astype(F32)
        for chosen, copy in stores:
            pl.when(chosen)(copy.start)
    for _, stores, *_ in moves:
        for chosen, copy in stores:
            pl.when(chosen)(copy.wait)


def unpack(part, owns, meta, sources, outs):
    scratch = []
    for source, rows in zip(sources, (outs[0].shape[2] // BLOCKS, outs[2].shape[1] // 2)):
        width = source.shape[1]
        scratch += [pltpu.VMEM((BLOCKS, rows, width), BF16), pltpu.VMEM((BLOCKS, rows, width), F32)]
    scratch += [pltpu.SemaphoreType.DMA((2 * BLOCKS,))] * 2
    return light_call(
        functools.partial(unpack_kernel, part, owns),
        [shaped(out.shape, F32) for out in outs],
        [smem()] + [hbm()] * (len(sources) + len(outs)),
        [hbm()] * len(outs),
        scratch=scratch,
        aliases={1 + len(sources) + at: at for at in range(len(outs))},
    )(meta, *sources, *outs)


def blank_kernel(*refs):
    pass


def blank(shapes):
    return pl.pallas_call(
        blank_kernel,
        out_shape=tuple(jax.ShapeDtypeStruct(shape, F32) for shape in shapes),
        out_specs=[hbm()] * len(shapes),
        cost_estimate=LIGHT,
    )()


def place_ffn(half, block, outs):
    grad_in, grad_out = outs
    width, hidden = grad_in.shape[1:]
    rows = hidden // BLOCKS
    per = width // rows
    inner = jnp.maximum(block - HALF_BLOCKS, 0)
    at_out = pl.multiple_of(half * (hidden // 2) + jnp.minimum(block, HALF_BLOCKS - 1) * rows, rows)
    at_row = pl.multiple_of((inner % per) * rows, rows)
    at_column = pl.multiple_of(half * (hidden // 2) + (inner // per) * width, 128)
    return [
        (block < HALF_BLOCKS, grad_out.at[0, pl.ds(at_out, rows), :]),
        (block >= HALF_BLOCKS, grad_in.at[0, pl.ds(at_row, rows), pl.ds(at_column, width)]),
    ]


def place_attn(half, block, outs):
    width = outs[0].shape[1]
    rows = width // 2
    at_row = pl.multiple_of((block % 2) * rows, rows)
    return [
        (block // 2 == which, outs[which].at[0, pl.ds(at_row, rows), pl.ds(half * rows, rows)]) for which in range(4)
    ]


def after(values, done):
    return lax.optimization_barrier(tuple(values) + tuple(done))[: len(values)]


def param_rows(gain_attn, gain_ffn, mix_pre, mix_post):
    heads = mix_pre.shape[1]
    width = gain_attn.shape[1]
    spread = lambda mix: jnp.repeat(mix, width // heads, axis=1)
    rows = jnp.concatenate([gain_attn, gain_ffn, spread(mix_pre[0]), spread(mix_post[0].T)], axis=0)
    return jnp.pad(rows, ((0, HEADS_ROWS - rows.shape[0]), (0, 0)))


def local(
    inputs, cotangent, lengths, w_query, w_key, w_value, w_output, w_in, w_out, gain_attn, gain_ffn, mix_pre, mix_post,
):
    core = lax.axis_index("section")
    rank = lax.axis_index("dp")
    is_first = core == 0
    swap = lambda shard: lax.ppermute(shard, "section", [(0, 1), (1, 0)])
    length, width = inputs.shape[2:]
    hidden = w_in.shape[2]
    heads = mix_pre.shape[1]

    own_rows = param_rows(gain_attn, gain_ffn, mix_pre, mix_post)
    own = after((w_query, w_key, w_value, w_output), (own_rows,)) + (w_in, w_out)
    other_rows = swap(own_rows)
    other = tuple(swap(weight) for weight in own[:4])
    other += tuple(swap(weight) for weight in after(own[4:], other + (other_rows,)))
    rows = (own_rows, other_rows)
    weights = (own, other)
    ffn_shift = block_shift(FFN_BITS, core, rank)
    attn_shift = block_shift(ATTN_BITS, core, rank)

    steps = {}
    state = {"last": ()}

    def tie(value):
        return after((value,), state["last"])[0] if state["last"] else value

    def chain(layer, make_ffn, make_attn):
        bits = (FFN_BITS, ATTN_BITS)
        keep, got = [None, None], [None, None]
        riding = layer == 0

        def made(group, make):
            def run():
                send, keep[group] = make()
                got[group] = exchange(send, bits[group][0])
                return keep[group]
            return run

        def split(at, groups):
            def run():
                keep[groups[0]] = tie(keep[groups[0]])
                if riding and groups == (0,):
                    send, kept, made_all["tail"] = add_split_ride(
                        keep[0], got[0], made_all["tail"], made_all["more"] if at == 1 else None
                    )
                    parts = [(send, kept)]
                else:
                    parts = add_split([(keep[group], got[group]) for group in groups])
                for group, (send, kept) in zip(groups, parts):
                    keep[group] = kept
                    got[group] = exchange(send, bits[group][at])
                return keep[groups[0]]
            return run

        def third(group):
            def run():
                keep[group] = tie(keep[group])
                if riding and group == 0:
                    keep[0], made_all["tail"] = add_ride(keep[0], got[0], made_all["tail"])
                else:
                    keep[group] = light_add(keep[group], got[group])
                got[group] = exchange(keep[group], (8, 8))
                return keep[group]
            return run

        def summed():
            keep[0] = tie(keep[0])
            rows, bit = keep[1].shape[0], 16
            while bit < lax.axis_size("dp"):
                more = got[0]
                keep[0], keep[1] = add(keep[0], more), add(keep[1], got[1])
                if riding:
                    tail = made_all["tail"] + more[rows : rows + HEADS_ROWS].astype(F32)
                    tail = tail + more[rows + HEADS_ROWS :].astype(F32)
                    high = tail.astype(BF16)
                    terms = [keep[0][:rows], high, (tail - high.astype(F32)).astype(BF16)]
                    made_all["tail"], keep[0] = tail, jnp.concatenate(terms, axis=0)
                got[:] = [exchange(array, (bit, bit)) for array in keep]
                bit *= 2
            pairs = ((keep[0], got[0]), (keep[1], got[1]))
            if riding:
                made_all[layer], made_all["tail"] = add_pack(*pairs, made_all["tail"])
            else:
                made_all[layer] = add_pack(*pairs)
            made_all["hand", layer] = lax.ppermute(made_all[layer], "section", [(1 - layer, layer)])
            return made_all[layer]

        name = str(layer)
        steps.update({
            "P" + name + "w": made(0, make_ffn), "Q" + name + "w": made(1, make_attn),
            "P" + name + "a1": split(1, (0,)), "Q" + name + "a1": split(1, (1,)), "L" + name + "a1": split(1, (0, 1)),
            "P" + name + "a2": split(2, (0,)), "Q" + name + "a2": split(2, (1,)), "L" + name + "a2": split(2, (0, 1)),
            "P" + name + "a3": third(0), "Q" + name + "a3": third(1), "L" + name + "ax": summed,
        })

    def gather():
        bits = [FFN_BITS, ATTN_BITS] + [[pair[::-1] for pair in group] for group in (FFN_BITS, ATTN_BITS)]
        held, got = [None] * 4, [None] * 4

        def send(at, parts=range(4)):
            for part in parts:
                got[part] = exchange(held[part], bits[part][at])
            return held[0]

        def start():
            arrays = (tie(made_all[0]), made_all[1], made_all["hand", 0], made_all["hand", 1])
            held[:] = choose(arrays, width)
            return send(2)

        def joined(at):
            def run():
                pairs = [(tie(held[0]), got[0])] + list(zip(held[1:], got[1:]))
                held[:] = join(pairs, made_all["tail"] if at == 0 else None)
                return send(at, range(4) if at else range(2))
            return run

        def others():
            *held[2:], got[0], got[1] = after(held[2:] + got[:2], state["last"])
            return send(0, (2, 3))

        def first():
            made_all["grads"] = unpack(0, (True, False), place_meta, (tie(held[0]), *held[1:]), made_all["grads"])
            return made_all["grads"][0]

        def second(own):
            def run():
                pair = got[:2] if own else got[2:]
                made_all["grads"] = unpack(1, (own,), place_meta, (tie(pair[0]), pair[1]), made_all["grads"])
                return made_all["grads"][0]
            return run

        def small_end():
            rows = HALF_BLOCKS * (hidden // BLOCKS)
            made["small"] = small_outputs(heads, tie(made_all["tail"]), got[0][rows:])
            return made["small"][0]

        steps.update({
            "g3": start, "g2": joined(1), "g1": joined(0), "uA": first, "g1x": others, "uB": second(True), "uC": second(False), "T1": small_end,
        })

    def ffn_blocks(first, second):
        factors = (tie(first[0]), first[1], second[0], swap(second[1]))
        locate = functools.partial(locate_ffn, hidden // BLOCKS, width, hidden // 2)
        return grad_blocks(locate, ffn_shift, factors, hidden // BLOCKS, width)

    def attn_blocks(both, pack):
        factors = (tie(both[0]), both[1], pack[0], swap(pack[1]))
        locate = functools.partial(locate_attn, width // 2)
        return grad_blocks(locate, attn_shift, factors, width // 2, width // 2)

    both0, *qkvp0, residual0, stats_a0 = attention_forward(0, heads, lengths, inputs, rows, weights)
    mid, own0, send0, slope0, stats_f0 = ffn_forward(0, lengths, residual0, rows, weights)
    both0_other, send0_other = swap(both0), swap(send0)
    both1, *qkvp1, residual1, stats_a1 = attention_forward(1, heads, lengths, mid, rows, weights)
    (residual1,) = after((residual1,), (both0_other, send0_other))
    both1_other = swap(both1)
    last, own1, send1, own1b, send1b, resid1, stats_f1 = ffn_forward(
        1, lengths, residual1, rows, weights, cotangent
    )
    own1, send1_other = after((own1, swap(send1)), (both1_other,))
    made = {}

    def attention1():
        made["pack1"], made["send_pack1"], made["grad1"], made["stats_b1"] = attention_backward(
            1, heads, mid, tie(resid1), qkvp1, rows, weights
        )
        return made["grad1"]

    def ffn0():
        made["own0b"], made["send0b"], made["resid0"], made["stats_g0"] = ffn_backward(
            0, lengths, residual0, tie(made["grad1"]), slope0, rows, weights
        )
        return made["resid0"]

    def attention0():
        made["pack0"], made["send_pack0"], made["grad0"], made["stats_b0"] = attention_backward(
            0, heads, inputs, tie(made["resid0"]), qkvp0, rows, weights
        )
        return made["grad0"]

    steps.update({"K1": attention1, "D0": ffn0, "K0": attention0})
    place_meta = jnp.stack(
        [core] + [block_shift(bits, which, rank) for bits in (FFN_BITS, ATTN_BITS) for which in range(2)]
    ).astype(jnp.int32)
    made_all = {"grads": blank((w_in.shape, w_out.shape) + (w_query.shape,) * 4)}
    chain(
        1,
        lambda: ffn_blocks((own1, send1_other), (own1b, send1b)),
        lambda: attn_blocks((both1, both1_other), (made["pack1"], made["send_pack1"])),
    )
    chain(
        0,
        lambda: ffn_blocks((own0, send0_other), (made["own0b"], made["send0b"])),
        lambda: attn_blocks((both0, both0_other), (made["pack0"], made["send_pack0"])),
    )

    def small_start():
        made_all["tail"], send = collect(
            heads, lengths, tie(made["stats_b0"]), made["stats_g0"], stats_a0, stats_f0, made["stats_b1"], stats_a1, stats_f1
        )
        made_all["more"] = swap(send)
        return made_all["tail"]

    def send_rows(name, first, second):
        def run():
            made[name] = swap(pick(tie(first()), second()))
            return first()
        return run

    def lay_rows(name, first, second):
        def run():
            made[name] = lay(tie(first()), second(), made[name])
            return made[name]
        return run

    mids = ("outputs", lambda: mid, lambda: last)
    grads = ("grads", lambda: made["grad0"], lambda: made["grad1"])
    steps.update({"O0": send_rows(*mids), "O1": lay_rows(*mids), "G0": send_rows(*grads), "G1": lay_rows(*grads)})
    steps["T0"] = small_start
    gather()
    for name in [name for line in ORDER for name in line.split()]:
        with jax.named_scope(name):
            state["last"] = (steps[name](),)

    w_in_grad, w_out_grad, *rest = made_all["grads"]
    return (made["outputs"], made["grads"], *rest, w_in_grad, w_out_grad, *made["small"])


def solution(mesh):
    in_specs = (
        P(None, "dp", None, None),
        P(None, "dp", None, None),
        P(None, "dp"),
        P("section", None, None),
        P("section", None, None),
        P("section", None, None),
        P("section", None, None),
        P("section", None, None),
        P("section", None, None),
        P("section", None),
        P("section", None),
        P("section", None, None),
        P("section", None, None),
    )
    out_specs = (
        P("section", None, "dp", None, None),
        P("section", None, "dp", None, None),
        P("section", None, None),
        P("section", None, None),
        P("section", None, None),
        P("section", None, None),
        P("section", None, None),
        P("section", None, None),
        P("section", None),
        P("section", None),
        P("section", None, None),
        P("section", None, None),
        P("section", None),
    )
    return jax.shard_map(local, mesh=mesh, in_specs=in_specs, out_specs=out_specs, check_vma=False)
```

```python
import functools

import jax
import jax.numpy as jnp
from jax import lax
from jax.experimental import pallas as pl
from jax.experimental.pallas import tpu as pltpu
from jax.sharding import PartitionSpec as P

EPSILON = 1e-06
MASKED = -1e30
F32 = jnp.float32
BF16 = jnp.bfloat16


HEADS_ROWS = 32
GROUP = 2
VMEM = 60 << 20
SPAN = 1536


def row_scale(values):
    return lax.rsqrt(jnp.mean(values * values, axis=-1, keepdims=True) + EPSILON)


def norm_back(values, gain, grad):
    scale = row_scale(values)
    weighted = grad * gain
    inner = jnp.mean(values * weighted, axis=-1, keepdims=True)
    grad_values = scale * weighted - values * (scale * scale * scale) * inner
    return grad_values, jnp.sum(grad * values * scale, axis=0, keepdims=True)


def gelu_pair(values):
    square = values * values
    tanh = jnp.tanh(values * (0.7978845608028654 + 0.7978845608028654 * 0.044715 * square))
    half = 0.5 * (1.0 + tanh)
    slope = half + 0.5 * values * (1.0 - tanh * tanh) * (
        0.7978845608028654 + 3.0 * 0.7978845608028654 * 0.044715 * square
    )
    return values * half, slope


def dot_nn(left, right):
    return lax.dot_general(left, right, (((1,), (0,)), ((), ())), preferred_element_type=F32)


def dot_nt(left, right):
    return lax.dot_general(left, right, (((1,), (1,)), ((), ())), preferred_element_type=F32)


def dot_tn(left, right):
    return lax.dot_general(left, right, (((0,), (0,)), ((), ())), preferred_element_type=F32)


def this_core():
    return lax.axis_index("section")


def sequence_rows(array):
    return array.at[this_core(), 0] if len(array.shape) == 4 else array


class Weight:
    def __init__(self, mine, own, other, held, sem):
        self.mine, self.own, self.other, self.held, self.sem = mine, own, other, held, sem

    def copy(self, source, cut):
        return pltpu.make_async_copy(source.at[(0,) + cut], self.held.at[cut], self.sem)

    def start(self, cut=(slice(None), slice(None))):
        @pl.when(self.mine)
        def _():
            self.copy(self.own, cut).start()

        @pl.when(jnp.logical_not(self.mine))
        def _():
            self.copy(self.other, cut).start()

    def wait(self, cut=(slice(None), slice(None))):
        self.copy(self.own, cut).wait()


def param_row(mine, own, other, at, count=1):
    rows = pl.ds(at, count)
    return jnp.where(mine, own[rows, :], other[rows, :])


def attention_kernel(
    layer, heads, lengths, x_in, own_rows, other_rows, wq, wk, wv, wo, wq2, wk2, wv2, wo2,
    both_out, query_out, key_out, value_out, probs_out, residual_out, stats_out,
    held_q, held_k, held_v, held_o, x, keys_upper, keys_lower, values_mixed, sems,
):
    mine = this_core() == layer
    brought = pltpu.make_async_copy(sequence_rows(x_in), x, sems.at[4])
    brought.start()
    weights = [
        Weight(mine, own, other, held, sems.at[at])
        for at, (own, other, held) in enumerate(
            ((wq, wq2, held_q), (wk, wk2, held_k), (wv, wv2, held_v), (wo, wo2, held_o))
        )
    ]
    for weight in weights:
        weight.start()
    length, width = x.shape
    half = length // 2
    brought.wait()
    values = x[...].astype(F32)
    gain = param_row(mine, own_rows, other_rows, 0)
    both_out[:, :width] = (values * row_scale(values) * gain).astype(BF16)
    for weight, held, out, factor in (
        (weights[0], held_q, query_out, (width // heads) ** -0.5),
        (weights[1], held_k, key_out, 1.0),
        (weights[2], held_v, value_out, 1.0),
    ):
        weight.wait()
        made = dot_nn(both_out[:, :width], held[...]).astype(BF16)
        out[...] = (made.astype(F32) * factor).astype(BF16) if factor != 1.0 else made

    def softmax(logits, first):
        rows = lax.broadcasted_iota(jnp.int32, logits.shape, 0)
        columns = lax.broadcasted_iota(jnp.int32, logits.shape, 1) + first
        logits = jnp.where(rows <= columns, logits, MASKED)
        exponent = jnp.exp(logits - jnp.max(logits, axis=0, keepdims=True))
        return (exponent * (1.0 / jnp.sum(exponent, axis=0, keepdims=True))).astype(BF16)

    for first in range(0, heads, GROUP):
        for at in range(first, first + GROUP):
            mixed = key_out[...].astype(F32) * param_row(mine, own_rows, other_rows, 2 + at)
            high = mixed.astype(BF16)
            low = (mixed - high.astype(F32)).astype(BF16)
            place = (at - first) * half
            for which, part in enumerate((high, low)):
                keys_upper[which, place : place + half, :] = part[:half]
                keys_lower[which, place : place + half, :] = part[half:]
        upper = dot_nt(keys_upper[0], query_out[...]) + dot_nt(keys_upper[1], query_out[...])
        lower = dot_nt(keys_lower[0], query_out[half:, :]) + dot_nt(keys_lower[1], query_out[half:, :])
        for at in range(first, first + GROUP):
            row = at * length
            part = slice((at - first) * half, (at - first + 1) * half)
            probs_out[row : row + half, :half] = softmax(upper[part, :half], 0)
            probs_out[row + half : row + length, :half] = jnp.zeros((length - half, half), BF16)
            late = jnp.concatenate([upper[part, half:], lower[part]], axis=0)
            probs_out[row : row + length, half:] = softmax(late, half)
            scale = param_row(mine, own_rows, other_rows, 2 + heads + at)
            values_mixed[row : row + length, :] = value_out[...] * scale.astype(BF16)
    both_out[:, width:] = dot_tn(probs_out[...], values_mixed[...]).astype(BF16)
    weights[3].wait()
    branch = dot_nn(both_out[:, width:], held_o[...])
    residual_out[...] = values + branch
    valid = lax.broadcasted_iota(jnp.int32, (length, 1), 0) < lengths[this_core(), 0]
    stats_out[...] = jnp.broadcast_to(
        jnp.sum(jnp.where(valid, branch * branch, 0.0), axis=0, keepdims=True), stats_out.shape
    )


def ffn_kernel(
    layer, backward, lengths, residual, own_rows, other_rows, w_in, w_out, w_in2, w_out2, *refs
):
    if backward:
        upstream_in, refs = refs[0], refs[1:]
        out, own_first, send_first, own_second, send_second, resid_out, stats_out = refs[:7]
        held_in, held_out, normed, act, total, pre_grad, branch_grad, back_total, upstream, sems, out_sems = refs[7:]
        brought = pltpu.make_async_copy(sequence_rows(upstream_in), upstream, out_sems.at[8])
        brought.start()
    else:
        out, own_first, send_first, slope_out, stats_out = refs[:5]
        held_in, held_out, normed, act, total, sems, out_sems = refs[5:]
    core = this_core()
    mine = core == layer
    length, width = residual.shape
    hidden = held_in.shape[1]
    steps = hidden // SPAN
    half = hidden // 2
    cuts_in = [(slice(None), pl.ds(step * SPAN, SPAN)) for step in range(steps)]
    cuts_out = [(pl.ds(step * SPAN, SPAN), slice(None)) for step in range(steps)]
    ins = [Weight(mine, w_in, w_in2, held_in, sems.at[step]) for step in range(steps)]
    outs = [Weight(mine, w_out, w_out2, held_out, sems.at[steps + step]) for step in range(steps)]
    for step in range(steps):
        ins[step].start(cuts_in[step])
        outs[step].start(cuts_out[step])
    values = residual[...]
    normed[...] = (values * row_scale(values) * param_row(mine, own_rows, other_rows, 1)).astype(BF16)
    valid = lax.broadcasted_iota(jnp.int32, (length, 1), 0) < lengths[core, 0]
    copies = []

    def send(source, target, at):
        copy = pltpu.make_async_copy(source, target, out_sems.at[at])
        copy.start()
        copies.append(copy)

    send(normed, own_first.at[:, pl.ds(half, width)], 0)
    send(normed, send_first.at[:, pl.ds(half, width)], 1)
    if backward:
        brought.wait()
        branch_grad[...] = jnp.where(valid, upstream[...], jnp.zeros_like(upstream))
        send(branch_grad, own_second.at[:, pl.ds(half, width)], 2)
        send(branch_grad, send_second.at[:, pl.ds(half, width)], 3)
    for step in range(steps):
        span = pl.ds(step * SPAN, SPAN)
        ins[step].wait(cuts_in[step])
        made, slope = gelu_pair(dot_nn(normed[...], held_in[:, span]))
        act[:, span] = made.astype(BF16)
        outs[step].wait(cuts_out[step])
        part = dot_nn(act[:, span], held_out[span, :])
        total[...] = part if step == 0 else total[...] + part
        if backward:
            grad = (dot_nt(branch_grad[...], held_out[span, :]) * slope).astype(BF16)
            pre_grad[:, span] = grad
            part = dot_nt(pre_grad[:, span], held_in[:, span])
            back_total[...] = part if step == 0 else back_total[...] + part
        else:
            slope_out[:, span] = slope.astype(BF16)
    mine_at = pl.ds(pl.multiple_of(core * half, 128), half)
    other_at = pl.ds(pl.multiple_of((1 - core) * half, 128), half)
    send(act.at[:, mine_at], own_first.at[:, pl.ds(0, half)], 4)
    send(act.at[:, other_at], send_first.at[:, pl.ds(0, half)], 5)
    if backward:
        send(pre_grad.at[:, mine_at], own_second.at[:, pl.ds(0, half)], 6)
        send(pre_grad.at[:, other_at], send_second.at[:, pl.ds(0, half)], 7)
    branch = total[...]
    made = jnp.where(valid, residual[...] + branch, 0.0)
    out[...] = made.astype(BF16)
    stats_out[0:1, :] = jnp.sum(made * made, axis=0, keepdims=True)
    stats_out[1:2, :] = jnp.sum(jnp.where(valid, branch * branch, 0.0), axis=0, keepdims=True)
    if backward:
        back, gain_grad = norm_back(
            residual[...], param_row(mine, own_rows, other_rows, 1), back_total[...]
        )
        resid_out[...] = branch_grad[...].astype(F32) + back
        stats_out[2:3, :] = gain_grad
    for copy in copies:
        copy.wait()


def ffn_back_kernel(
    layer, lengths, residual, upstream, slope, own_rows, other_rows, w_in, w_out, w_in2, w_out2,
    own_second, send_second, resid_out, stats_out,
    held_in, held_out, pre_grad, branch_grad, back_total, sems, out_sems,
):
    core = this_core()
    mine = core == layer
    length, width = residual.shape
    hidden = held_in.shape[1]
    steps = hidden // SPAN
    half = hidden // 2
    cuts_in = [(slice(None), pl.ds(step * SPAN, SPAN)) for step in range(steps)]
    cuts_out = [(pl.ds(step * SPAN, SPAN), slice(None)) for step in range(steps)]
    ins = [Weight(mine, w_in, w_in2, held_in, sems.at[step]) for step in range(steps)]
    outs = [Weight(mine, w_out, w_out2, held_out, sems.at[steps + step]) for step in range(steps)]
    for step in range(steps):
        outs[step].start(cuts_out[step])
        ins[step].start(cuts_in[step])
    valid = lax.broadcasted_iota(jnp.int32, (length, 1), 0) < lengths[core, 0]
    branch_grad[...] = jnp.where(valid, upstream[...], jnp.zeros_like(upstream))
    copies = []

    def send(source, target, at):
        copy = pltpu.make_async_copy(source, target, out_sems.at[at])
        copy.start()
        copies.append(copy)

    send(branch_grad, own_second.at[:, pl.ds(half, width)], 0)
    send(branch_grad, send_second.at[:, pl.ds(half, width)], 1)
    for step in range(steps):
        span = pl.ds(step * SPAN, SPAN)
        outs[step].wait(cuts_out[step])
        grad = dot_nt(branch_grad[...], held_out[span, :]) * slope[:, span].astype(F32)
        pre_grad[:, span] = grad.astype(BF16)
        ins[step].wait(cuts_in[step])
        part = dot_nt(pre_grad[:, span], held_in[:, span])
        back_total[...] = part if step == 0 else back_total[...] + part
    send(pre_grad.at[:, pl.ds(pl.multiple_of(core * half, 128), half)], own_second.at[:, pl.ds(0, half)], 2)
    send(pre_grad.at[:, pl.ds(pl.multiple_of((1 - core) * half, 128), half)], send_second.at[:, pl.ds(0, half)], 3)
    back, gain_grad = norm_back(residual[...], param_row(mine, own_rows, other_rows, 1), back_total[...])
    resid_out[...] = branch_grad[...].astype(F32) + back
    stats_out[0:1, :] = gain_grad
    for copy in copies:
        copy.wait()


def attention_back_kernel(
    layer, heads, x_in, resid_grad, query, key, value, probs, own_rows, other_rows,
    wq, wk, wv, wo, wq2, wk2, wv2, wo2,
    own_pack, send_pack, grad_out, stats_out,
    held_q, held_k, held_v, held_o, x, attn_grad, head_grad, logit_grad, key_scaled, value_scaled,
    key_grad, value_grad, piece, total, sems, out_sems,
):
    core = this_core()
    brought = pltpu.make_async_copy(sequence_rows(x_in), x, sems.at[4])
    brought.start()
    mine = core == layer
    weights = [
        Weight(mine, own, other, held, sems.at[at])
        for at, (own, other, held) in enumerate(
            ((wo, wo2, held_o), (wq, wq2, held_q), (wk, wk2, held_k), (wv, wv2, held_v))
        )
    ]
    for weight in weights:
        weight.start()
    length, width = x.shape
    half = width // 2
    copies = []

    def send(source, at, sem):
        for target, which in ((own_pack, core), (send_pack, 1 - core)):
            copy = pltpu.make_async_copy(
                source.at[:, pl.ds(pl.multiple_of(which * half, 128), half)],
                target.at[:, pl.ds(at * half, half)],
                out_sems.at[sem + (0 if target is own_pack else 1)],
            )
            copy.start()
            copies.append(copy)

    attn_grad[...] = resid_grad[...].astype(BF16)
    send(attn_grad, 3, 0)
    weights[0].wait()
    head_grad[...] = dot_nt(attn_grad[...], held_o[...]).astype(BF16)

    for first in range(0, heads, GROUP):
        span = slice(first * length, (first + GROUP) * length)
        pres, posts = [], []
        for at in range(first, first + GROUP):
            pres.append(param_row(mine, own_rows, other_rows, 2 + at))
            posts.append(param_row(mine, own_rows, other_rows, 2 + heads + at))
            rows = slice(at * length, (at + 1) * length)
            key_scaled[rows, :] = key[...] * pres[-1].astype(BF16)
            place = (at - first) * length
            value_scaled[place : place + length, :] = value[...] * posts[-1].astype(BF16)
        grad_probs = dot_nt(value_scaled[...], head_grad[...])
        routed = dot_nn(probs[span, :], head_grad[...])
        for at in range(first, first + GROUP):
            part = slice((at - first) * length, (at - first + 1) * length)
            prob = probs[at * length : (at + 1) * length, :].astype(F32)
            inner = jnp.sum(prob * grad_probs[part], axis=0, keepdims=True)
            logit_grad[at * length : (at + 1) * length, :] = (prob * (grad_probs[part] - inner)).astype(BF16)
            stats_out[HEADS_ROWS // 2 + at : HEADS_ROWS // 2 + at + 1, :] = jnp.sum(
                routed[part] * value[...].astype(F32), axis=0, keepdims=True
            )
            more = routed[part] * posts[at - first]
            value_grad[...] = more if at == 0 else value_grad[...] + more
        routed = dot_nn(logit_grad[span, :], query[...])
        for at in range(first, first + GROUP):
            part = slice((at - first) * length, (at - first + 1) * length)
            stats_out[at : at + 1, :] = jnp.sum(routed[part] * key[...].astype(F32), axis=0, keepdims=True)
            more = routed[part] * pres[at - first]
            key_grad[...] = more if at == 0 else key_grad[...] + more
    piece[2] = value_grad[...].astype(BF16)
    send(piece.at[2], 2, 6)
    piece[1] = key_grad[...].astype(BF16)
    send(piece.at[1], 1, 4)
    weights[3].wait()
    total[...] = dot_nt(piece[2], held_v[...])
    weights[2].wait()
    total[...] += dot_nt(piece[1], held_k[...])
    factor = (width // heads) ** -0.5
    piece[0] = (dot_tn(logit_grad[...], key_scaled[...]) * factor).astype(BF16)
    send(piece.at[0], 0, 2)
    weights[1].wait()
    brought.wait()
    back, gain_grad = norm_back(
        x[...].astype(F32),
        param_row(mine, own_rows, other_rows, 0),
        total[...] + dot_nt(piece[0], held_q[...]),
    )
    grad_out[...] = (resid_grad[...] + back).astype(BF16)
    stats_out[heads : heads + 1, :] = gain_grad
    for copy in copies:
        copy.wait()


def vmem():
    return pl.BlockSpec(memory_space=pltpu.VMEM)


def smem():
    return pl.BlockSpec(memory_space=pltpu.SMEM)


def shaped(shape, kind):
    return jax.ShapeDtypeStruct(shape, kind)


def call(kernel, in_specs, outs, out_specs, scratch, flops, bytes_accessed):
    return pl.pallas_call(
        kernel,
        out_shape=outs,
        in_specs=in_specs,
        out_specs=out_specs,
        scratch_shapes=scratch,
        compiler_params=pltpu.CompilerParams(vmem_limit_bytes=VMEM),
        cost_estimate=pl.CostEstimate(flops=flops, bytes_accessed=bytes_accessed, transcendentals=0) if flops else LIGHT,
    )


def attention_forward(layer, heads, lengths, x, rows, weights):
    length, width = x.shape[-2:]
    square = length * width
    outs = (
        shaped((length, 2 * width), BF16),
        shaped((length, width), BF16),
        shaped((length, width), BF16),
        shaped((length, width), BF16),
        shaped((heads * length, length), BF16),
        shaped((length, width), F32),
        shaped((8, width), F32),
    )
    scratch = [pltpu.VMEM((width, width), BF16)] * 4 + [pltpu.VMEM((length, width), BF16)]
    scratch += [pltpu.VMEM((2, GROUP * length // 2, width), BF16)] * 2
    scratch += [pltpu.VMEM((heads * length, width), BF16), pltpu.SemaphoreType.DMA((5,))]
    kernel = functools.partial(attention_kernel, layer, heads)
    run = call(
        kernel, [smem(), hbm(), vmem(), vmem()] + [hbm()] * 8, outs, [vmem()] * 7, scratch,
        8 * square * width + 6 * heads * length * square, 8 * width * width + 20 * square,
    )
    own, other = weights
    return run(lengths, x, *rows, *own[:4], *other[:4])


def ffn_forward(layer, lengths, residual, rows, weights, upstream=None):
    length, width = residual.shape
    hidden = weights[0][4].shape[2]
    half = hidden // 2
    pack = shaped((length, half + width), BF16)
    steps = hidden // SPAN
    held = [pltpu.VMEM((width, hidden), BF16), pltpu.VMEM((hidden, width), BF16)]
    held += [pltpu.VMEM((length, width), BF16), pltpu.VMEM((length, hidden), BF16), pltpu.VMEM((length, width), F32)]
    sems = [pltpu.SemaphoreType.DMA((2 * steps,)), pltpu.SemaphoreType.DMA((9,))]
    ins = [smem(), vmem(), vmem(), vmem()] + [hbm()] * 4
    work = 4 * length * width * hidden
    moved = 4 * width * hidden + 8 * length * hidden
    own, other = weights
    args = (lengths, residual) + rows + own[4:6] + other[4:6]
    if upstream is None:
        outs = (shaped((length, width), BF16), pack, pack, shaped((length, hidden), BF16), shaped((8, width), F32))
        specs = [vmem(), hbm(), hbm(), vmem(), vmem()]
        return call(functools.partial(ffn_kernel, layer, False), ins, outs, specs, held + sems, work, moved)(*args)
    outs = (shaped((length, width), BF16), pack, pack, pack, pack, shaped((length, width), F32), shaped((8, width), F32))
    specs = [vmem()] + [hbm()] * 4 + [vmem()] * 2
    held += [pltpu.VMEM((length, hidden), BF16), pltpu.VMEM((length, width), BF16), pltpu.VMEM((length, width), F32)]
    held += [pltpu.VMEM((length, width), BF16)]
    kernel = functools.partial(ffn_kernel, layer, True)
    return call(kernel, ins + [hbm()], outs, specs, held + sems, 2 * work, moved)(*args, upstream)


def ffn_backward(layer, lengths, residual, upstream, slope, rows, weights):
    length, width = residual.shape
    hidden = slope.shape[1]
    pack = shaped((length, hidden // 2 + width), BF16)
    steps = hidden // SPAN
    scratch = [pltpu.VMEM((width, hidden), BF16), pltpu.VMEM((hidden, width), BF16)]
    scratch += [pltpu.VMEM((length, hidden), BF16), pltpu.VMEM((length, width), BF16), pltpu.VMEM((length, width), F32)]
    scratch += [pltpu.SemaphoreType.DMA((2 * steps,)), pltpu.SemaphoreType.DMA((4,))]
    own, other = weights
    return call(
        functools.partial(ffn_back_kernel, layer),
        [smem()] + [vmem()] * 5 + [hbm()] * 4,
        (pack, pack, shaped((length, width), F32), shaped((8, width), F32)),
        [hbm(), hbm(), vmem(), vmem()],
        scratch,
        0,
        0,
    )(lengths, residual, upstream, slope, *rows, *own[4:6], *other[4:6])


def attention_backward(layer, heads, x, resid_grad, saved, rows, weights):
    length, width = x.shape[-2:]
    square = length * width
    pack = shaped((length, 2 * width), BF16)
    scratch = [pltpu.VMEM((width, width), BF16)] * 4 + [pltpu.VMEM((length, width), BF16)]
    scratch += [pltpu.VMEM((length, width), BF16)] * 2
    scratch += [pltpu.VMEM((heads * length, length), BF16)]
    scratch += [pltpu.VMEM((heads * length, width), BF16), pltpu.VMEM((GROUP * length, width), BF16)]
    scratch += [pltpu.VMEM((length, width), F32)] * 2
    scratch += [pltpu.VMEM((3, length, width), BF16), pltpu.VMEM((length, width), F32)]
    scratch += [pltpu.SemaphoreType.DMA((5,)), pltpu.SemaphoreType.DMA((8,))]
    own, other = weights
    return call(
        functools.partial(attention_back_kernel, layer, heads),
        [hbm()] + [vmem()] * 7 + [hbm()] * 8,
        (pack, pack, shaped((length, width), BF16), shaped((HEADS_ROWS, width), F32)),
        [hbm(), hbm(), vmem(), vmem()],
        scratch,
        0,
        0,
    )(x, resid_grad, *saved, *rows, *own[:4], *other[:4])


LIGHT = pl.CostEstimate(flops=1, bytes_accessed=1, transcendentals=0)
BLOCKS = 8
HALF_BLOCKS = BLOCKS // 2
FFN_BITS = ((1, 2), (2, 4), (4, 1))
ATTN_BITS = ((4, 4), (1, 1), (2, 2))
ORDER = (
    "P1w K1 D0 Q1w",
    "P1a1 P0w K0 Q0w",
    "T0 Q1a1 P1a2 P0a1",
    "Q1a2 P1a3 Q0a1 P0a2",
    "Q1a3 Q0a2 P0a3 Q0a3",
    "L1ax O0 O1 L0ax",
    "g3 g2 g1 x1",
    "uA G0 G1 g1x",
    "uB T1 uC",
)


def hbm():
    return pl.BlockSpec(memory_space=pl.ANY)


def block_shift(bits, core, rank):
    shift = 0
    for pair in bits:
        on = jnp.where(core == 0, (rank & pair[0]) != 0, (rank & pair[1]) != 0)
        shift = shift * 2 + on.astype(jnp.int32)
    return shift


def exchange(array, bits):
    count = lax.axis_size("dp")
    pairs = [(at, at ^ bits[0]) for at in range(count)]
    pairs += [(count + at, count + (at ^ bits[1])) for at in range(count)]
    return lax.ppermute(array, ("section", "dp"), pairs)


def add(left, right):
    return (left.astype(F32) + right.astype(F32)).astype(BF16)


def grad_kernel(locate, meta, first, first2, second, second2, send, keep, lefts, rights, made, in_sems, out_sems):
    length = first.shape[0]
    rows = made.shape[1]
    fetched = []
    for at, (source, target) in enumerate(((first, lefts), (second, rights), (first2, lefts), (second2, rights))):
        window = target.at[pl.ds((at // 2) * length, length)]
        fetched.append(pltpu.make_async_copy(source, window, in_sems.at[at]))
        fetched[-1].start()
    for copy in fetched:
        copy.wait()
    stored = []
    for step in range(BLOCKS):
        block = ((step + HALF_BLOCKS) % BLOCKS) ^ meta[0]
        left, right = locate(block)
        made[step] = dot_tn(lefts[:, left], rights[:, right]).astype(BF16)
        target = send if step < HALF_BLOCKS else keep
        window = target.at[pl.ds((step % HALF_BLOCKS) * rows, rows)]
        stored.append(pltpu.make_async_copy(made.at[step], window, out_sems.at[step]))
        stored[-1].start()
    for copy in stored:
        copy.wait()


def locate_ffn(rows, width, half, block):
    per = width // rows
    place = jnp.maximum(block - HALF_BLOCKS, 0)
    down = block < HALF_BLOCKS
    left = pl.multiple_of(jnp.where(down, block * rows, half + (place % per) * rows), 128)
    right = pl.multiple_of(jnp.where(down, half, (place // per) * width), 128)
    return pl.ds(left, rows), pl.ds(right, width)


def locate_attn(rows, block):
    which = block // 2
    left = pl.multiple_of(jnp.where(which == 3, 2 * rows, 0) + (block % 2) * rows, 128)
    return pl.ds(left, rows), pl.ds(pl.multiple_of(which * rows, 128), rows)


def grad_blocks(locate, shift, factors, rows, width):
    first, first2, second, second2 = factors
    out = shaped((HALF_BLOCKS * rows, width), BF16)
    length = first.shape[0]
    return light_call(
        functools.partial(grad_kernel, locate),
        (out, out),
        [smem()] + [hbm()] * 4,
        [hbm()] * 2,
        scratch=[
            pltpu.VMEM((2 * length, first.shape[1]), BF16),
            pltpu.VMEM((2 * length, second.shape[1]), BF16),
            pltpu.VMEM((BLOCKS, rows, width), BF16),
            pltpu.SemaphoreType.DMA((4,)),
            pltpu.SemaphoreType.DMA((BLOCKS,)),
        ],
    )(shift.reshape(1), *factors)


def light_call(kernel, outs, in_specs, out_specs, grid=(), scratch=(), aliases=None):
    return pl.pallas_call(
        kernel,
        out_shape=outs,
        grid=grid,
        in_specs=in_specs,
        out_specs=out_specs,
        scratch_shapes=list(scratch),
        input_output_aliases=aliases or {},
        compiler_params=pltpu.CompilerParams(vmem_limit_bytes=VMEM),
        cost_estimate=LIGHT,
    )


def put_ride(total, send, rows):
    count = total.shape[0]
    width = total.shape[1]
    high = total.astype(BF16)
    send[rows : rows + count, :width] = high
    send[rows + count :, :width] = (total - high.astype(F32)).astype(BF16)


def take_ride(total, got, rows):
    count, width = total.shape
    return total + got[rows : rows + count, :width].astype(F32) + got[rows + count :, :width].astype(F32)


def add_split_kernel(*refs):
    count = len(refs) // 6
    for at in range(count):
        keep_low, keep_high, got_low, got_high = refs[4 * at : 4 * at + 4]
        send, keep = refs[4 * count + 2 * at : 4 * count + 2 * at + 2]
        keep[...] = add(keep_low[...], got_low[...])
        send[...] = add(keep_high[...], got_high[...])


def add_split(pairs):
    args, in_specs, outs, out_specs = [], [], [], []
    for keep, got in pairs:
        rows, width = keep.shape
        low = pl.BlockSpec((rows // 4, width), lambda at: (at, 0))
        high = pl.BlockSpec((rows // 4, width), lambda at: (at + 2, 0))
        args += [keep, keep, got, got]
        in_specs += [low, high, low, high]
        outs += [shaped((rows // 2, width), BF16)] * 2
        out_specs += [low, low]
    made = light_call(add_split_kernel, outs, in_specs, out_specs, (2,))(*args)
    return list(zip(made[0::2], made[1::2]))


def add_split_ride_kernel(riding, keep_in, got, tail, more, send, keep, tail_out):
    rows = keep.shape[0]
    keep[...] = add(keep_in[:rows, :], got[:rows, :])
    send[:rows, :] = add(keep_in[rows:, :], got[rows : 2 * rows, :])
    total = take_ride(tail[...], got, 2 * rows) if riding else tail[...] + more[...]
    tail_out[...] = total
    put_ride(total, send, rows)


def add_split_ride(keep, got, tail, more=None):
    rows, width = keep.shape
    half = rows // 2
    count = 2 * tail.shape[0]
    outs = (shaped((half + count, width), BF16), shaped((half, width), BF16), shaped(tail.shape, F32))
    kernel = functools.partial(add_split_ride_kernel, more is None)
    return light_call(kernel, outs, [vmem()] * 4, [vmem()] * 3)(keep, got, tail, tail if more is None else more)


def add_ride_kernel(keep, got, tail, out, tail_out):
    rows = keep.shape[0]
    total = take_ride(tail[...], got, rows)
    tail_out[...] = total
    put_ride(total, out, rows)
    out[:rows, :] = add(keep[...], got[:rows, :])


def add_ride(keep, got, tail):
    rows, width = keep.shape
    outs = (shaped((rows + 2 * tail.shape[0], width), BF16), shaped(tail.shape, F32))
    return light_call(add_ride_kernel, outs, [vmem()] * 3, [vmem()] * 2)(keep, got, tail)


def add_pack_kernel(first, first_got, second, second_got, *refs):
    rows, width = second.shape[0], first.shape[1]
    if len(refs) > 1:
        tail, out, tail_out = refs
        tail_out[...] = take_ride(tail[...], first_got, rows)
    else:
        (out,) = refs
    out[:, :width] = add(first[:rows, :], first_got[:rows, :])
    out[:, width:] = add(second[...], second_got[...])


def add_pack(first, second, tail=None):
    rows, width = second[0].shape[0], first[0].shape[1]
    out = shaped((rows, width + second[0].shape[1]), BF16)
    if tail is None:
        return light_call(add_pack_kernel, out, [vmem()] * 4, vmem())(*first, *second)
    outs = (out, shaped(tail.shape, F32))
    return light_call(add_pack_kernel, outs, [vmem()] * 5, [vmem()] * 2)(*first, *second, tail)


def choose_kernel(first, second, first_other, second_other, *outs):
    width = outs[0].shape[1]
    for core, pair in ((0, (first, first_other)), (1, (second, second_other))):
        @pl.when(this_core() == core)
        def _():
            for at, source in enumerate(pair):
                outs[2 * at][...] = source[:, :width]
                outs[2 * at + 1][...] = source[:, width:]


def choose(arrays, width):
    rows, both = arrays[0].shape
    outs = [shaped((rows, width), BF16), shaped((rows, both - width), BF16)] * 2
    return light_call(choose_kernel, outs, [vmem()] * 4, [vmem()] * 4)(*arrays)


def add_kernel(left, right, out):
    out[...] = add(left[...], right[...]) if out.dtype == BF16 else left[...] + right[...]


def light_add(left, right):
    return light_call(add_kernel, shaped(left.shape, left.dtype), [vmem()] * 2, vmem())(left, right)


def join_kernel(count, *refs):
    outs = refs[-count:]
    for at in range(count):
        rows = refs[2 * at].shape[0]
        outs[at][:rows] = refs[2 * at][...]
        outs[at][rows : 2 * rows] = refs[2 * at + 1][...]
    if len(refs) > 3 * count:
        put_ride(refs[2 * count][...], outs[0], 2 * refs[0].shape[0])


def join(pairs, tail=None):
    outs = [shaped((2 * upper.shape[0], upper.shape[1]), upper.dtype) for upper, _ in pairs]
    args = [array for pair in pairs for array in pair]
    if tail is not None:
        args.append(tail)
        outs[0] = shaped((outs[0].shape[0] + 2 * tail.shape[0], outs[0].shape[1]), BF16)
    kernel = functools.partial(join_kernel, len(pairs))
    return light_call(kernel, outs, [vmem()] * len(args), [vmem()] * len(outs))(*args)


def pick_kernel(first, second, out):
    @pl.when(this_core() == 0)
    def _():
        out[...] = second[...]

    @pl.when(this_core() == 1)
    def _():
        out[...] = first[...]


def pick(first, second):
    return light_call(pick_kernel, shaped(first.shape, first.dtype), [vmem()] * 2, vmem())(first, second)


def lay_kernel(first, second, other, out, sems):
    core = this_core()
    theirs = pltpu.make_async_copy(other, out.at[0, 1 - core, 0], sems.at[0])
    theirs.start()
    for at, source in ((0, first), (1, second)):
        @pl.when(core == at)
        def _():
            mine = pltpu.make_async_copy(source, out.at[0, at, 0], sems.at[1])
            mine.start()
            mine.wait()
    theirs.wait()


def lay(first, second, other):
    out = shaped((1, 2, 1) + first.shape, first.dtype)
    scratch = [pltpu.SemaphoreType.DMA((2,))]
    return light_call(lay_kernel, out, [vmem()] * 3, hbm(), scratch=scratch)(first, second, other)


def collect_kernel(heads, lengths, back0, gain0, attn0, ffn0, back1, attn1, ffn1, keep, send):
    width = keep.shape[1]
    at = HEADS_ROWS // 2
    count = jnp.full((1, width), lengths[this_core(), 0], jnp.int32).astype(F32)
    for layer, back, gain, attn, ffn in ((0, back0, gain0[0:1, :], attn0, ffn0), (1, back1, ffn1[2:3, :], attn1, ffn1)):
        rows = jnp.concatenate(
            [
                back[: heads + 1, :], gain, jnp.zeros((at - heads - 2, width), F32), back[at : at + heads, :],
                ffn[0:1, :], attn[0:1, :], ffn[1:2, :], count,
            ],
            axis=0,
        )

        @pl.when(this_core() == layer)
        def _():
            keep[...] = rows

        @pl.when(this_core() != layer)
        def _():
            send[...] = rows


def collect(heads, lengths, *stats):
    out = jax.ShapeDtypeStruct((HEADS_ROWS, stats[0].shape[1]), F32)
    return pl.pallas_call(
        functools.partial(collect_kernel, heads),
        out_shape=(out, out),
        in_specs=[smem()] + [vmem()] * len(stats),
        out_specs=[vmem()] * 2,
        cost_estimate=LIGHT,
    )(lengths, *stats)


def small_kernel(heads, tail, got, attn_out, ffn_out, pre_out, post_out, rms_out):
    width = tail.shape[1]
    total = take_ride(tail[...], got, 0)
    at = HEADS_ROWS // 2
    attn_out[...] = total[heads : heads + 1, :]
    ffn_out[...] = total[heads + 1 : heads + 2, :]
    lane = lax.broadcasted_iota(jnp.int32, (width, heads), 0) // (width // heads)
    ones = (lane == lax.broadcasted_iota(jnp.int32, (width, heads), 1)).astype(F32)
    high = lax.Precision.HIGHEST
    pre_out[0] = lax.dot_general(
        total[:heads, :], ones, (((1,), (0,)), ((), ())), precision=high, preferred_element_type=F32
    )
    post_out[0] = lax.dot_general(
        ones, total[at : at + heads, :], (((0,), (1,)), ((), ())), precision=high, preferred_element_type=F32
    )
    tokens = total[HEADS_ROWS - 1 : HEADS_ROWS, 0:1]
    for which in range(3):
        row = total[at + heads + which : at + heads + which + 1, :]
        rms_out[:, which : which + 1] = jnp.sqrt(jnp.sum(row, axis=1, keepdims=True) / width / tokens)


def small_outputs(heads, tail, got):
    width = tail.shape[1]
    shapes = ((1, width), (1, width), (1, heads, heads), (1, heads, heads), (1, 3))
    return pl.pallas_call(
        functools.partial(small_kernel, heads),
        out_shape=tuple(jax.ShapeDtypeStruct(shape, F32) for shape in shapes),
        cost_estimate=LIGHT,
    )(tail, got)


def unpack_kernel(part, owns, meta, *refs):
    count = 2 * len(owns)
    sources, outs, scratch = refs[:count], refs[count + 6 : count + 12], refs[count + 12 :]
    taken_ffn, given_ffn, taken_attn, given_attn, taken_sem, given_sem = scratch
    core = this_core()
    moves = []
    for which, own in enumerate(owns):
        half = core if own else 1 - core
        for group, (taken, given, place, grads) in enumerate((
            (taken_ffn, given_ffn, place_ffn, outs[:2]), (taken_attn, given_attn, place_attn, outs[2:]),
        )):
            rows = taken.shape[1]
            shift = jnp.where(half == 0, meta[1 + 2 * group], meta[2 + 2 * group])
            for step in range(HALF_BLOCKS):
                slot = HALF_BLOCKS * which + step
                at = BLOCKS * group + slot
                block = (HALF_BLOCKS * part + step) ^ shift
                window = sources[2 * which + group].at[pl.ds(step * rows, rows)]
                fetch = pltpu.make_async_copy(window, taken.at[slot], taken_sem.at[at])
                stores = [
                    (chosen, pltpu.make_async_copy(given.at[slot], target, given_sem.at[at]))
                    for chosen, target in place(half, block, grads)
                ]
                moves.append((fetch, stores, taken, given, slot))
    for fetch, *_ in moves:
        fetch.start()
    for fetch, stores, taken, given, slot in moves:
        fetch.wait()
        given[slot] = taken[slot].astype(F32)
        for chosen, copy in stores:
            pl.when(chosen)(copy.start)
    for _, stores, *_ in moves:
        for chosen, copy in stores:
            pl.when(chosen)(copy.wait)


def unpack(part, owns, meta, sources, outs):
    scratch = []
    for source, rows in zip(sources, (outs[0].shape[2] // BLOCKS, outs[2].shape[1] // 2)):
        width = source.shape[1]
        scratch += [pltpu.VMEM((BLOCKS, rows, width), BF16), pltpu.VMEM((BLOCKS, rows, width), F32)]
    scratch += [pltpu.SemaphoreType.DMA((2 * BLOCKS,))] * 2
    return light_call(
        functools.partial(unpack_kernel, part, owns),
        [shaped(out.shape, F32) for out in outs],
        [smem()] + [hbm()] * (len(sources) + len(outs)),
        [hbm()] * len(outs),
        scratch=scratch,
        aliases={1 + len(sources) + at: at for at in range(len(outs))},
    )(meta, *sources, *outs)


def blank_kernel(*refs):
    pass


def blank(shapes):
    return pl.pallas_call(
        blank_kernel,
        out_shape=tuple(jax.ShapeDtypeStruct(shape, F32) for shape in shapes),
        out_specs=[hbm()] * len(shapes),
        cost_estimate=LIGHT,
    )()


def place_ffn(half, block, outs):
    grad_in, grad_out = outs
    width, hidden = grad_in.shape[1:]
    rows = hidden // BLOCKS
    per = width // rows
    inner = jnp.maximum(block - HALF_BLOCKS, 0)
    at_out = pl.multiple_of(half * (hidden // 2) + jnp.minimum(block, HALF_BLOCKS - 1) * rows, rows)
    at_row = pl.multiple_of((inner % per) * rows, rows)
    at_column = pl.multiple_of(half * (hidden // 2) + (inner // per) * width, 128)
    return [
        (block < HALF_BLOCKS, grad_out.at[0, pl.ds(at_out, rows), :]),
        (block >= HALF_BLOCKS, grad_in.at[0, pl.ds(at_row, rows), pl.ds(at_column, width)]),
    ]


def place_attn(half, block, outs):
    width = outs[0].shape[1]
    rows = width // 2
    at_row = pl.multiple_of((block % 2) * rows, rows)
    return [
        (block // 2 == which, outs[which].at[0, pl.ds(at_row, rows), pl.ds(half * rows, rows)]) for which in range(4)
    ]


def after(values, done):
    return lax.optimization_barrier(tuple(values) + tuple(done))[: len(values)]


def param_rows(gain_attn, gain_ffn, mix_pre, mix_post):
    heads = mix_pre.shape[1]
    width = gain_attn.shape[1]
    spread = lambda mix: jnp.repeat(mix, width // heads, axis=1)
    rows = jnp.concatenate([gain_attn, gain_ffn, spread(mix_pre[0]), spread(mix_post[0].T)], axis=0)
    return jnp.pad(rows, ((0, HEADS_ROWS - rows.shape[0]), (0, 0)))


def local(
    inputs, cotangent, lengths, w_query, w_key, w_value, w_output, w_in, w_out, gain_attn, gain_ffn, mix_pre, mix_post,
):
    core = lax.axis_index("section")
    rank = lax.axis_index("dp")
    is_first = core == 0
    swap = lambda shard: lax.ppermute(shard, "section", [(0, 1), (1, 0)])
    length, width = inputs.shape[2:]
    hidden = w_in.shape[2]
    heads = mix_pre.shape[1]

    own_rows = param_rows(gain_attn, gain_ffn, mix_pre, mix_post)
    own = after((w_query, w_key, w_value, w_output), (own_rows,)) + (w_in, w_out)
    other_rows = swap(own_rows)
    other = tuple(swap(weight) for weight in own[:4])
    other += tuple(swap(weight) for weight in after(own[4:], other + (other_rows,)))
    rows = (own_rows, other_rows)
    weights = (own, other)
    ffn_shift = block_shift(FFN_BITS, core, rank)
    attn_shift = block_shift(ATTN_BITS, core, rank)

    steps = {}
    state = {"last": ()}

    def tie(value):
        return after((value,), state["last"])[0] if state["last"] else value

    def chain(layer, make_ffn, make_attn):
        bits = (FFN_BITS, ATTN_BITS)
        keep, got = [None, None], [None, None]
        riding = layer == 0

        def made(group, make):
            def run():
                send, keep[group] = make()
                got[group] = exchange(send, bits[group][0])
                return keep[group]
            return run

        def split(at, groups):
            def run():
                keep[groups[0]] = tie(keep[groups[0]])
                if riding and groups == (0,):
                    send, kept, made_all["tail"] = add_split_ride(
                        keep[0], got[0], made_all["tail"], made_all["more"] if at == 1 else None
                    )
                    parts = [(send, kept)]
                else:
                    parts = add_split([(keep[group], got[group]) for group in groups])
                for group, (send, kept) in zip(groups, parts):
                    keep[group] = kept
                    got[group] = exchange(send, bits[group][at])
                return keep[groups[0]]
            return run

        def third(group):
            def run():
                keep[group] = tie(keep[group])
                if riding and group == 0:
                    keep[0], made_all["tail"] = add_ride(keep[0], got[0], made_all["tail"])
                else:
                    keep[group] = light_add(keep[group], got[group])
                got[group] = exchange(keep[group], (8, 8))
                return keep[group]
            return run

        def summed():
            keep[0] = tie(keep[0])
            rows, bit = keep[1].shape[0], 16
            while bit < lax.axis_size("dp"):
                more = got[0]
                keep[0], keep[1] = add(keep[0], more), add(keep[1], got[1])
                if riding:
                    tail = made_all["tail"] + more[rows : rows + HEADS_ROWS].astype(F32)
                    tail = tail + more[rows + HEADS_ROWS :].astype(F32)
                    high = tail.astype(BF16)
                    terms = [keep[0][:rows], high, (tail - high.astype(F32)).astype(BF16)]
                    made_all["tail"], keep[0] = tail, jnp.concatenate(terms, axis=0)
                got[:] = [exchange(array, (bit, bit)) for array in keep]
                bit *= 2
            pairs = ((keep[0], got[0]), (keep[1], got[1]))
            if riding:
                made_all[layer], made_all["tail"] = add_pack(*pairs, made_all["tail"])
            else:
                made_all[layer] = add_pack(*pairs)
            made_all["hand", layer] = lax.ppermute(made_all[layer], "section", [(1 - layer, layer)])
            return made_all[layer]

        name = str(layer)
        steps.update({
            "P" + name + "w": made(0, make_ffn), "Q" + name + "w": made(1, make_attn),
            "P" + name + "a1": split(1, (0,)), "Q" + name + "a1": split(1, (1,)), "L" + name + "a1": split(1, (0, 1)),
            "P" + name + "a2": split(2, (0,)), "Q" + name + "a2": split(2, (1,)), "L" + name + "a2": split(2, (0, 1)),
            "P" + name + "a3": third(0), "Q" + name + "a3": third(1), "L" + name + "ax": summed,
        })

    def gather():
        bits = [FFN_BITS, ATTN_BITS] + [[pair[::-1] for pair in group] for group in (FFN_BITS, ATTN_BITS)]
        held, got = [None] * 4, [None] * 4

        def send(at):
            got[:] = [exchange(held[part], bits[part][at]) for part in range(4)]
            return held[0]

        def start():
            arrays = (tie(made_all[0]), made_all[1], made_all["hand", 0], made_all["hand", 1])
            held[:] = choose(arrays, width)
            return send(2)

        def second_gather():
            held[:] = join([(tie(held[0]), got[0])] + list(zip(held[1:], got[1:])))
            return send(1)

        def last_own():
            held[0], *got[:] = after(held[:1] + got, state["last"])
            held[:2] = join(list(zip(held[:2], got[:2])), made_all["tail"])
            got[:2] = [exchange(held[part], bits[part][0]) for part in range(2)]
            return held[0]

        def last_other():
            held[2] = tie(held[2])
            held[2:] = join(list(zip(held[2:], got[2:])))
            return held[2]

        def others():
            *held[2:], got[0], got[1] = after(held[2:] + got[:2], state["last"])
            got[2:] = [exchange(held[part], bits[part][0]) for part in (2, 3)]
            return held[2]

        def first():
            made_all["grads"] = unpack(0, (True, False), place_meta, (tie(held[0]), *held[1:]), made_all["grads"])
            return made_all["grads"][0]

        def second(own):
            def run():
                pair = got[:2] if own else got[2:]
                made_all["grads"] = unpack(1, (own,), place_meta, (tie(pair[0]), pair[1]), made_all["grads"])
                return made_all["grads"][0]
            return run

        def small_end():
            rows = HALF_BLOCKS * (hidden // BLOCKS)
            made["small"] = small_outputs(heads, tie(made_all["tail"]), got[0][rows:])
            return made["small"][0]

        steps.update({
            "g3": start, "g2": second_gather, "g1": last_own, "x1": last_other, "uA": first, "g1x": others, "uB": second(True), "uC": second(False), "T1": small_end,
        })

    def ffn_blocks(first, second):
        factors = (tie(first[0]), first[1], second[0], swap(second[1]))
        locate = functools.partial(locate_ffn, hidden // BLOCKS, width, hidden // 2)
        return grad_blocks(locate, ffn_shift, factors, hidden // BLOCKS, width)

    def attn_blocks(both, pack):
        factors = (tie(both[0]), both[1], pack[0], swap(pack[1]))
        locate = functools.partial(locate_attn, width // 2)
        return grad_blocks(locate, attn_shift, factors, width // 2, width // 2)

    both0, *qkvp0, residual0, stats_a0 = attention_forward(0, heads, lengths, inputs, rows, weights)
    mid, own0, send0, slope0, stats_f0 = ffn_forward(0, lengths, residual0, rows, weights)
    both0_other, send0_other = swap(both0), swap(send0)
    both1, *qkvp1, residual1, stats_a1 = attention_forward(1, heads, lengths, mid, rows, weights)
    (residual1,) = after((residual1,), (both0_other, send0_other))
    both1_other = swap(both1)
    last, own1, send1, own1b, send1b, resid1, stats_f1 = ffn_forward(
        1, lengths, residual1, rows, weights, cotangent
    )
    own1, send1_other = after((own1, swap(send1)), (both1_other,))
    made = {}

    def attention1():
        made["pack1"], made["send_pack1"], made["grad1"], made["stats_b1"] = attention_backward(
            1, heads, mid, tie(resid1), qkvp1, rows, weights
        )
        return made["grad1"]

    def ffn0():
        made["own0b"], made["send0b"], made["resid0"], made["stats_g0"] = ffn_backward(
            0, lengths, residual0, tie(made["grad1"]), slope0, rows, weights
        )
        return made["resid0"]

    def attention0():
        made["pack0"], made["send_pack0"], made["grad0"], made["stats_b0"] = attention_backward(
            0, heads, inputs, tie(made["resid0"]), qkvp0, rows, weights
        )
        return made["grad0"]

    steps.update({"K1": attention1, "D0": ffn0, "K0": attention0})
    place_meta = jnp.stack(
        [core] + [block_shift(bits, which, rank) for bits in (FFN_BITS, ATTN_BITS) for which in range(2)]
    ).astype(jnp.int32)
    made_all = {"grads": blank((w_in.shape, w_out.shape) + (w_query.shape,) * 4)}
    chain(
        1,
        lambda: ffn_blocks((own1, send1_other), (own1b, send1b)),
        lambda: attn_blocks((both1, both1_other), (made["pack1"], made["send_pack1"])),
    )
    chain(
        0,
        lambda: ffn_blocks((own0, send0_other), (made["own0b"], made["send0b"])),
        lambda: attn_blocks((both0, both0_other), (made["pack0"], made["send_pack0"])),
    )

    def small_start():
        made_all["tail"], send = collect(
            heads, lengths, tie(made["stats_b0"]), made["stats_g0"], stats_a0, stats_f0, made["stats_b1"], stats_a1, stats_f1
        )
        made_all["more"] = swap(send)
        return made_all["tail"]

    def send_rows(name, first, second):
        def run():
            made[name] = swap(pick(tie(first()), second()))
            return first()
        return run

    def lay_rows(name, first, second):
        def run():
            made[name] = lay(tie(first()), second(), made[name])
            return made[name]
        return run

    mids = ("outputs", lambda: mid, lambda: last)
    grads = ("grads", lambda: made["grad0"], lambda: made["grad1"])
    steps.update({"O0": send_rows(*mids), "O1": lay_rows(*mids), "G0": send_rows(*grads), "G1": lay_rows(*grads)})
    steps["T0"] = small_start
    gather()
    for name in [name for line in ORDER for name in line.split()]:
        with jax.named_scope(name):
            state["last"] = (steps[name](),)

    w_in_grad, w_out_grad, *rest = made_all["grads"]
    return (made["outputs"], made["grads"], *rest, w_in_grad, w_out_grad, *made["small"])


def solution(mesh):
    in_specs = (
        P(None, "dp", None, None),
        P(None, "dp", None, None),
        P(None, "dp"),
        P("section", None, None),
        P("section", None, None),
        P("section", None, None),
        P("section", None, None),
        P("section", None, None),
        P("section", None, None),
        P("section", None),
        P("section", None),
        P("section", None, None),
        P("section", None, None),
    )
    out_specs = (
        P("section", None, "dp", None, None),
        P("section", None, "dp", None, None),
        P("section", None, None),
        P("section", None, None),
        P("section", None, None),
        P("section", None, None),
        P("section", None, None),
        P("section", None, None),
        P("section", None),
        P("section", None),
        P("section", None, None),
        P("section", None, None),
        P("section", None),
    )
    return jax.shard_map(local, mesh=mesh, in_specs=in_specs, out_specs=out_specs, check_vma=False)
```

```python
import functools

import jax
import jax.numpy as jnp
from jax import lax
from jax.experimental import pallas as pl
from jax.experimental.pallas import tpu as pltpu
from jax.sharding import PartitionSpec as P

EPSILON = 1e-06
MASKED = -1e30
F32 = jnp.float32
BF16 = jnp.bfloat16


HEADS_ROWS = 32
GROUP = 2
VMEM = 60 << 20
SPAN = 1536


def row_scale(values):
    return lax.rsqrt(jnp.mean(values * values, axis=-1, keepdims=True) + EPSILON)


def norm_back(values, gain, grad):
    scale = row_scale(values)
    weighted = grad * gain
    inner = jnp.mean(values * weighted, axis=-1, keepdims=True)
    grad_values = scale * weighted - values * (scale * scale * scale) * inner
    return grad_values, jnp.sum(grad * values * scale, axis=0, keepdims=True)


def gelu_pair(values):
    square = values * values
    tanh = jnp.tanh(values * (0.7978845608028654 + 0.7978845608028654 * 0.044715 * square))
    half = 0.5 * (1.0 + tanh)
    slope = half + 0.5 * values * (1.0 - tanh * tanh) * (
        0.7978845608028654 + 3.0 * 0.7978845608028654 * 0.044715 * square
    )
    return values * half, slope


def dot_nn(left, right):
    return lax.dot_general(left, right, (((1,), (0,)), ((), ())), preferred_element_type=F32)


def dot_nt(left, right):
    return lax.dot_general(left, right, (((1,), (1,)), ((), ())), preferred_element_type=F32)


def dot_tn(left, right):
    return lax.dot_general(left, right, (((0,), (0,)), ((), ())), preferred_element_type=F32)


def this_core():
    return lax.axis_index("section")


def sequence_rows(array):
    return array.at[this_core(), 0] if len(array.shape) == 4 else array


class Weight:
    def __init__(self, mine, own, other, held, sem):
        self.mine, self.own, self.other, self.held, self.sem = mine, own, other, held, sem

    def copy(self, source, cut):
        return pltpu.make_async_copy(source.at[(0,) + cut], self.held.at[cut], self.sem)

    def start(self, cut=(slice(None), slice(None))):
        @pl.when(self.mine)
        def _():
            self.copy(self.own, cut).start()

        @pl.when(jnp.logical_not(self.mine))
        def _():
            self.copy(self.other, cut).start()

    def wait(self, cut=(slice(None), slice(None))):
        self.copy(self.own, cut).wait()


def param_row(mine, own, other, at, count=1):
    rows = pl.ds(at, count)
    return jnp.where(mine, own[rows, :], other[rows, :])


def attention_kernel(
    layer, heads, lengths, x_in, own_rows, other_rows, wq, wk, wv, wo, wq2, wk2, wv2, wo2,
    both_out, query_out, key_out, value_out, probs_out, residual_out, stats_out,
    held_q, held_k, held_v, held_o, x, keys_upper, keys_lower, values_mixed, sems,
):
    mine = this_core() == layer
    brought = pltpu.make_async_copy(sequence_rows(x_in), x, sems.at[4])
    brought.start()
    weights = [
        Weight(mine, own, other, held, sems.at[at])
        for at, (own, other, held) in enumerate(
            ((wq, wq2, held_q), (wk, wk2, held_k), (wv, wv2, held_v), (wo, wo2, held_o))
        )
    ]
    for weight in weights:
        weight.start()
    length, width = x.shape
    half = length // 2
    brought.wait()
    values = x[...].astype(F32)
    gain = param_row(mine, own_rows, other_rows, 0)
    both_out[:, :width] = (values * row_scale(values) * gain).astype(BF16)
    for weight, held, out, factor in (
        (weights[0], held_q, query_out, (width // heads) ** -0.5),
        (weights[1], held_k, key_out, 1.0),
        (weights[2], held_v, value_out, 1.0),
    ):
        weight.wait()
        made = dot_nn(both_out[:, :width], held[...]).astype(BF16)
        out[...] = (made.astype(F32) * factor).astype(BF16) if factor != 1.0 else made

    def softmax(logits, first):
        rows = lax.broadcasted_iota(jnp.int32, logits.shape, 0)
        columns = lax.broadcasted_iota(jnp.int32, logits.shape, 1) + first
        logits = jnp.where(rows <= columns, logits, MASKED)
        exponent = jnp.exp(logits - jnp.max(logits, axis=0, keepdims=True))
        return (exponent * (1.0 / jnp.sum(exponent, axis=0, keepdims=True))).astype(BF16)

    for first in range(0, heads, GROUP):
        for at in range(first, first + GROUP):
            mixed = key_out[...].astype(F32) * param_row(mine, own_rows, other_rows, 2 + at)
            high = mixed.astype(BF16)
            low = (mixed - high.astype(F32)).astype(BF16)
            place = (at - first) * half
            for which, part in enumerate((high, low)):
                keys_upper[which, place : place + half, :] = part[:half]
                keys_lower[which, place : place + half, :] = part[half:]
        upper = dot_nt(keys_upper[0], query_out[...]) + dot_nt(keys_upper[1], query_out[...])
        lower = dot_nt(keys_lower[0], query_out[half:, :]) + dot_nt(keys_lower[1], query_out[half:, :])
        for at in range(first, first + GROUP):
            row = at * length
            part = slice((at - first) * half, (at - first + 1) * half)
            probs_out[row : row + half, :half] = softmax(upper[part, :half], 0)
            probs_out[row + half : row + length, :half] = jnp.zeros((length - half, half), BF16)
            late = jnp.concatenate([upper[part, half:], lower[part]], axis=0)
            probs_out[row : row + length, half:] = softmax(late, half)
            scale = param_row(mine, own_rows, other_rows, 2 + heads + at)
            values_mixed[row : row + length, :] = value_out[...] * scale.astype(BF16)
    both_out[:, width:] = dot_tn(probs_out[...], values_mixed[...]).astype(BF16)
    weights[3].wait()
    branch = dot_nn(both_out[:, width:], held_o[...])
    residual_out[...] = values + branch
    valid = lax.broadcasted_iota(jnp.int32, (length, 1), 0) < lengths[this_core(), 0]
    stats_out[...] = jnp.broadcast_to(
        jnp.sum(jnp.where(valid, branch * branch, 0.0), axis=0, keepdims=True), stats_out.shape
    )


def ffn_kernel(
    layer, backward, lengths, residual, own_rows, other_rows, w_in, w_out, w_in2, w_out2, *refs
):
    if backward:
        upstream_in, refs = refs[0], refs[1:]
        out, own_first, send_first, own_second, send_second, resid_out, stats_out = refs[:7]
        held_in, held_out, normed, act, total, pre_grad, branch_grad, back_total, upstream, sems, out_sems = refs[7:]
        brought = pltpu.make_async_copy(sequence_rows(upstream_in), upstream, out_sems.at[8])
        brought.start()
    else:
        out, own_first, send_first, slope_out, stats_out = refs[:5]
        held_in, held_out, normed, act, total, sems, out_sems = refs[5:]
    core = this_core()
    mine = core == layer
    length, width = residual.shape
    hidden = held_in.shape[1]
    steps = hidden // SPAN
    half = hidden // 2
    cuts_in = [(slice(None), pl.ds(step * SPAN, SPAN)) for step in range(steps)]
    cuts_out = [(pl.ds(step * SPAN, SPAN), slice(None)) for step in range(steps)]
    ins = [Weight(mine, w_in, w_in2, held_in, sems.at[step]) for step in range(steps)]
    outs = [Weight(mine, w_out, w_out2, held_out, sems.at[steps + step]) for step in range(steps)]
    for step in range(steps):
        ins[step].start(cuts_in[step])
        outs[step].start(cuts_out[step])
    values = residual[...]
    normed[...] = (values * row_scale(values) * param_row(mine, own_rows, other_rows, 1)).astype(BF16)
    valid = lax.broadcasted_iota(jnp.int32, (length, 1), 0) < lengths[core, 0]
    copies = []

    def send(source, target, at):
        copy = pltpu.make_async_copy(source, target, out_sems.at[at])
        copy.start()
        copies.append(copy)

    send(normed, own_first.at[:, pl.ds(half, width)], 0)
    send(normed, send_first.at[:, pl.ds(half, width)], 1)
    if backward:
        brought.wait()
        branch_grad[...] = jnp.where(valid, upstream[...], jnp.zeros_like(upstream))
        send(branch_grad, own_second.at[:, pl.ds(half, width)], 2)
        send(branch_grad, send_second.at[:, pl.ds(half, width)], 3)
    for step in range(steps):
        span = pl.ds(step * SPAN, SPAN)
        ins[step].wait(cuts_in[step])
        made, slope = gelu_pair(dot_nn(normed[...], held_in[:, span]))
        act[:, span] = made.astype(BF16)
        outs[step].wait(cuts_out[step])
        part = dot_nn(act[:, span], held_out[span, :])
        total[...] = part if step == 0 else total[...] + part
        if backward:
            grad = (dot_nt(branch_grad[...], held_out[span, :]) * slope).astype(BF16)
            pre_grad[:, span] = grad
            part = dot_nt(pre_grad[:, span], held_in[:, span])
            back_total[...] = part if step == 0 else back_total[...] + part
        else:
            slope_out[:, span] = slope.astype(BF16)
    mine_at = pl.ds(pl.multiple_of(core * half, 128), half)
    other_at = pl.ds(pl.multiple_of((1 - core) * half, 128), half)
    send(act.at[:, mine_at], own_first.at[:, pl.ds(0, half)], 4)
    send(act.at[:, other_at], send_first.at[:, pl.ds(0, half)], 5)
    if backward:
        send(pre_grad.at[:, mine_at], own_second.at[:, pl.ds(0, half)], 6)
        send(pre_grad.at[:, other_at], send_second.at[:, pl.ds(0, half)], 7)
    branch = total[...]
    made = jnp.where(valid, residual[...] + branch, 0.0)
    out[...] = made.astype(BF16)
    stats_out[0:1, :] = jnp.sum(made * made, axis=0, keepdims=True)
    stats_out[1:2, :] = jnp.sum(jnp.where(valid, branch * branch, 0.0), axis=0, keepdims=True)
    if backward:
        back, gain_grad = norm_back(
            residual[...], param_row(mine, own_rows, other_rows, 1), back_total[...]
        )
        resid_out[...] = branch_grad[...].astype(F32) + back
        stats_out[2:3, :] = gain_grad
    for copy in copies:
        copy.wait()


def ffn_back_kernel(
    layer, lengths, residual, upstream, slope, own_rows, other_rows, w_in, w_out, w_in2, w_out2,
    own_second, send_second, resid_out, stats_out,
    held_in, held_out, pre_grad, branch_grad, back_total, sems, out_sems,
):
    core = this_core()
    mine = core == layer
    length, width = residual.shape
    hidden = held_in.shape[1]
    steps = hidden // SPAN
    half = hidden // 2
    cuts_in = [(slice(None), pl.ds(step * SPAN, SPAN)) for step in range(steps)]
    cuts_out = [(pl.ds(step * SPAN, SPAN), slice(None)) for step in range(steps)]
    ins = [Weight(mine, w_in, w_in2, held_in, sems.at[step]) for step in range(steps)]
    outs = [Weight(mine, w_out, w_out2, held_out, sems.at[steps + step]) for step in range(steps)]
    for step in range(steps):
        outs[step].start(cuts_out[step])
        ins[step].start(cuts_in[step])
    valid = lax.broadcasted_iota(jnp.int32, (length, 1), 0) < lengths[core, 0]
    branch_grad[...] = jnp.where(valid, upstream[...], jnp.zeros_like(upstream))
    copies = []

    def send(source, target, at):
        copy = pltpu.make_async_copy(source, target, out_sems.at[at])
        copy.start()
        copies.append(copy)

    send(branch_grad, own_second.at[:, pl.ds(half, width)], 0)
    send(branch_grad, send_second.at[:, pl.ds(half, width)], 1)
    for step in range(steps):
        span = pl.ds(step * SPAN, SPAN)
        outs[step].wait(cuts_out[step])
        grad = dot_nt(branch_grad[...], held_out[span, :]) * slope[:, span].astype(F32)
        pre_grad[:, span] = grad.astype(BF16)
        ins[step].wait(cuts_in[step])
        part = dot_nt(pre_grad[:, span], held_in[:, span])
        back_total[...] = part if step == 0 else back_total[...] + part
    send(pre_grad.at[:, pl.ds(pl.multiple_of(core * half, 128), half)], own_second.at[:, pl.ds(0, half)], 2)
    send(pre_grad.at[:, pl.ds(pl.multiple_of((1 - core) * half, 128), half)], send_second.at[:, pl.ds(0, half)], 3)
    back, gain_grad = norm_back(residual[...], param_row(mine, own_rows, other_rows, 1), back_total[...])
    resid_out[...] = branch_grad[...].astype(F32) + back
    stats_out[0:1, :] = gain_grad
    for copy in copies:
        copy.wait()


def attention_back_kernel(
    layer, heads, x_in, resid_grad, query, key, value, probs, own_rows, other_rows,
    wq, wk, wv, wo, wq2, wk2, wv2, wo2,
    own_pack, send_pack, grad_out, stats_out,
    held_q, held_k, held_v, held_o, x, attn_grad, head_grad, logit_grad, key_scaled, value_scaled,
    key_grad, value_grad, piece, total, sems, out_sems,
):
    core = this_core()
    brought = pltpu.make_async_copy(sequence_rows(x_in), x, sems.at[4])
    brought.start()
    mine = core == layer
    weights = [
        Weight(mine, own, other, held, sems.at[at])
        for at, (own, other, held) in enumerate(
            ((wo, wo2, held_o), (wq, wq2, held_q), (wk, wk2, held_k), (wv, wv2, held_v))
        )
    ]
    for weight in weights:
        weight.start()
    length, width = x.shape
    half = width // 2
    copies = []

    def send(source, at, sem):
        for target, which in ((own_pack, core), (send_pack, 1 - core)):
            copy = pltpu.make_async_copy(
                source.at[:, pl.ds(pl.multiple_of(which * half, 128), half)],
                target.at[:, pl.ds(at * half, half)],
                out_sems.at[sem + (0 if target is own_pack else 1)],
            )
            copy.start()
            copies.append(copy)

    attn_grad[...] = resid_grad[...].astype(BF16)
    send(attn_grad, 3, 0)
    weights[0].wait()
    head_grad[...] = dot_nt(attn_grad[...], held_o[...]).astype(BF16)

    for first in range(0, heads, GROUP):
        span = slice(first * length, (first + GROUP) * length)
        pres, posts = [], []
        for at in range(first, first + GROUP):
            pres.append(param_row(mine, own_rows, other_rows, 2 + at))
            posts.append(param_row(mine, own_rows, other_rows, 2 + heads + at))
            rows = slice(at * length, (at + 1) * length)
            key_scaled[rows, :] = key[...] * pres[-1].astype(BF16)
            place = (at - first) * length
            value_scaled[place : place + length, :] = value[...] * posts[-1].astype(BF16)
        grad_probs = dot_nt(value_scaled[...], head_grad[...])
        routed = dot_nn(probs[span, :], head_grad[...])
        for at in range(first, first + GROUP):
            part = slice((at - first) * length, (at - first + 1) * length)
            prob = probs[at * length : (at + 1) * length, :].astype(F32)
            inner = jnp.sum(prob * grad_probs[part], axis=0, keepdims=True)
            logit_grad[at * length : (at + 1) * length, :] = (prob * (grad_probs[part] - inner)).astype(BF16)
            stats_out[HEADS_ROWS // 2 + at : HEADS_ROWS // 2 + at + 1, :] = jnp.sum(
                routed[part] * value[...].astype(F32), axis=0, keepdims=True
            )
            more = routed[part] * posts[at - first]
            value_grad[...] = more if at == 0 else value_grad[...] + more
        routed = dot_nn(logit_grad[span, :], query[...])
        for at in range(first, first + GROUP):
            part = slice((at - first) * length, (at - first + 1) * length)
            stats_out[at : at + 1, :] = jnp.sum(routed[part] * key[...].astype(F32), axis=0, keepdims=True)
            more = routed[part] * pres[at - first]
            key_grad[...] = more if at == 0 else key_grad[...] + more
    piece[2] = value_grad[...].astype(BF16)
    send(piece.at[2], 2, 6)
    piece[1] = key_grad[...].astype(BF16)
    send(piece.at[1], 1, 4)
    weights[3].wait()
    total[...] = dot_nt(piece[2], held_v[...])
    weights[2].wait()
    total[...] += dot_nt(piece[1], held_k[...])
    factor = (width // heads) ** -0.5
    piece[0] = (dot_tn(logit_grad[...], key_scaled[...]) * factor).astype(BF16)
    send(piece.at[0], 0, 2)
    weights[1].wait()
    brought.wait()
    back, gain_grad = norm_back(
        x[...].astype(F32),
        param_row(mine, own_rows, other_rows, 0),
        total[...] + dot_nt(piece[0], held_q[...]),
    )
    grad_out[...] = (resid_grad[...] + back).astype(BF16)
    stats_out[heads : heads + 1, :] = gain_grad
    for copy in copies:
        copy.wait()


def vmem():
    return pl.BlockSpec(memory_space=pltpu.VMEM)


def smem():
    return pl.BlockSpec(memory_space=pltpu.SMEM)


def shaped(shape, kind):
    return jax.ShapeDtypeStruct(shape, kind)


def call(kernel, in_specs, outs, out_specs, scratch, flops, bytes_accessed):
    return pl.pallas_call(
        kernel,
        out_shape=outs,
        in_specs=in_specs,
        out_specs=out_specs,
        scratch_shapes=scratch,
        compiler_params=pltpu.CompilerParams(vmem_limit_bytes=VMEM),
        cost_estimate=pl.CostEstimate(flops=flops, bytes_accessed=bytes_accessed, transcendentals=0) if flops else LIGHT,
    )


def attention_forward(layer, heads, lengths, x, rows, weights):
    length, width = x.shape[-2:]
    square = length * width
    outs = (
        shaped((length, 2 * width), BF16),
        shaped((length, width), BF16),
        shaped((length, width), BF16),
        shaped((length, width), BF16),
        shaped((heads * length, length), BF16),
        shaped((length, width), F32),
        shaped((8, width), F32),
    )
    scratch = [pltpu.VMEM((width, width), BF16)] * 4 + [pltpu.VMEM((length, width), BF16)]
    scratch += [pltpu.VMEM((2, GROUP * length // 2, width), BF16)] * 2
    scratch += [pltpu.VMEM((heads * length, width), BF16), pltpu.SemaphoreType.DMA((5,))]
    kernel = functools.partial(attention_kernel, layer, heads)
    run = call(
        kernel, [smem(), hbm(), vmem(), vmem()] + [hbm()] * 8, outs, [vmem()] * 7, scratch,
        8 * square * width + 6 * heads * length * square, 8 * width * width + 20 * square,
    )
    own, other = weights
    return run(lengths, x, *rows, *own[:4], *other[:4])


def ffn_forward(layer, lengths, residual, rows, weights, upstream=None):
    length, width = residual.shape
    hidden = weights[0][4].shape[2]
    half = hidden // 2
    pack = shaped((length, half + width), BF16)
    steps = hidden // SPAN
    held = [pltpu.VMEM((width, hidden), BF16), pltpu.VMEM((hidden, width), BF16)]
    held += [pltpu.VMEM((length, width), BF16), pltpu.VMEM((length, hidden), BF16), pltpu.VMEM((length, width), F32)]
    sems = [pltpu.SemaphoreType.DMA((2 * steps,)), pltpu.SemaphoreType.DMA((9,))]
    ins = [smem(), vmem(), vmem(), vmem()] + [hbm()] * 4
    work = 4 * length * width * hidden
    moved = 4 * width * hidden + 8 * length * hidden
    own, other = weights
    args = (lengths, residual) + rows + own[4:6] + other[4:6]
    if upstream is None:
        outs = (shaped((length, width), BF16), pack, pack, shaped((length, hidden), BF16), shaped((8, width), F32))
        specs = [vmem(), hbm(), hbm(), vmem(), vmem()]
        return call(functools.partial(ffn_kernel, layer, False), ins, outs, specs, held + sems, work, moved)(*args)
    outs = (shaped((length, width), BF16), pack, pack, pack, pack, shaped((length, width), F32), shaped((8, width), F32))
    specs = [vmem()] + [hbm()] * 4 + [vmem()] * 2
    held += [pltpu.VMEM((length, hidden), BF16), pltpu.VMEM((length, width), BF16), pltpu.VMEM((length, width), F32)]
    held += [pltpu.VMEM((length, width), BF16)]
    kernel = functools.partial(ffn_kernel, layer, True)
    return call(kernel, ins + [hbm()], outs, specs, held + sems, 2 * work, moved)(*args, upstream)


def ffn_backward(layer, lengths, residual, upstream, slope, rows, weights):
    length, width = residual.shape
    hidden = slope.shape[1]
    pack = shaped((length, hidden // 2 + width), BF16)
    steps = hidden // SPAN
    scratch = [pltpu.VMEM((width, hidden), BF16), pltpu.VMEM((hidden, width), BF16)]
    scratch += [pltpu.VMEM((length, hidden), BF16), pltpu.VMEM((length, width), BF16), pltpu.VMEM((length, width), F32)]
    scratch += [pltpu.SemaphoreType.DMA((2 * steps,)), pltpu.SemaphoreType.DMA((4,))]
    own, other = weights
    return call(
        functools.partial(ffn_back_kernel, layer),
        [smem()] + [vmem()] * 5 + [hbm()] * 4,
        (pack, pack, shaped((length, width), F32), shaped((8, width), F32)),
        [hbm(), hbm(), vmem(), vmem()],
        scratch,
        0,
        0,
    )(lengths, residual, upstream, slope, *rows, *own[4:6], *other[4:6])


def attention_backward(layer, heads, x, resid_grad, saved, rows, weights):
    length, width = x.shape[-2:]
    square = length * width
    pack = shaped((length, 2 * width), BF16)
    scratch = [pltpu.VMEM((width, width), BF16)] * 4 + [pltpu.VMEM((length, width), BF16)]
    scratch += [pltpu.VMEM((length, width), BF16)] * 2
    scratch += [pltpu.VMEM((heads * length, length), BF16)]
    scratch += [pltpu.VMEM((heads * length, width), BF16), pltpu.VMEM((GROUP * length, width), BF16)]
    scratch += [pltpu.VMEM((length, width), F32)] * 2
    scratch += [pltpu.VMEM((3, length, width), BF16), pltpu.VMEM((length, width), F32)]
    scratch += [pltpu.SemaphoreType.DMA((5,)), pltpu.SemaphoreType.DMA((8,))]
    own, other = weights
    return call(
        functools.partial(attention_back_kernel, layer, heads),
        [hbm()] + [vmem()] * 7 + [hbm()] * 8,
        (pack, pack, shaped((length, width), BF16), shaped((HEADS_ROWS, width), F32)),
        [hbm(), hbm(), vmem(), vmem()],
        scratch,
        0,
        0,
    )(x, resid_grad, *saved, *rows, *own[:4], *other[:4])


LIGHT = pl.CostEstimate(flops=1, bytes_accessed=1, transcendentals=0)
BLOCKS = 8
HALF_BLOCKS = BLOCKS // 2
FFN_BITS = ((1, 2), (2, 4), (4, 1))
ATTN_BITS = ((4, 4), (1, 1), (2, 2))
ORDER = (
    "P1w K1 D0 Q1w",
    "P1a1 P0w K0 Q0w",
    "T0 Q1a1 P1a2 P0a1",
    "Q1a2 P1a3 Q0a1 P0a2",
    "Q0a2 Q1a3 P0a3 Q0a3",
    "L1ax O0 O1 L0ax",
    "g3 g2 g1 x1",
    "uA G0 G1 g1x",
    "uB T1 uC",
)


def hbm():
    return pl.BlockSpec(memory_space=pl.ANY)


def block_shift(bits, core, rank):
    shift = 0
    for pair in bits:
        on = jnp.where(core == 0, (rank & pair[0]) != 0, (rank & pair[1]) != 0)
        shift = shift * 2 + on.astype(jnp.int32)
    return shift


def exchange(array, bits):
    count = lax.axis_size("dp")
    pairs = [(at, at ^ bits[0]) for at in range(count)]
    pairs += [(count + at, count + (at ^ bits[1])) for at in range(count)]
    return lax.ppermute(array, ("section", "dp"), pairs)


def add(left, right):
    return (left.astype(F32) + right.astype(F32)).astype(BF16)


def grad_kernel(locate, meta, first, first2, second, second2, send, keep, lefts, rights, made, in_sems, out_sems):
    length = first.shape[0]
    rows = made.shape[1]
    fetched = []
    for at, (source, target) in enumerate(((first, lefts), (second, rights), (first2, lefts), (second2, rights))):
        window = target.at[pl.ds((at // 2) * length, length)]
        fetched.append(pltpu.make_async_copy(source, window, in_sems.at[at]))
        fetched[-1].start()
    for copy in fetched:
        copy.wait()
    stored = []
    for step in range(BLOCKS):
        block = ((step + HALF_BLOCKS) % BLOCKS) ^ meta[0]
        left, right = locate(block)
        made[step] = dot_tn(lefts[:, left], rights[:, right]).astype(BF16)
        target = send if step < HALF_BLOCKS else keep
        window = target.at[pl.ds((step % HALF_BLOCKS) * rows, rows)]
        stored.append(pltpu.make_async_copy(made.at[step], window, out_sems.at[step]))
        stored[-1].start()
    for copy in stored:
        copy.wait()


def locate_ffn(rows, width, half, block):
    per = width // rows
    place = jnp.maximum(block - HALF_BLOCKS, 0)
    down = block < HALF_BLOCKS
    left = pl.multiple_of(jnp.where(down, block * rows, half + (place % per) * rows), 128)
    right = pl.multiple_of(jnp.where(down, half, (place // per) * width), 128)
    return pl.ds(left, rows), pl.ds(right, width)


def locate_attn(rows, block):
    which = block // 2
    left = pl.multiple_of(jnp.where(which == 3, 2 * rows, 0) + (block % 2) * rows, 128)
    return pl.ds(left, rows), pl.ds(pl.multiple_of(which * rows, 128), rows)


def grad_blocks(locate, shift, factors, rows, width):
    first, first2, second, second2 = factors
    out = shaped((HALF_BLOCKS * rows, width), BF16)
    length = first.shape[0]
    return light_call(
        functools.partial(grad_kernel, locate),
        (out, out),
        [smem()] + [hbm()] * 4,
        [hbm()] * 2,
        scratch=[
            pltpu.VMEM((2 * length, first.shape[1]), BF16),
            pltpu.VMEM((2 * length, second.shape[1]), BF16),
            pltpu.VMEM((BLOCKS, rows, width), BF16),
            pltpu.SemaphoreType.DMA((4,)),
            pltpu.SemaphoreType.DMA((BLOCKS,)),
        ],
    )(shift.reshape(1), *factors)


def light_call(kernel, outs, in_specs, out_specs, grid=(), scratch=(), aliases=None):
    return pl.pallas_call(
        kernel,
        out_shape=outs,
        grid=grid,
        in_specs=in_specs,
        out_specs=out_specs,
        scratch_shapes=list(scratch),
        input_output_aliases=aliases or {},
        compiler_params=pltpu.CompilerParams(vmem_limit_bytes=VMEM),
        cost_estimate=LIGHT,
    )


def put_ride(total, send, rows):
    count = total.shape[0]
    width = total.shape[1]
    high = total.astype(BF16)
    send[rows : rows + count, :width] = high
    send[rows + count :, :width] = (total - high.astype(F32)).astype(BF16)


def take_ride(total, got, rows):
    count, width = total.shape
    return total + got[rows : rows + count, :width].astype(F32) + got[rows + count :, :width].astype(F32)


def add_split_kernel(*refs):
    count = len(refs) // 6
    for at in range(count):
        keep_low, keep_high, got_low, got_high = refs[4 * at : 4 * at + 4]
        send, keep = refs[4 * count + 2 * at : 4 * count + 2 * at + 2]
        keep[...] = add(keep_low[...], got_low[...])
        send[...] = add(keep_high[...], got_high[...])


def add_split(pairs):
    args, in_specs, outs, out_specs = [], [], [], []
    for keep, got in pairs:
        rows, width = keep.shape
        low = pl.BlockSpec((rows // 4, width), lambda at: (at, 0))
        high = pl.BlockSpec((rows // 4, width), lambda at: (at + 2, 0))
        args += [keep, keep, got, got]
        in_specs += [low, high, low, high]
        outs += [shaped((rows // 2, width), BF16)] * 2
        out_specs += [low, low]
    made = light_call(add_split_kernel, outs, in_specs, out_specs, (2,))(*args)
    return list(zip(made[0::2], made[1::2]))


def add_split_ride_kernel(riding, keep_in, got, tail, more, send, keep, tail_out):
    rows = keep.shape[0]
    keep[...] = add(keep_in[:rows, :], got[:rows, :])
    send[:rows, :] = add(keep_in[rows:, :], got[rows : 2 * rows, :])
    total = take_ride(tail[...], got, 2 * rows) if riding else tail[...] + more[...]
    tail_out[...] = total
    put_ride(total, send, rows)


def add_split_ride(keep, got, tail, more=None):
    rows, width = keep.shape
    half = rows // 2
    count = 2 * tail.shape[0]
    outs = (shaped((half + count, width), BF16), shaped((half, width), BF16), shaped(tail.shape, F32))
    kernel = functools.partial(add_split_ride_kernel, more is None)
    return light_call(kernel, outs, [vmem()] * 4, [vmem()] * 3)(keep, got, tail, tail if more is None else more)


def add_ride_kernel(keep, got, tail, out, tail_out):
    rows = keep.shape[0]
    total = take_ride(tail[...], got, rows)
    tail_out[...] = total
    put_ride(total, out, rows)
    out[:rows, :] = add(keep[...], got[:rows, :])


def add_ride(keep, got, tail):
    rows, width = keep.shape
    outs = (shaped((rows + 2 * tail.shape[0], width), BF16), shaped(tail.shape, F32))
    return light_call(add_ride_kernel, outs, [vmem()] * 3, [vmem()] * 2)(keep, got, tail)


def add_pack_kernel(first, first_got, second, second_got, *refs):
    rows, width = second.shape[0], first.shape[1]
    if len(refs) > 1:
        tail, out, tail_out = refs
        tail_out[...] = take_ride(tail[...], first_got, rows)
    else:
        (out,) = refs
    out[:, :width] = add(first[:rows, :], first_got[:rows, :])
    out[:, width:] = add(second[...], second_got[...])


def add_pack(first, second, tail=None):
    rows, width = second[0].shape[0], first[0].shape[1]
    out = shaped((rows, width + second[0].shape[1]), BF16)
    if tail is None:
        return light_call(add_pack_kernel, out, [vmem()] * 4, vmem())(*first, *second)
    outs = (out, shaped(tail.shape, F32))
    return light_call(add_pack_kernel, outs, [vmem()] * 5, [vmem()] * 2)(*first, *second, tail)


def choose_kernel(first, second, first_other, second_other, *outs):
    width = outs[0].shape[1]
    for core, pair in ((0, (first, first_other)), (1, (second, second_other))):
        @pl.when(this_core() == core)
        def _():
            for at, source in enumerate(pair):
                outs[2 * at][...] = source[:, :width]
                outs[2 * at + 1][...] = source[:, width:]


def choose(arrays, width):
    rows, both = arrays[0].shape
    outs = [shaped((rows, width), BF16), shaped((rows, both - width), BF16)] * 2
    return light_call(choose_kernel, outs, [vmem()] * 4, [vmem()] * 4)(*arrays)


def add_kernel(left, right, out):
    out[...] = add(left[...], right[...]) if out.dtype == BF16 else left[...] + right[...]


def light_add(left, right):
    return light_call(add_kernel, shaped(left.shape, left.dtype), [vmem()] * 2, vmem())(left, right)


def join_kernel(count, *refs):
    outs = refs[-count:]
    for at in range(count):
        rows = refs[2 * at].shape[0]
        outs[at][:rows] = refs[2 * at][...]
        outs[at][rows : 2 * rows] = refs[2 * at + 1][...]
    if len(refs) > 3 * count:
        put_ride(refs[2 * count][...], outs[0], 2 * refs[0].shape[0])


def join(pairs, tail=None):
    outs = [shaped((2 * upper.shape[0], upper.shape[1]), upper.dtype) for upper, _ in pairs]
    args = [array for pair in pairs for array in pair]
    if tail is not None:
        args.append(tail)
        outs[0] = shaped((outs[0].shape[0] + 2 * tail.shape[0], outs[0].shape[1]), BF16)
    kernel = functools.partial(join_kernel, len(pairs))
    return light_call(kernel, outs, [vmem()] * len(args), [vmem()] * len(outs))(*args)


def pick_kernel(first, second, out):
    @pl.when(this_core() == 0)
    def _():
        out[...] = second[...]

    @pl.when(this_core() == 1)
    def _():
        out[...] = first[...]


def pick(first, second):
    return light_call(pick_kernel, shaped(first.shape, first.dtype), [vmem()] * 2, vmem())(first, second)


def lay_kernel(first, second, other, out, sems):
    core = this_core()
    theirs = pltpu.make_async_copy(other, out.at[0, 1 - core, 0], sems.at[0])
    theirs.start()
    for at, source in ((0, first), (1, second)):
        @pl.when(core == at)
        def _():
            mine = pltpu.make_async_copy(source, out.at[0, at, 0], sems.at[1])
            mine.start()
            mine.wait()
    theirs.wait()


def lay(first, second, other):
    out = shaped((1, 2, 1) + first.shape, first.dtype)
    scratch = [pltpu.SemaphoreType.DMA((2,))]
    return light_call(lay_kernel, out, [vmem()] * 3, hbm(), scratch=scratch)(first, second, other)


def collect_kernel(heads, lengths, back0, gain0, attn0, ffn0, back1, attn1, ffn1, keep, send):
    width = keep.shape[1]
    at = HEADS_ROWS // 2
    count = jnp.full((1, width), lengths[this_core(), 0], jnp.int32).astype(F32)
    for layer, back, gain, attn, ffn in ((0, back0, gain0[0:1, :], attn0, ffn0), (1, back1, ffn1[2:3, :], attn1, ffn1)):
        rows = jnp.concatenate(
            [
                back[: heads + 1, :], gain, jnp.zeros((at - heads - 2, width), F32), back[at : at + heads, :],
                ffn[0:1, :], attn[0:1, :], ffn[1:2, :], count,
            ],
            axis=0,
        )

        @pl.when(this_core() == layer)
        def _():
            keep[...] = rows

        @pl.when(this_core() != layer)
        def _():
            send[...] = rows


def collect(heads, lengths, *stats):
    out = jax.ShapeDtypeStruct((HEADS_ROWS, stats[0].shape[1]), F32)
    return pl.pallas_call(
        functools.partial(collect_kernel, heads),
        out_shape=(out, out),
        in_specs=[smem()] + [vmem()] * len(stats),
        out_specs=[vmem()] * 2,
        cost_estimate=LIGHT,
    )(lengths, *stats)


def small_kernel(heads, tail, got, attn_out, ffn_out, pre_out, post_out, rms_out):
    width = tail.shape[1]
    total = take_ride(tail[...], got, 0)
    at = HEADS_ROWS // 2
    attn_out[...] = total[heads : heads + 1, :]
    ffn_out[...] = total[heads + 1 : heads + 2, :]
    lane = lax.broadcasted_iota(jnp.int32, (width, heads), 0) // (width // heads)
    ones = (lane == lax.broadcasted_iota(jnp.int32, (width, heads), 1)).astype(F32)
    high = lax.Precision.HIGHEST
    pre_out[0] = lax.dot_general(
        total[:heads, :], ones, (((1,), (0,)), ((), ())), precision=high, preferred_element_type=F32
    )
    post_out[0] = lax.dot_general(
        ones, total[at : at + heads, :], (((0,), (1,)), ((), ())), precision=high, preferred_element_type=F32
    )
    tokens = total[HEADS_ROWS - 1 : HEADS_ROWS, 0:1]
    for which in range(3):
        row = total[at + heads + which : at + heads + which + 1, :]
        rms_out[:, which : which + 1] = jnp.sqrt(jnp.sum(row, axis=1, keepdims=True) / width / tokens)


def small_outputs(heads, tail, got):
    width = tail.shape[1]
    shapes = ((1, width), (1, width), (1, heads, heads), (1, heads, heads), (1, 3))
    return pl.pallas_call(
        functools.partial(small_kernel, heads),
        out_shape=tuple(jax.ShapeDtypeStruct(shape, F32) for shape in shapes),
        cost_estimate=LIGHT,
    )(tail, got)


def unpack_kernel(part, owns, meta, *refs):
    count = 2 * len(owns)
    sources, outs, scratch = refs[:count], refs[count + 6 : count + 12], refs[count + 12 :]
    taken_ffn, given_ffn, taken_attn, given_attn, taken_sem, given_sem = scratch
    core = this_core()
    moves = []
    for which, own in enumerate(owns):
        half = core if own else 1 - core
        for group, (taken, given, place, grads) in enumerate((
            (taken_ffn, given_ffn, place_ffn, outs[:2]), (taken_attn, given_attn, place_attn, outs[2:]),
        )):
            rows = taken.shape[1]
            shift = jnp.where(half == 0, meta[1 + 2 * group], meta[2 + 2 * group])
            for step in range(HALF_BLOCKS):
                slot = HALF_BLOCKS * which + step
                at = BLOCKS * group + slot
                block = (HALF_BLOCKS * part + step) ^ shift
                window = sources[2 * which + group].at[pl.ds(step * rows, rows)]
                fetch = pltpu.make_async_copy(window, taken.at[slot], taken_sem.at[at])
                stores = [
                    (chosen, pltpu.make_async_copy(given.at[slot], target, given_sem.at[at]))
                    for chosen, target in place(half, block, grads)
                ]
                moves.append((fetch, stores, taken, given, slot))
    for fetch, *_ in moves:
        fetch.start()
    for fetch, stores, taken, given, slot in moves:
        fetch.wait()
        given[slot] = taken[slot].astype(F32)
        for chosen, copy in stores:
            pl.when(chosen)(copy.start)
    for _, stores, *_ in moves:
        for chosen, copy in stores:
            pl.when(chosen)(copy.wait)


def unpack(part, owns, meta, sources, outs):
    scratch = []
    for source, rows in zip(sources, (outs[0].shape[2] // BLOCKS, outs[2].shape[1] // 2)):
        width = source.shape[1]
        scratch += [pltpu.VMEM((BLOCKS, rows, width), BF16), pltpu.VMEM((BLOCKS, rows, width), F32)]
    scratch += [pltpu.SemaphoreType.DMA((2 * BLOCKS,))] * 2
    return light_call(
        functools.partial(unpack_kernel, part, owns),
        [shaped(out.shape, F32) for out in outs],
        [smem()] + [hbm()] * (len(sources) + len(outs)),
        [hbm()] * len(outs),
        scratch=scratch,
        aliases={1 + len(sources) + at: at for at in range(len(outs))},
    )(meta, *sources, *outs)


def blank_kernel(*refs):
    pass


def blank(shapes):
    return pl.pallas_call(
        blank_kernel,
        out_shape=tuple(jax.ShapeDtypeStruct(shape, F32) for shape in shapes),
        out_specs=[hbm()] * len(shapes),
        cost_estimate=LIGHT,
    )()


def place_ffn(half, block, outs):
    grad_in, grad_out = outs
    width, hidden = grad_in.shape[1:]
    rows = hidden // BLOCKS
    per = width // rows
    inner = jnp.maximum(block - HALF_BLOCKS, 0)
    at_out = pl.multiple_of(half * (hidden // 2) + jnp.minimum(block, HALF_BLOCKS - 1) * rows, rows)
    at_row = pl.multiple_of((inner % per) * rows, rows)
    at_column = pl.multiple_of(half * (hidden // 2) + (inner // per) * width, 128)
    return [
        (block < HALF_BLOCKS, grad_out.at[0, pl.ds(at_out, rows), :]),
        (block >= HALF_BLOCKS, grad_in.at[0, pl.ds(at_row, rows), pl.ds(at_column, width)]),
    ]


def place_attn(half, block, outs):
    width = outs[0].shape[1]
    rows = width // 2
    at_row = pl.multiple_of((block % 2) * rows, rows)
    return [
        (block // 2 == which, outs[which].at[0, pl.ds(at_row, rows), pl.ds(half * rows, rows)]) for which in range(4)
    ]


def after(values, done):
    return lax.optimization_barrier(tuple(values) + tuple(done))[: len(values)]


def param_rows(gain_attn, gain_ffn, mix_pre, mix_post):
    heads = mix_pre.shape[1]
    width = gain_attn.shape[1]
    spread = lambda mix: jnp.repeat(mix, width // heads, axis=1)
    rows = jnp.concatenate([gain_attn, gain_ffn, spread(mix_pre[0]), spread(mix_post[0].T)], axis=0)
    return jnp.pad(rows, ((0, HEADS_ROWS - rows.shape[0]), (0, 0)))


def local(
    inputs, cotangent, lengths, w_query, w_key, w_value, w_output, w_in, w_out, gain_attn, gain_ffn, mix_pre, mix_post,
):
    core = lax.axis_index("section")
    rank = lax.axis_index("dp")
    is_first = core == 0
    swap = lambda shard: lax.ppermute(shard, "section", [(0, 1), (1, 0)])
    length, width = inputs.shape[2:]
    hidden = w_in.shape[2]
    heads = mix_pre.shape[1]

    own_rows = param_rows(gain_attn, gain_ffn, mix_pre, mix_post)
    own = after((w_query, w_key, w_value, w_output), (own_rows,)) + (w_in, w_out)
    other_rows = swap(own_rows)
    other = tuple(swap(weight) for weight in own[:4])
    other += tuple(swap(weight) for weight in after(own[4:], other + (other_rows,)))
    rows = (own_rows, other_rows)
    weights = (own, other)
    ffn_shift = block_shift(FFN_BITS, core, rank)
    attn_shift = block_shift(ATTN_BITS, core, rank)

    steps = {}
    state = {"last": ()}

    def tie(value):
        return after((value,), state["last"])[0] if state["last"] else value

    def chain(layer, make_ffn, make_attn):
        bits = (FFN_BITS, ATTN_BITS)
        keep, got = [None, None], [None, None]
        riding = layer == 0

        def made(group, make):
            def run():
                send, keep[group] = make()
                got[group] = exchange(send, bits[group][0])
                return keep[group]
            return run

        def split(at, groups):
            def run():
                keep[groups[0]] = tie(keep[groups[0]])
                if riding and groups == (0,):
                    send, kept, made_all["tail"] = add_split_ride(
                        keep[0], got[0], made_all["tail"], made_all["more"] if at == 1 else None
                    )
                    parts = [(send, kept)]
                else:
                    parts = add_split([(keep[group], got[group]) for group in groups])
                for group, (send, kept) in zip(groups, parts):
                    keep[group] = kept
                    got[group] = exchange(send, bits[group][at])
                return keep[groups[0]]
            return run

        def third(group):
            def run():
                keep[group] = tie(keep[group])
                if riding and group == 0:
                    keep[0], made_all["tail"] = add_ride(keep[0], got[0], made_all["tail"])
                else:
                    keep[group] = light_add(keep[group], got[group])
                got[group] = exchange(keep[group], (8, 8))
                return keep[group]
            return run

        def summed():
            keep[0] = tie(keep[0])
            rows, bit = keep[1].shape[0], 16
            while bit < lax.axis_size("dp"):
                more = got[0]
                keep[0], keep[1] = add(keep[0], more), add(keep[1], got[1])
                if riding:
                    tail = made_all["tail"] + more[rows : rows + HEADS_ROWS].astype(F32)
                    tail = tail + more[rows + HEADS_ROWS :].astype(F32)
                    high = tail.astype(BF16)
                    terms = [keep[0][:rows], high, (tail - high.astype(F32)).astype(BF16)]
                    made_all["tail"], keep[0] = tail, jnp.concatenate(terms, axis=0)
                got[:] = [exchange(array, (bit, bit)) for array in keep]
                bit *= 2
            pairs = ((keep[0], got[0]), (keep[1], got[1]))
            if riding:
                made_all[layer], made_all["tail"] = add_pack(*pairs, made_all["tail"])
            else:
                made_all[layer] = add_pack(*pairs)
            made_all["hand", layer] = lax.ppermute(made_all[layer], "section", [(1 - layer, layer)])
            return made_all[layer]

        name = str(layer)
        steps.update({
            "P" + name + "w": made(0, make_ffn), "Q" + name + "w": made(1, make_attn),
            "P" + name + "a1": split(1, (0,)), "Q" + name + "a1": split(1, (1,)), "L" + name + "a1": split(1, (0, 1)),
            "P" + name + "a2": split(2, (0,)), "Q" + name + "a2": split(2, (1,)), "L" + name + "a2": split(2, (0, 1)),
            "P" + name + "a3": third(0), "Q" + name + "a3": third(1), "L" + name + "ax": summed,
        })

    def gather():
        bits = [FFN_BITS, ATTN_BITS] + [[pair[::-1] for pair in group] for group in (FFN_BITS, ATTN_BITS)]
        held, got = [None] * 4, [None] * 4

        def send(at):
            got[:] = [exchange(held[part], bits[part][at]) for part in range(4)]
            return held[0]

        def start():
            arrays = (tie(made_all[0]), made_all[1], made_all["hand", 0], made_all["hand", 1])
            held[:] = choose(arrays, width)
            return send(2)

        def second_gather():
            held[:] = join([(tie(held[0]), got[0])] + list(zip(held[1:], got[1:])))
            return send(1)

        def last_own():
            held[0], *got[:] = after(held[:1] + got, state["last"])
            held[:2] = join(list(zip(held[:2], got[:2])), made_all["tail"])
            got[:2] = [exchange(held[part], bits[part][0]) for part in range(2)]
            return held[0]

        def last_other():
            held[2] = tie(held[2])
            held[2:] = join(list(zip(held[2:], got[2:])))
            return held[2]

        def others():
            *held[2:], got[0], got[1] = after(held[2:] + got[:2], state["last"])
            got[2:] = [exchange(held[part], bits[part][0]) for part in (2, 3)]
            return held[2]

        def first():
            made_all["grads"] = unpack(0, (True, False), place_meta, (tie(held[0]), *held[1:]), made_all["grads"])
            return made_all["grads"][0]

        def second(own):
            def run():
                pair = got[:2] if own else got[2:]
                made_all["grads"] = unpack(1, (own,), place_meta, (tie(pair[0]), pair[1]), made_all["grads"])
                return made_all["grads"][0]
            return run

        def small_end():
            rows = HALF_BLOCKS * (hidden // BLOCKS)
            made["small"] = small_outputs(heads, tie(made_all["tail"]), got[0][rows:])
            return made["small"][0]

        steps.update({
            "g3": start, "g2": second_gather, "g1": last_own, "x1": last_other, "uA": first, "g1x": others, "uB": second(True), "uC": second(False), "T1": small_end,
        })

    def ffn_blocks(first, second):
        factors = (tie(first[0]), first[1], second[0], swap(second[1]))
        locate = functools.partial(locate_ffn, hidden // BLOCKS, width, hidden // 2)
        return grad_blocks(locate, ffn_shift, factors, hidden // BLOCKS, width)

    def attn_blocks(both, pack):
        factors = (tie(both[0]), both[1], pack[0], swap(pack[1]))
        locate = functools.partial(locate_attn, width // 2)
        return grad_blocks(locate, attn_shift, factors, width // 2, width // 2)

    both0, *qkvp0, residual0, stats_a0 = attention_forward(0, heads, lengths, inputs, rows, weights)
    mid, own0, send0, slope0, stats_f0 = ffn_forward(0, lengths, residual0, rows, weights)
    both0_other, send0_other = swap(both0), swap(send0)
    both1, *qkvp1, residual1, stats_a1 = attention_forward(1, heads, lengths, mid, rows, weights)
    (residual1,) = after((residual1,), (both0_other, send0_other))
    both1_other = swap(both1)
    last, own1, send1, own1b, send1b, resid1, stats_f1 = ffn_forward(
        1, lengths, residual1, rows, weights, cotangent
    )
    own1, send1_other = after((own1, swap(send1)), (both1_other,))
    made = {}

    def attention1():
        made["pack1"], made["send_pack1"], made["grad1"], made["stats_b1"] = attention_backward(
            1, heads, mid, tie(resid1), qkvp1, rows, weights
        )
        return made["grad1"]

    def ffn0():
        made["own0b"], made["send0b"], made["resid0"], made["stats_g0"] = ffn_backward(
            0, lengths, residual0, tie(made["grad1"]), slope0, rows, weights
        )
        return made["resid0"]

    def attention0():
        made["pack0"], made["send_pack0"], made["grad0"], made["stats_b0"] = attention_backward(
            0, heads, inputs, tie(made["resid0"]), qkvp0, rows, weights
        )
        return made["grad0"]

    steps.update({"K1": attention1, "D0": ffn0, "K0": attention0})
    place_meta = jnp.stack(
        [core] + [block_shift(bits, which, rank) for bits in (FFN_BITS, ATTN_BITS) for which in range(2)]
    ).astype(jnp.int32)
    made_all = {"grads": blank((w_in.shape, w_out.shape) + (w_query.shape,) * 4)}
    chain(
        1,
        lambda: ffn_blocks((own1, send1_other), (own1b, send1b)),
        lambda: attn_blocks((both1, both1_other), (made["pack1"], made["send_pack1"])),
    )
    chain(
        0,
        lambda: ffn_blocks((own0, send0_other), (made["own0b"], made["send0b"])),
        lambda: attn_blocks((both0, both0_other), (made["pack0"], made["send_pack0"])),
    )

    def small_start():
        made_all["tail"], send = collect(
            heads, lengths, tie(made["stats_b0"]), made["stats_g0"], stats_a0, stats_f0, made["stats_b1"], stats_a1, stats_f1
        )
        made_all["more"] = swap(send)
        return made_all["tail"]

    def send_rows(name, first, second):
        def run():
            made[name] = swap(pick(tie(first()), second()))
            return first()
        return run

    def lay_rows(name, first, second):
        def run():
            made[name] = lay(tie(first()), second(), made[name])
            return made[name]
        return run

    mids = ("outputs", lambda: mid, lambda: last)
    grads = ("grads", lambda: made["grad0"], lambda: made["grad1"])
    steps.update({"O0": send_rows(*mids), "O1": lay_rows(*mids), "G0": send_rows(*grads), "G1": lay_rows(*grads)})
    steps["T0"] = small_start
    gather()
    for name in [name for line in ORDER for name in line.split()]:
        with jax.named_scope(name):
            state["last"] = (steps[name](),)

    w_in_grad, w_out_grad, *rest = made_all["grads"]
    return (made["outputs"], made["grads"], *rest, w_in_grad, w_out_grad, *made["small"])


def solution(mesh):
    in_specs = (
        P(None, "dp", None, None),
        P(None, "dp", None, None),
        P(None, "dp"),
        P("section", None, None),
        P("section", None, None),
        P("section", None, None),
        P("section", None, None),
        P("section", None, None),
        P("section", None, None),
        P("section", None),
        P("section", None),
        P("section", None, None),
        P("section", None, None),
    )
    out_specs = (
        P("section", None, "dp", None, None),
        P("section", None, "dp", None, None),
        P("section", None, None),
        P("section", None, None),
        P("section", None, None),
        P("section", None, None),
        P("section", None, None),
        P("section", None, None),
        P("section", None),
        P("section", None),
        P("section", None, None),
        P("section", None, None),
        P("section", None),
    )
    return jax.shard_map(local, mesh=mesh, in_specs=in_specs, out_specs=out_specs, check_vma=False)
```
